32 devices in a mesh: rep: 4 (over x, core), shard: 8 (over z, y).
Axes of the slice: x: 2, y: 2, z: 4, core: 2. Of those that a mesh axis runs over, the one named last changes fastest.
Arguments:
- tokens: bfloat16 [4096, 2048], P(('rep', 'shard')), may hold values from -6 to 6
- segment_ids: int32 [4096], P(('rep', 'shard')), may hold values from 0 to 15, as said below
- positions: int32 [4096], P(('rep', 'shard')), may hold values from 0 to 127, as said below
- first_gain: float32 [2048], P('shard'), may hold values from 0.1 to 1.9
- first_shift: float32 [2048], P('shard'), may hold values from -1.75 to 1.75
- project_weight: bfloat16 [2048, 6144], P('shard'), may hold values from -0.125 to 0.125
- project_bias: float32 [6144], P('shard'), may hold values from -1.75 to 1.75
- mixing_weight: bfloat16 [2048, 2048], P('shard'), may hold values from -1 to 1
- mixing_bias: float32 [2048], P('shard'), may hold values from -1.75 to 1.75
- second_gain: float32 [2048], P('shard'), may hold values from 0.1 to 1.9
- second_shift: float32 [2048], P('shard'), may hold values from -1.75 to 1.75
- widen_weight: bfloat16 [2048, 8192], P('shard'), may hold values from -0.125 to 0.125
- widen_bias: float32 [8192], P('shard'), may hold values from -3 to 3
- narrow_weight: bfloat16 [8192, 2048], P('shard'), may hold values from -0.0625 to 0.0625
- narrow_bias: float32 [2048], P('shard'), may hold values from -1.75 to 1.75
- cotangent: bfloat16 [4096, 2048], P(('rep', 'shard')), may hold values from -6 to 6
Outputs:
- output: bfloat16 [4096, 2048], P(('rep', 'shard'))
- input_grad: bfloat16 [4096, 2048], P(('rep', 'shard'))
- first_gain_grad: float32 [2048], P('shard')
- first_shift_grad: float32 [2048], P('shard')
- project_weight_grad: float32 [2048, 6144], P('shard')
- project_bias_grad: float32 [6144], P('shard')
- mixing_weight_grad: float32 [2048, 2048], P('shard')
- mixing_bias_grad: float32 [2048], P('shard')
- second_gain_grad: float32 [2048], P('shard')
- second_shift_grad: float32 [2048], P('shard')
- widen_weight_grad: float32 [2048, 8192], P('shard')
- widen_bias_grad: float32 [8192], P('shard')
- narrow_weight_grad: float32 [8192, 2048], P('shard')
- narrow_bias_grad: float32 [2048], P('shard')
The draws below stay inside these ranges and needn't reach their ends.
Inputs may be any that keep to these rules, and one draw needn't show every extreme that they name: `segment_ids`: documents never cross an aligned block of 128 tokens and begin only at positions within the block that are multiples of 8; in each block ids start at 0 and rise by one at each new document; some block holds 16 documents. `positions`: each token's position counts from 0 at the first token of its document; some block holds a single document.
All inputs are finite; a program needn't handle non-finite values.
Results may differ from the reference program's by a relative error of at most 0.015.
Values may be sent and summed in bfloat16 or wider, within the bound.
A program may use at most 640 MiB of HBM per device.

```python
import math
import jax
import jax.numpy as jnp
from jax import lax

D = 2048
HEADS = 8
HEAD_DIM = 256
ROT = 64
FF = 8192
TOK_DEV = 128
TOKENS = 4096


def pack_layout(key):
    base = jax.random.fold_in(key, 7)
    blocks = TOKENS // TOK_DEV
    index = jnp.arange(TOK_DEV, dtype=jnp.int32)
    spacing = max(TOK_DEV // 16, 1)
    candidate = index % spacing == 0
    starts = (jax.random.randint(base, (blocks, TOK_DEV), 0, 4) == 0) & candidate[None, :]
    starts = starts | (index == 0)[None, :]
    single = jax.random.randint(jax.random.fold_in(base, 1), (), 0, blocks)
    full = (single + 1) % blocks
    block_index = jnp.arange(blocks)
    starts = jnp.where((block_index == full)[:, None], candidate[None, :], starts)
    starts = jnp.where((block_index == single)[:, None], (index == 0)[None, :], starts)
    segments = jnp.cumsum(starts.astype(jnp.int32), axis=1) - 1
    first_index = lax.cummax(jnp.where(starts, index[None, :], 0), axis=1)
    places = index[None, :] - first_index
    return (segments.reshape(-1).astype(jnp.int32), places.reshape(-1).astype(jnp.int32))


def draw_segment_ids(key, part):
    return pack_layout(key)[0]


def draw_positions(key, part):
    return pack_layout(key)[1]


def raised(values, key, source, target, parts, factor):
    owner, partner = [(jnp.arange(values.shape[dim]) // (values.shape[dim] // parts)).reshape([-1 if axis == dim else 1 for axis in range(values.ndim)]) for dim in (source, target)]
    chosen = jax.random.permutation(key, parts)[partner]
    strong = (owner == chosen) | (owner == (partner + parts // 2) % parts)
    return jnp.where(strong, factor * values, values)


def block_scale(stream_key, shape, cuts, low, largest):
    def one(dim, shards_of):
        steps = jax.random.uniform(jax.random.fold_in(jax.random.fold_in(stream_key, 6), dim), (shards_of,), jnp.float32, low / len(cuts), largest / len(cuts))
        return jnp.repeat(jnp.exp(steps), shape[dim] // shards_of).reshape((-1,) + (1,) * (len(shape) - dim - 1))

    factor_of = one(*cuts[0])
    for cut in cuts[1:]:
        factor_of = factor_of * one(*cut)
    return factor_of


def noise(rng, shape, scale, limit, pieces=(), kind=jnp.bfloat16):
    drawn = scale * jax.random.normal(rng, shape, jnp.float32)
    if pieces:
        drawn = drawn * block_scale(rng, shape, pieces, -0.22, 0.18)
    return jnp.clip(drawn, -limit, limit).astype(kind)


def gaussian_with(key, extent, scale, most, cuts, heavy, kind=jnp.bfloat16):
    values = scale * jax.random.normal(key, extent, jnp.float32)
    if cuts:
        values = values * block_scale(key, extent, cuts, -0.22, 0.18)
    return jnp.clip(raised(values, jax.random.fold_in(key, 3), *heavy), -most, most).astype(kind)


def setup_inputs(seed: int = 0) -> dict:
    splits = jax.random.split(jax.random.key(seed), 17)
    return {
        "tokens": gaussian_with(splits[0], (TOKENS, D), 1.0, 6.0, ((0, 32),), (0, 1, 32, 2.75)),
        "segment_ids": draw_segment_ids(jax.random.fold_in(splits[16], 71), 0),
        "positions": draw_positions(jax.random.fold_in(splits[16], 71), 0),
        "first_gain": jnp.clip(1.0 + 0.18 * jax.random.normal(splits[3], (D,), jnp.float32), 0.1, 1.9),
        "first_shift": noise(splits[4], (D,), 0.3, 1.75, ((0, 8),), jnp.float32),
        "project_weight": noise(splits[5], (D, 3 * D), D ** -0.5, 0.125, ((0, 8),)),
        "project_bias": noise(splits[6], (3 * D,), 0.3, 1.75, ((0, 8),), jnp.float32),
        "mixing_weight": noise(splits[7], (D, D), (D // 48) ** -0.5, 1.0, ((0, 8),)),
        "mixing_bias": noise(splits[8], (D,), 0.3, 1.75, ((0, 8),), jnp.float32),
        "second_gain": jnp.clip(1.0 + 0.18 * jax.random.normal(splits[9], (D,), jnp.float32), 0.1, 1.9),
        "second_shift": noise(splits[10], (D,), 0.3, 1.75, ((0, 8),), jnp.float32),
        "widen_weight": noise(splits[11], (D, FF), D ** -0.5, 0.125, ((0, 8),)),
        "widen_bias": noise(splits[12], (FF,), 0.5, 3.0, ((0, 8),), jnp.float32),
        "narrow_weight": noise(splits[13], (FF, D), FF ** -0.5, 0.0625, ((0, 8),)),
        "narrow_bias": noise(splits[14], (D,), 0.3, 1.75, ((0, 8),), jnp.float32),
        "cotangent": noise(splits[15], (TOKENS, D), 1.0, 6.0, ((0, 32),)),
    }


HIGHEST = lax.Precision.HIGHEST

@jax.custom_vjp
def low(v):
    return lax.optimization_barrier(v.astype(jnp.bfloat16)).astype(jnp.float32)

@jax.custom_vjp
def low_back(v):
    return v

def low_keep(v):
    return (low(v), None)

def low_pass(kept, grad):
    return (grad,)

def back_keep(v):
    return (v, None)

def back_low(kept, grad):
    return (low(grad),)
low.defvjp(low_keep, low_pass)
low_back.defvjp(back_keep, back_low)

def layer_norm(values, gain, shift):
    center = values - lax.optimization_barrier(jnp.mean(values, axis=-1, keepdims=True))
    spread = lax.optimization_barrier(jnp.mean(center * center, axis=-1, keepdims=True))
    return center * lax.rsqrt(spread + 1e-05) * gain + shift

def angles(positions):
    freqs = 10000.0 ** (-(jnp.arange(ROT // 2, dtype=jnp.float32) * 2.0 / ROT))
    turned = positions.astype(jnp.float32)[..., None] * freqs
    return (jnp.cos(turned), jnp.sin(turned))

def rotary(values, cosine, sine):
    half = ROT // 2
    front = values[..., :half]
    back = values[..., half:ROT]
    return jnp.concatenate([front * cosine - back * sine, back * cosine + front * sine, values[..., ROT:]], axis=-1)

def forward(params, inputs, segments, positions):
    first_gain, first_shift, project_weight, project_bias, mixing_weight, mixing_bias, second_gain, second_shift, widen_weight, widen_bias, narrow_weight, narrow_bias = params
    packs, length, width = inputs.shape
    first = low(layer_norm(inputs, first_gain, first_shift))
    second = low(layer_norm(inputs, second_gain, second_shift))
    joint = low_back(jnp.einsum('psd,de->pse', first, project_weight, precision=HIGHEST) + project_bias)
    shaped = joint.reshape(packs, length, 3, HEADS, HEAD_DIM)
    cosine, sine = angles(positions)
    cosine = cosine[:, :, None, :]
    sine = sine[:, :, None, :]
    query = low(rotary(shaped[:, :, 0], cosine, sine) * HEAD_DIM ** (-0.5))
    keys = low(rotary(shaped[:, :, 1], cosine, sine))
    values = low(shaped[:, :, 2])
    scores = low_back(jnp.einsum('pqhe,pkhe->phqk', query, keys, precision=HIGHEST))
    order = jnp.arange(length)
    allowed = (segments[:, :, None] == segments[:, None, :]) & (order[:, None] >= order[None, :])[None]
    weights = low(jax.nn.softmax(jnp.where(allowed[:, None], scores, -1e+30), axis=-1))
    context = jnp.einsum('phqk,pkhe->pqhe', weights, values, precision=HIGHEST).reshape(packs, length, width)
    context = low(low_back(context))
    attention = jnp.einsum('psd,de->pse', context, mixing_weight, precision=HIGHEST) + mixing_bias
    widened = low_back(jnp.einsum('psd,df->psf', second, widen_weight, precision=HIGHEST) + widen_bias)
    active = low(jax.nn.gelu(widened, approximate=False))
    mlp = jnp.einsum('psf,fd->psd', active, narrow_weight, precision=HIGHEST) + narrow_bias
    return inputs + attention + mlp

def reference(tokens, segment_ids, positions, first_gain, first_shift, project_weight, project_bias, mixing_weight, mixing_bias, second_gain, second_shift, widen_weight, widen_bias, narrow_weight, narrow_bias, cotangent):
    params = tuple((item.astype(jnp.float32) for item in (first_gain, first_shift, project_weight, project_bias, mixing_weight, mixing_bias, second_gain, second_shift, widen_weight, widen_bias, narrow_weight, narrow_bias)))
    packs = tokens.shape[0] // TOK_DEV
    group = math.gcd(packs, max(1, 4096 // TOK_DEV))
    rounds = packs // group

    def split(array):
        return array.reshape((rounds, group, TOK_DEV) + array.shape[1:])

    def one_round(totals, item):
        block, segments, places, incoming = item

        def run(params_in, inputs):
            return forward(params_in, inputs, segments, places)
        result, pull = jax.vjp(run, params, block.astype(jnp.float32))
        grads, block_grad = pull(incoming.astype(jnp.float32))
        totals = jax.tree.map(lambda left, right: left + right, totals, grads)
        return (totals, (result.astype(jnp.bfloat16), block_grad.astype(jnp.bfloat16)))
    zeros = jax.tree.map(jnp.zeros_like, params)
    totals, (outputs, input_grads) = lax.scan(one_round, zeros, (split(tokens), split(segment_ids), split(positions), split(cotangent)))
    return (outputs.reshape(tokens.shape), input_grads.reshape(tokens.shape), totals[0], totals[1], totals[2], totals[3], totals[4], totals[5], totals[6], totals[7], totals[8], totals[9], totals[10], totals[11])
```

```python
import jax
import jax.numpy as jnp
from jax import lax
from jax.experimental import pallas as pl
from jax.experimental.pallas import tpu as pltpu
from jax.sharding import PartitionSpec as P

D = 2048
HEADS = 8
HEAD_DIM = 256
ROT = 64
FF = 8192


def layer_norm(values, gain, shift):
    center = values - jnp.mean(values, axis=-1, keepdims=True)
    spread = jnp.mean(center * center, axis=-1, keepdims=True)
    return center * lax.rsqrt(spread + 1e-05) * gain + shift


def angles(positions):
    freqs = 10000.0 ** (-(jnp.arange(ROT // 2, dtype=jnp.float32) * 2.0 / ROT))
    turned = positions.astype(jnp.float32)[..., None] * freqs
    return (jnp.cos(turned), jnp.sin(turned))


def rotary(values, cosine, sine):
    half = ROT // 2
    front = values[..., :half]
    back = values[..., half:ROT]
    return jnp.concatenate(
        [front * cosine - back * sine, back * cosine + front * sine, values[..., ROT:]], axis=-1
    )


def exact_gelu(values):
    return jax.nn.gelu(values, approximate=False)


def contract_rows(left, right):
    return lax.dot_general(
        left, right, (((0,), (0,)), ((), ())), preferred_element_type=jnp.float32
    )


def times_rows(left, piece):
    return lax.dot_general(
        left, piece, (((1,), (1,)), ((), ())), preferred_element_type=jnp.float32
    )


def weight_terms(left_one, left_two, left_mix, left_act, d_joint, d_widened, cotangent):

    def wide_term(start, count):
        return jnp.concatenate(
            [
                contract_rows(left_one, d_joint),
                contract_rows(left_two, d_widened),
                contract_rows(left_mix, cotangent),
            ],
            axis=1,
        )

    def down_term(start, count):
        return contract_rows(left_act, cotangent)

    return (wide_term, down_term)


def per_device(
    tokens,
    segment_ids,
    positions,
    first_gain,
    first_shift,
    project_weight,
    project_bias,
    mixing_weight,
    mixing_bias,
    second_gain,
    second_shift,
    widen_weight,
    widen_bias,
    narrow_weight,
    narrow_bias,
    cotangent,
):
    length = tokens.shape[0]
    shards = lax.axis_size("shard")
    gain_one, shift_one, gain_two, shift_two, joint_bias, mix_bias, wide_bias, narrow_full = (
        lax.all_gather(first_gain, "shard", axis=0, tiled=True),
        lax.all_gather(first_shift, "shard", axis=0, tiled=True),
        lax.all_gather(second_gain, "shard", axis=0, tiled=True),
        lax.all_gather(second_shift, "shard", axis=0, tiled=True),
        lax.all_gather(project_bias, "shard", axis=0, tiled=True),
        lax.all_gather(mixing_bias, "shard", axis=0, tiled=True),
        lax.all_gather(widen_bias, "shard", axis=0, tiled=True),
        lax.all_gather(narrow_bias, "shard", axis=0, tiled=True),
    )
    inputs = tokens.astype(jnp.float32)
    first_norm, first_pull = jax.vjp(layer_norm, inputs, gain_one, shift_one)
    second_norm, second_pull = jax.vjp(layer_norm, inputs, gain_two, shift_two)
    first = first_norm.astype(jnp.bfloat16)
    second = second_norm.astype(jnp.bfloat16)
    pieces = (
        lax.all_gather(project_weight, "shard", axis=0, tiled=True),
        lax.all_gather(widen_weight, "shard", axis=0, tiled=True),
    )
    part_one = jnp.dot(first, pieces[0], preferred_element_type=jnp.float32)
    part_two = jnp.dot(second, pieces[1], preferred_element_type=jnp.float32)
    joint = part_one + joint_bias
    widened = part_two + wide_bias
    shaped = joint.reshape(length, 3, HEADS, HEAD_DIM)
    cosine, sine = angles(positions)
    cosine = cosine[:, None, :]
    sine = sine[:, None, :]

    def place(query_in, key_in):
        return (rotary(query_in, cosine, sine) * HEAD_DIM ** (-0.5), rotary(key_in, cosine, sine))

    (query_turned, key_turned), rotate_pull = jax.vjp(place, shaped[:, 0], shaped[:, 1])
    query = query_turned.astype(jnp.bfloat16)
    keys = key_turned.astype(jnp.bfloat16)
    values = shaped[:, 2].astype(jnp.bfloat16)
    order = jnp.arange(length)
    allowed = ((segment_ids[:, None] == segment_ids[None, :]) & (order[:, None] >= order[None, :]))[
        None
    ]

    def masked_scores():
        raw = jnp.einsum("qhe,khe->hqk", query, keys, preferred_element_type=jnp.float32)
        return jnp.where(allowed, raw, -1e30)

    scores = masked_scores()
    highest = jnp.max(scores, axis=-1, keepdims=True)
    raised = jnp.exp(scores - highest)
    summed = jnp.sum(raised, axis=-1, keepdims=True)
    log_summed = highest + jnp.log(summed)
    weights = (raised / summed).astype(jnp.bfloat16)
    context = (
        jnp.einsum("hqk,khe->qhe", weights, values, preferred_element_type=jnp.float32)
        .reshape(length, D)
        .astype(jnp.bfloat16)
    )
    attention = (
        jnp.dot(
            context,
            lax.all_gather(mixing_weight, "shard", axis=0, tiled=True),
            preferred_element_type=jnp.float32,
        )
        + mix_bias
    )
    active_full, gelu_pull = jax.vjp(exact_gelu, widened)
    active = active_full.astype(jnp.bfloat16)
    mlp = (
        jnp.dot(
            active,
            lax.all_gather(narrow_weight, "shard", axis=0, tiled=True),
            preferred_element_type=jnp.float32,
        )
        + narrow_full
    )
    output = (inputs + attention + mlp).astype(jnp.bfloat16)

    def back_rows(piece):
        return times_rows(cotangent, piece)

    d_active = back_rows(lax.all_gather(narrow_weight, "shard", axis=0, tiled=True))
    d_widened = gelu_pull(d_active)[0].astype(jnp.bfloat16)
    d_context = back_rows(lax.all_gather(mixing_weight, "shard", axis=0, tiled=True))
    d_context = d_context.astype(jnp.bfloat16).reshape(length, HEADS, HEAD_DIM)
    again = jnp.exp(masked_scores() - log_summed)
    again_low = again.astype(jnp.bfloat16)
    d_weights = jnp.einsum("qhe,khe->hqk", d_context, values, preferred_element_type=jnp.float32)
    d_values = jnp.einsum("hqk,qhe->khe", again_low, d_context, preferred_element_type=jnp.float32)
    d_scores = (again * (d_weights - jnp.sum(d_weights * again, axis=-1, keepdims=True))).astype(
        jnp.bfloat16
    )
    d_query = jnp.einsum("hqk,khe->qhe", d_scores, keys, preferred_element_type=jnp.float32)
    d_keys = jnp.einsum("hqk,qhe->khe", d_scores, query, preferred_element_type=jnp.float32)
    d_query_in, d_key_in = rotate_pull((d_query, d_keys))
    d_joint = jnp.concatenate(
        [d_query_in.reshape(length, D), d_key_in.reshape(length, D), d_values.reshape(length, D)],
        axis=1,
    ).astype(jnp.bfloat16)
    pieces = lax.all_gather((project_weight, widen_weight), "shard", axis=0, tiled=True)
    stacked = jnp.concatenate(
        [times_rows(d_joint, pieces[0]), times_rows(d_widened, pieces[1])], axis=0
    )
    d_in_one, d_gain_one, d_shift_one = first_pull(stacked[:length])
    d_in_two, d_gain_two, d_shift_two = second_pull(stacked[length:])
    input_grad = (cotangent.astype(jnp.float32) + d_in_one + d_in_two).astype(jnp.bfloat16)
    sums = lax.psum(
        (
            d_gain_one,
            d_shift_one,
            d_gain_two,
            d_shift_two,
            jnp.sum(d_joint, axis=0, dtype=jnp.float32),
            jnp.sum(cotangent, axis=0, dtype=jnp.float32),
            jnp.sum(d_widened, axis=0, dtype=jnp.float32),
        ),
        ("rep", "shard"),
    )
    owner = lax.axis_index("shard")

    def own_part(vector):
        share = vector.shape[0] // shards
        return lax.dynamic_slice_in_dim(vector, owner * share, share)

    owned = [own_part(vector) for vector in sums]
    wide_term, down_term = weight_terms(
        first, second, context, active, d_joint, d_widened, cotangent
    )
    wide_part = lax.psum_scatter(
        wide_term(jnp.int32(0), lax.axis_size("shard") * (D // shards)).astype(jnp.bfloat16),
        "shard",
        scatter_dimension=0,
        tiled=True,
    ).astype(jnp.float32)
    down_part = lax.psum_scatter(
        down_term(jnp.int32(0), lax.axis_size("shard") * (FF // shards)).astype(jnp.bfloat16),
        "shard",
        scatter_dimension=0,
        tiled=True,
    ).astype(jnp.float32)
    wide_part, down_part = (
        lax.psum(wide_part.astype(jnp.bfloat16), "rep").astype(jnp.float32),
        lax.psum(down_part.astype(jnp.bfloat16), "rep").astype(jnp.float32),
    )
    return (
        output,
        input_grad,
        owned[0],
        owned[1],
        wide_part[:, : 3 * D],
        owned[4],
        wide_part[:, 3 * D + FF :],
        owned[5],
        owned[2],
        owned[3],
        wide_part[:, 3 * D : 3 * D + FF],
        owned[6],
        down_part,
        owned[5],
    )


MESH = pl.DeviceIdType.MESH
ANY = pl.BlockSpec(memory_space=pl.ANY)


def places():
    rep, me = lax.axis_index("rep"), lax.axis_index("shard")
    core, side = rep % 2, rep // 2
    col, line = me % 2, me // 2
    return rep, me, core, side, col, line


def greet(peers):
    barrier = pltpu.get_barrier_semaphore()
    for peer in peers:
        pl.semaphore_signal(barrier, inc=1, device_id=peer, device_id_type=MESH)
    pl.semaphore_wait(barrier, len(peers))


def remote(source, target, send, recv, device):
    return pltpu.make_async_remote_copy(
        src_ref=source,
        dst_ref=target,
        send_sem=send,
        recv_sem=recv,
        device_id=device,
        device_id_type=MESH,
    )


def spread_kernel(
    tok, cot, wide_one, wide_two, small,
    tok_all, cot_all, cols_one, cols_two, small_all,
    line_send, line_recv, col_send, col_recv,
    own_sem, piece_send, piece_recv, side_send, side_recv, core_send, core_recv,
    small_send, small_recv,
):
    rep, me, core, side, col, line = places()
    twin = rep + 1 - 2 * core
    across = rep + 2 - 4 * side
    other = me + 1 - 2 * col
    wide = cols_one.shape[1] // 3
    two_wide = cols_two.shape[1]
    rows = wide_one.shape[0]
    share = rows // 4
    greet(
        [(rep, (me + step) % 8) for step in range(1, 8)]
        + [(twin, me), (across, me)]
    )

    def block(array, index):
        return array.at[index]

    def along(which, array, gathered, direction, step):
        owner = line - direction * (step - 1)
        source = array if step == 1 else gathered.at[owner * 2 + col]
        lane = which * 6 + (0 if direction == 1 else 3) + step - 1
        return remote(
            source,
            gathered.at[owner * 2 + col],
            line_send.at[lane],
            line_recv.at[lane],
            (rep, (line + direction) * 2 + col),
        )

    def sends(direction, step):
        if direction == 1:
            return (line >= step - 1) & (line <= 2)
        return (line <= 4 - step) & (line >= 1)

    def gets(direction, step):
        if direction == 1:
            return line >= step
        return line <= 3 - step

    def sideways(which, array, gathered, direction, step):
        owner = line - direction * step
        source = array if step == 0 else gathered.at[owner * 2 + col]
        lane = which * 7 + (0 if direction == 1 else 3) + step
        return remote(
            source,
            gathered.at[owner * 2 + col],
            col_send.at[lane],
            col_recv.at[lane],
            (rep, other),
        )

    def from_other(which, gathered, direction, step):
        owner = line - direction * step
        lane = which * 7 + (0 if direction == 1 else 3) + step
        return remote(
            gathered.at[owner * 2 + 1 - col],
            gathered.at[owner * 2 + 1 - col],
            col_send.at[lane],
            col_recv.at[lane],
            (rep, other),
        )

    pairs = ((tok, tok_all), (cot, cot_all))
    turns = [(direction, step) for step in (1, 2, 3) for direction in (1, -1)]

    def begin(which):
        array, gathered = pairs[which]
        for direction in (1, -1):
            @pl.when(sends(direction, 1))
            def _(direction=direction):
                along(which, array, gathered, direction, 1).start()
        sideways(which, array, gathered, 1, 0).start()

    def pass_on(which):
        array, gathered = pairs[which]
        for direction, step in turns:
            @pl.when(gets(direction, step))
            def _(direction=direction, step=step):
                owner = line - direction * step
                lane = which * 6 + (0 if direction == 1 else 3) + step - 1
                here = gathered.at[owner * 2 + col]
                remote(
                    here, here, line_send.at[lane], line_recv.at[lane], (rep, me)
                ).wait_recv()
                sideways(which, array, gathered, direction, step).start()

            if step < 3:
                @pl.when(sends(direction, step + 1))
                def _(direction=direction, step=step):
                    along(which, array, gathered, direction, step + 1).start()

    def finish(which):
        array, gathered = pairs[which]
        for direction, step in turns:
            @pl.when(sends(direction, step))
            def _(direction=direction, step=step):
                along(which, array, gathered, direction, step).wait_send()

            @pl.when(gets(direction, step))
            def _(direction=direction, step=step):
                sideways(which, array, gathered, direction, step).wait_send()
                from_other(which, gathered, direction, step).wait_recv()

        sideways(which, array, gathered, 1, 0).wait_send()
        from_other(which, gathered, 1, 0).wait_recv()

    mine = pl.multiple_of(rep * share, share)

    def pieces(step):
        target = (me + step) % 8
        place = pl.ds(pl.multiple_of(me * rows + rep * share, share), share)
        out = []
        for part in range(3):
            out.append(
                remote(
                    wide_one.at[
                        pl.ds(mine, share),
                        pl.ds(pl.multiple_of((part * 8 + target) * wide, wide), wide),
                    ],
                    cols_one.at[place, pl.ds(part * wide, wide)],
                    piece_send.at[step - 1, part],
                    piece_recv.at[step - 1, part],
                    (rep, target),
                )
            )
        out.append(
            remote(
                wide_two.at[
                    pl.ds(mine, share),
                    pl.ds(pl.multiple_of(target * two_wide, two_wide), two_wide),
                ],
                cols_two.at[place, :],
                piece_send.at[step - 1, 3],
                piece_recv.at[step - 1, 3],
                (rep, target),
            )
        )
        return out

    def arrived(step):
        source = (me + 8 - step) % 8
        place = pl.ds(pl.multiple_of(source * rows + rep * share, share), share)
        out = []
        for part in range(3):
            here = cols_one.at[place, pl.ds(part * wide, wide)]
            out.append(
                remote(
                    here, here, piece_send.at[step - 1, part],
                    piece_recv.at[step - 1, part], (rep, source),
                )
            )
        here = cols_two.at[place, :]
        out.append(
            remote(
                here, here, piece_send.at[step - 1, 3], piece_recv.at[step - 1, 3],
                (rep, source),
            )
        )
        return out

    def shares(step, quarter, send, recv, lane, device):
        source = (me + 8 - step) % 8
        place = pl.ds(pl.multiple_of(source * rows + quarter * share, share), share)
        return [
            remote(
                array.at[place, :], array.at[place, :],
                send.at[lane, step - 1, index], recv.at[lane, step - 1, index], device,
            )
            for index, array in enumerate((cols_one, cols_two))
        ]

    def little(step):
        return remote(
            small, small_all.at[me], small_send.at[step - 1], small_recv.at[step - 1],
            (rep, (me + step) % 8),
        )

    begin(0)
    for step in range(1, 8):
        little(step).start()
    for step in range(1, 8):
        for copy in pieces(step):
            copy.start()
    own = [
        pltpu.make_async_copy(tok, tok_all.at[me], own_sem.at[0]),
        pltpu.make_async_copy(cot, cot_all.at[me], own_sem.at[1]),
        pltpu.make_async_copy(small, small_all.at[me], own_sem.at[2]),
        pltpu.make_async_copy(
            wide_two.at[:, pl.ds(pl.multiple_of(me * two_wide, two_wide), two_wide)],
            cols_two.at[pl.ds(pl.multiple_of(me * rows, rows), rows), :],
            own_sem.at[3],
        ),
    ] + [
        pltpu.make_async_copy(
            wide_one.at[:, pl.ds(pl.multiple_of((part * 8 + me) * wide, wide), wide)],
            cols_one.at[
                pl.ds(pl.multiple_of(me * rows, rows), rows), pl.ds(part * wide, wide)
            ],
            own_sem.at[4 + part],
        )
        for part in range(3)
    ]
    for copy in own:
        copy.start()
    pass_on(0)
    begin(1)
    for step in range(1, 8):
        for copy in arrived(step):
            copy.wait_recv()
        for copy in shares(step, rep, side_send, side_recv, 0, (across, me)):
            copy.start()
        for copy in shares(step, rep, core_send, core_recv, 0, (twin, me)):
            copy.start()
    pass_on(1)
    for step in range(1, 8):
        for copy in shares(step, across, side_send, side_recv, 0, (across, me)):
            copy.wait_recv()
        for copy in shares(step, across, core_send, core_recv, 1, (twin, me)):
            copy.start()
    finish(0)
    finish(1)
    twin_across = across + 1 - 2 * core
    for step in range(1, 8):
        for copy in pieces(step):
            copy.wait_send()
        for copy in shares(step, rep, side_send, side_recv, 0, (across, me)):
            copy.wait_send()
        for copy in shares(step, rep, core_send, core_recv, 0, (twin, me)):
            copy.wait_send()
        for copy in shares(step, across, core_send, core_recv, 1, (twin, me)):
            copy.wait_send()
        for copy in shares(step, twin, core_send, core_recv, 0, (twin, me)):
            copy.wait_recv()
        for copy in shares(step, twin_across, core_send, core_recv, 1, (twin, me)):
            copy.wait_recv()
        source = (me + 8 - step) % 8
        little(step).wait_send()
        remote(
            small_all.at[source], small_all.at[source], small_send.at[step - 1],
            small_recv.at[step - 1], (rep, source),
        ).wait_recv()
    for copy in own:
        copy.wait()


def spread(tok, cot, wide_one, wide_two, small):
    dma = pltpu.SemaphoreType.DMA
    length, width = tok.shape
    rows, one = wide_one.shape
    two = wide_two.shape[1]
    bf16 = jnp.bfloat16
    return pl.pallas_call(
        spread_kernel,
        out_shape=(
            jax.ShapeDtypeStruct((8, length, width), bf16),
            jax.ShapeDtypeStruct((8, length, width), bf16),
            jax.ShapeDtypeStruct((rows * 8, one // 8), bf16),
            jax.ShapeDtypeStruct((rows * 8, two // 8), bf16),
            jax.ShapeDtypeStruct((8,) + small.shape, jnp.float32),
        ),
        in_specs=[ANY] * 5,
        out_specs=(ANY,) * 5,
        scratch_shapes=[
            dma((12,)), dma((12,)), dma((14,)), dma((14,)),
            dma((7,)), dma((7, 4)), dma((7, 4)),
            dma((1, 7, 2)), dma((1, 7, 2)), dma((2, 7, 2)), dma((2, 7, 2)),
            dma((7,)), dma((7,)),
        ],
        compiler_params=pltpu.CompilerParams(collective_id=0, has_side_effects=True),
        name="spread",
    )(tok, cot, wide_one, wide_two, small)


def rows_loop(extent, chunk, body):
    @pl.loop(0, extent // chunk)
    def _(index):
        body(pl.ds(pl.multiple_of(index * chunk, chunk), chunk))


def add_two(target, left, right, chunk):
    def body(rows):
        target[rows, :] = (
            left[rows, :].astype(jnp.float32) + right[rows, :].astype(jnp.float32)
        ).astype(target.dtype)

    rows_loop(target.shape[0], chunk, body)


def add_three(target, left, right, third, chunk):
    def body(rows):
        target[rows, :] = (
            left[rows, :].astype(jnp.float32)
            + right[rows, :].astype(jnp.float32)
            + third[rows, :].astype(jnp.float32)
        ).astype(target.dtype)

    rows_loop(target.shape[0], chunk, body)


def gather_sums_kernel(
    out_part, in_part, one, two, mix, narrow, vec,
    out_sum, in_sum, one_full, two_full, mix_full, narrow_full, vec_full,
    loc_one, loc_two, loc_mix, loc_nar,
    core_one, core_two, core_mix, core_nar,
    side_one, side_two, side_mix, side_nar,
    loc_act, col_act, line_act, total, vec_loc, vec_got, vec_mid, vec_rep,
    load_sem, cs, cr, ss, sr, ys, yr, zs, zr, ps, pr, fs, fr, vs, vr, us, ur, ds_sem,
):
    rep, me, core, side, col, line = places()
    twin = rep + 1 - 2 * core
    across = rep + 2 - 4 * side
    diagonal = across + 1 - 2 * core
    other = me + 1 - 2 * col
    greet(
        [(rep, (me + step) % 8) for step in range(1, 8)]
        + [(twin, me), (across, me), (diagonal, me)]
    )
    grads = (
        (one, loc_one, core_one, side_one),
        (two, loc_two, core_two, side_two),
        (mix, loc_mix, core_mix, side_mix),
        (narrow, loc_nar, core_nar, side_nar),
    )
    acts = (out_part, in_part)

    def quarter_of(index, quarter):
        full = grads[index][0]
        return full.at[:, quarter] if index < 2 else full.at[quarter]

    def core_copy(index, slot):
        full, _, got, _ = grads[index]
        quarter = (across if slot == 0 else rep) + 1 - 2 * core
        return remote(
            quarter_of(index, quarter), got.at[slot], cs.at[index, slot], cr.at[index, slot],
            (twin, me),
        )

    def load(index, slot):
        full, local, _, _ = grads[index]
        quarter = across if slot == 0 else rep
        return pltpu.make_async_copy(
            quarter_of(index, quarter), local.at[slot], load_sem.at[index, slot]
        )

    def side_copy(index):
        _, local, _, got = grads[index]
        return remote(local.at[0], got, ss.at[index], sr.at[index], (across, me))

    def col_copy(index, step):
        target = (line + step) % 4
        return remote(
            acts[index].at[target * 2 + 1 - col], col_act.at[index, step],
            ys.at[index, step], yr.at[index, step], (rep, other),
        )

    def act_load(index, step):
        target = (line + step) % 4
        return pltpu.make_async_copy(
            acts[index].at[target * 2 + col], loc_act.at[index, step],
            load_sem.at[4 + index, step],
        )

    def line_copy(index, step):
        return remote(
            loc_act.at[index, step], line_act.at[index, step - 1],
            zs.at[index, step - 1], zr.at[index, step - 1],
            (rep, ((line + step) % 4) * 2 + col),
        )

    def vec_copy(step):
        target = (me + step) % 8
        return remote(
            vec.at[target], vec_got.at[step - 1], vs.at[step - 1], vr.at[step - 1],
            (rep, target),
        )

    def vec_share(step):
        target = (rep + step) % 4
        return remote(
            vec_mid, vec_rep.at[step - 1], us.at[step - 1], ur.at[step - 1],
            (target, me),
        )

    for index in (0, 1):
        for slot in (0, 1):
            core_copy(index, slot).start()
            load(index, slot).start()
    for index in (2, 3):
        for slot in (0, 1):
            core_copy(index, slot).start()
            load(index, slot).start()
    for step in range(1, 8):
        vec_copy(step).start()
    vec_load = pltpu.make_async_copy(vec.at[me], vec_loc, ds_sem.at[0])
    vec_load.start()
    for index in (0, 1):
        for step in (2, 1, 3, 0):
            col_copy(index, step).start()
            act_load(index, step).start()

    def flat(ref):
        if len(ref.shape) == 3:
            return [ref.at[i] for i in range(ref.shape[0])]
        return [ref]

    for index in range(4):
        _, local, got, _ = grads[index]
        core_copy(index, 0).wait_recv()
        load(index, 0).wait()
        for here, there in zip(flat(local.at[0]), flat(got.at[0])):
            add_two(here, here, there, 16)
        side_copy(index).start()

    for index in (0, 1):
        for step in (2, 1, 3):
            col_copy(index, step).wait_recv()
            act_load(index, step).wait()
            here = loc_act.at[index, step]
            add_two(here, here, col_act.at[index, step], 16)
            line_copy(index, step).start()

    vec_load.wait()
    for step in range(1, 8):
        vec_copy(step).wait_recv()
    running = vec_loc[...]
    for step in range(1, 8):
        running = running + vec_got[step - 1]
    vec_mid[...] = running
    for step in range(1, 4):
        vec_share(step).start()

    share_one = one_full.shape[0] // 4
    wide = loc_one.shape[3] // 3
    two_wide = loc_two.shape[3]
    my_rows = pl.ds(pl.multiple_of(rep * share_one, share_one), share_one)

    def whole(index):
        _, local, got, arrived = grads[index]
        core_copy(index, 1).wait_recv()
        load(index, 1).wait()
        side_copy(index).wait_recv()
        for here, there, far in zip(flat(local.at[1]), flat(got.at[1]), flat(arrived)):
            add_three(here, here, there, far, 16)

    def piece(index, step, part, source_shard, target_shard, local):
        if index == 0:
            return remote(
                local.at[:, pl.ds(part * wide, wide)],
                one_full.at[
                    my_rows,
                    pl.ds(pl.multiple_of((part * 8 + source_shard) * wide, wide), wide),
                ],
                ps.at[step, part], pr.at[step, part], (rep, target_shard),
            )
        return remote(
            local,
            two_full.at[
                my_rows, pl.ds(pl.multiple_of(source_shard * two_wide, two_wide), two_wide)
            ],
            ps.at[step, 3], pr.at[step, 3], (rep, target_shard),
        )

    def pieces(index, step, source_shard, target_shard):
        local = grads[index][1].at[1, target_shard]
        parts = range(3) if index == 0 else (0,)
        return [
            piece(index, step, part, source_shard, target_shard, local) for part in parts
        ]

    def own_pieces(index):
        if index == 0:
            return [
                pltpu.make_async_copy(
                    loc_one.at[1, me, :, pl.ds(part * wide, wide)],
                    one_full.at[
                        my_rows,
                        pl.ds(pl.multiple_of((part * 8 + me) * wide, wide), wide),
                    ],
                    ds_sem.at[1 + part],
                )
                for part in range(3)
            ]
        return [
            pltpu.make_async_copy(
                loc_two.at[1, me],
                two_full.at[
                    my_rows, pl.ds(pl.multiple_of(me * two_wide, two_wide), two_wide)
                ],
                ds_sem.at[4],
            )
        ]

    for index in (0, 1):
        whole(index)
        for step in range(1, 8):
            for copy in pieces(index, step, me, (me + step) % 8):
                copy.start()
        for copy in own_pieces(index):
            copy.start()

    fulls = (one_full, two_full, mix_full, narrow_full)

    def spot(index, quarter):
        count = fulls[index].shape[0] // 4
        return fulls[index].at[pl.ds(pl.multiple_of(quarter * count, count), count), :]

    def hand(index, lane, source, quarter, device):
        return remote(
            source, spot(index, quarter), fs.at[index, lane], fr.at[index, lane], device
        )

    own_full = []
    for index in (2, 3):
        whole(index)
        source = grads[index][1].at[1]
        hand(index, 0, source, rep, (across, me)).start()
        hand(index, 1, source, rep, (twin, me)).start()
        copy = pltpu.make_async_copy(source, spot(index, rep), ds_sem.at[3 + index])
        copy.start()
        own_full.append(copy)

    for index in (0, 1):
        for copy in own_pieces(index):
            copy.wait()
        for step in range(1, 8):
            source_shard = (me + 8 - step) % 8
            for copy in pieces(index, step, source_shard, me):
                copy.wait_recv()
        hand(index, 0, spot(index, rep), rep, (across, me)).start()
        hand(index, 1, spot(index, rep), rep, (twin, me)).start()

    for index in (0, 1):
        col_copy(index, 0).wait_recv()
        act_load(index, 0).wait()
        for step in range(1, 4):
            line_copy(index, step).wait_recv()

        def body(rows, index=index):
            value = loc_act[index, 0, rows, :].astype(jnp.float32)
            value = value + col_act[index, 0, rows, :].astype(jnp.float32)
            for step in range(3):
                value = value + line_act[index, step, rows, :].astype(jnp.float32)
            total[index, rows, :] = value

        rows_loop(total.shape[1], 16, body)
    outs = [
        pltpu.make_async_copy(total.at[0], out_sum, ds_sem.at[7]),
        pltpu.make_async_copy(total.at[1], in_sum, ds_sem.at[8]),
    ]
    for copy in outs:
        copy.start()

    for step in range(1, 4):
        vec_share(step).wait_recv()
    vec_full[...] = vec_mid[...] + vec_rep[0] + vec_rep[1] + vec_rep[2]

    for index in (2, 3, 0, 1):
        hand(index, 0, spot(index, across), across, (across, me)).wait_recv()
        hand(index, 2, spot(index, across), across, (twin, me)).start()
    for index in range(4):
        source = grads[index][1].at[1] if index > 1 else spot(index, rep)
        hand(index, 0, source, rep, (across, me)).wait_send()
        hand(index, 1, source, rep, (twin, me)).wait_send()
        hand(index, 1, spot(index, twin), twin, (twin, me)).wait_recv()
        hand(index, 2, spot(index, across), across, (twin, me)).wait_send()
        hand(index, 2, spot(index, diagonal), diagonal, (twin, me)).wait_recv()
        side_copy(index).wait_send()
        for slot in (0, 1):
            core_copy(index, slot).wait_send()
    for index in (0, 1):
        for step in range(1, 8):
            for copy in pieces(index, step, me, (me + step) % 8):
                copy.wait_send()
        for step in range(4):
            col_copy(index, step).wait_send()
            if step:
                line_copy(index, step).wait_send()
    for step in range(1, 8):
        vec_copy(step).wait_send()
    for step in range(1, 4):
        vec_share(step).wait_send()
    for copy in own_full + outs:
        copy.wait()


def gather_sums(out_part, in_part, one, two, mix, narrow, vec):
    dma = pltpu.SemaphoreType.DMA
    bf16, f32 = jnp.bfloat16, jnp.float32
    _, length, width = out_part.shape
    shards, _, share, one_wide = one.shape
    two_wide = two.shape[3]
    struct = jax.ShapeDtypeStruct
    grads = [(g.shape[0],) + g.shape[2:] for g in (one, two)]
    grads += [g.shape[1:] for g in (mix, narrow)]
    return pl.pallas_call(
        gather_sums_kernel,
        out_shape=(
            struct((length, width), f32),
            struct((length, width), f32),
            struct((4 * share, shards * one_wide), bf16),
            struct((4 * share, shards * two_wide), bf16),
            struct((4 * mix.shape[1], width), bf16),
            struct((4 * narrow.shape[1], width), bf16),
            struct(vec.shape[1:], f32),
        ),
        in_specs=[ANY] * 7,
        out_specs=(ANY,) * 6 + (pl.BlockSpec(memory_space=pltpu.VMEM),),
        scratch_shapes=[pltpu.VMEM((2,) + g, bf16) for g in grads]
        + [pltpu.VMEM((2,) + g, bf16) for g in grads]
        + [pltpu.VMEM(g, bf16) for g in grads]
        + [
            pltpu.VMEM((2, 4, length, width), bf16),
            pltpu.VMEM((2, 4, length, width), bf16),
            pltpu.VMEM((2, 3, length, width), bf16),
            pltpu.VMEM((2, length, width), f32),
            pltpu.VMEM(vec.shape[1:], f32),
            pltpu.VMEM((7,) + vec.shape[1:], f32),
            pltpu.VMEM(vec.shape[1:], f32),
            pltpu.VMEM((3,) + vec.shape[1:], f32),
            dma((6, 4)),
            dma((4, 2)), dma((4, 2)), dma((4,)), dma((4,)),
            dma((2, 4)), dma((2, 4)), dma((2, 3)), dma((2, 3)),
            dma((8, 4)), dma((8, 4)), dma((4, 3)), dma((4, 3)),
            dma((7,)), dma((7,)), dma((3,)), dma((3,)), dma((9,)),
        ],
        compiler_params=pltpu.CompilerParams(
            collective_id=1, has_side_effects=True, vmem_limit_bytes=56 << 20
        ),
        name="gather_sums",
    )(out_part, in_part, one, two, mix, narrow, vec)


def turn(values, cosine, sine, sign):
    half = ROT // 2
    front, back = values[..., :half], values[..., half:ROT]
    return jnp.concatenate(
        [
            front * cosine - sign * back * sine,
            back * cosine + sign * front * sine,
            values[..., ROT:],
        ],
        axis=-1,
    )


def matmul(left, right):
    return jnp.dot(left, right, preferred_element_type=jnp.float32)


def tensor_parallel(
    tokens,
    segment_ids,
    positions,
    first_gain,
    first_shift,
    project_weight,
    project_bias,
    mixing_weight,
    mixing_bias,
    second_gain,
    second_shift,
    widen_weight,
    widen_bias,
    narrow_weight,
    narrow_bias,
    cotangent,
):
    f32, bf16 = jnp.float32, jnp.bfloat16
    length = tokens.shape[0]
    me = lax.axis_index("shard")
    packed = jnp.concatenate(
        [
            first_gain, first_shift, second_gain, second_shift, mixing_bias, narrow_bias,
            project_bias, widen_bias, segment_ids.astype(f32), positions.astype(f32),
            jnp.zeros((512,), f32),
        ]
    ).reshape(32, 128)
    tok_all, cot_all, cols_one, cols_two, small = spread(
        tokens, cotangent, project_weight, widen_weight, packed
    )

    def param(start, rows):
        return small[:, start : start + rows].reshape(-1)

    gain_one, shift_one, gain_two, shift_two = (param(2 * i, 2) for i in range(4))
    out_bias = param(8, 2) + param(10, 2)
    head_bias = lax.dynamic_index_in_dim(
        param(12, 6).reshape(3, HEADS, HEAD_DIM), me, 1, keepdims=False
    ).reshape(-1)
    segments = small[:, 26]
    places_all = small[:, 27]

    inputs = tok_all.reshape(-1, D).astype(f32)
    center = inputs - jnp.mean(inputs, axis=-1, keepdims=True)
    scale = lax.rsqrt(jnp.mean(center * center, axis=-1, keepdims=True) + 1e-05)
    norm = center * scale
    first = (norm * gain_one + shift_one).astype(bf16)
    second = (norm * gain_two + shift_two).astype(bf16)
    cot = cot_all.reshape(-1, D)

    widened = matmul(second, cols_two) + widen_bias
    cdf = 0.5 * (1.0 + lax.erf(widened * (0.5**0.5)))
    density = jnp.exp(-0.5 * widened * widened) * (1.0 / (2.0 * jnp.pi) ** 0.5)
    active = (widened * cdf).astype(bf16)
    slope = cdf + widened * density
    d_widened = (times_rows(cot, narrow_weight) * slope).astype(bf16)

    joint = matmul(first, cols_one) + head_bias
    cosine, sine = angles(places_all.reshape(-1))
    raw_q, raw_k, raw_v = (
        joint[:, i * HEAD_DIM : (i + 1) * HEAD_DIM] for i in range(3)
    )
    shape = (8, length, HEAD_DIM)
    query = (turn(raw_q, cosine, sine, 1.0) * HEAD_DIM**-0.5).astype(bf16).reshape(shape)
    keys = turn(raw_k, cosine, sine, 1.0).astype(bf16).reshape(shape)
    values = raw_v.astype(bf16).reshape(shape)
    order = jnp.arange(length)
    allowed = (segments[:, :, None] == segments[:, None, :]) & (
        order[:, None] >= order[None, :]
    )

    def batched(left, right, dims):
        return lax.dot_general(
            left, right, (dims, ((0,), (0,))), preferred_element_type=f32
        )

    scores = jnp.where(allowed, batched(query, keys, ((2,), (2,))), -1e30)
    highest = jnp.max(scores, axis=-1, keepdims=True)
    lifted = jnp.exp(scores - highest)
    probs = lifted / jnp.sum(lifted, axis=-1, keepdims=True)
    probs_low = probs.astype(bf16)
    context = batched(probs_low, values, ((2,), (1,))).astype(bf16)
    d_context = times_rows(cot, mixing_weight).astype(bf16).reshape(shape)
    d_probs = batched(d_context, values, ((2,), (2,)))
    d_values = batched(probs_low, d_context, ((1,), (1,)))
    d_scores = (
        probs * (d_probs - jnp.sum(d_probs * probs, axis=-1, keepdims=True))
    ).astype(bf16)
    d_query = batched(d_scores, keys, ((2,), (1,))).reshape(-1, HEAD_DIM)
    d_keys = batched(d_scores, query, ((1,), (1,))).reshape(-1, HEAD_DIM)
    d_joint = jnp.concatenate(
        [
            turn(d_query, cosine, sine, -1.0) * HEAD_DIM**-0.5,
            turn(d_keys, cosine, sine, -1.0),
            d_values.reshape(-1, HEAD_DIM),
        ],
        axis=1,
    ).astype(bf16)
    context = context.reshape(-1, HEAD_DIM)

    out_part = (matmul(context, mixing_weight) + matmul(active, narrow_weight)).astype(bf16)
    out_part = out_part.reshape(8, length, D)
    d_first = times_rows(d_joint, cols_one)
    d_second = times_rows(d_widened, cols_two)
    in_part = (d_first * gain_one + d_second * gain_two).astype(bf16)
    in_part = in_part.reshape(8, length, D)

    def quarters(array):
        return array.reshape(8, 4, -1, array.shape[1])

    grad_one = quarters(contract_rows(first, d_joint).astype(bf16))
    grad_two = quarters(contract_rows(second, d_widened).astype(bf16))
    grad_mix = contract_rows(context, cot).astype(bf16).reshape(4, -1, D)
    grad_narrow = contract_rows(active, cot).astype(bf16).reshape(4, -1, D)

    def at_own(array, count):
        zeros = jnp.zeros((8, count), f32)
        return lax.dynamic_update_slice(zeros, array.reshape(1, count), (me, 0))

    head_sums = jnp.sum(d_joint, axis=0, dtype=f32).reshape(3, 1, HEAD_DIM)
    head_sums = lax.dynamic_update_slice(
        jnp.zeros((3, HEADS, HEAD_DIM), f32), head_sums, (0, me, 0)
    )
    vec = jnp.concatenate(
        [
            jnp.sum(d_first * norm, axis=0).reshape(8, -1),
            jnp.sum(d_first, axis=0).reshape(8, -1),
            jnp.sum(d_second * norm, axis=0).reshape(8, -1),
            jnp.sum(d_second, axis=0).reshape(8, -1),
            head_sums.reshape(8, -1),
            jnp.sum(cotangent, axis=0, dtype=f32).reshape(8, -1),
            at_own(jnp.sum(d_widened, axis=0, dtype=f32), FF // 8),
        ],
        axis=1,
    ).reshape(8, 24, 128)

    out_sum, in_sum, full_one, full_two, full_mix, full_narrow, sums = gather_sums(
        out_part, in_part, grad_one, grad_two, grad_mix, grad_narrow, vec
    )
    own = tokens.astype(f32)
    own_center = own - jnp.mean(own, axis=-1, keepdims=True)
    own_scale = lax.rsqrt(
        jnp.mean(own_center * own_center, axis=-1, keepdims=True) + 1e-05
    )
    own_norm = own_center * own_scale
    output = (own + out_sum + out_bias).astype(bf16)
    pulled = own_scale * (
        in_sum
        - jnp.mean(in_sum, axis=-1, keepdims=True)
        - own_norm * jnp.mean(in_sum * own_norm, axis=-1, keepdims=True)
    )
    input_grad = (cotangent.astype(f32) + pulled).astype(bf16)
    flat = sums.reshape(-1)
    return (
        output,
        input_grad,
        flat[:256],
        flat[256:512],
        full_one.astype(f32),
        flat[1024:1792],
        full_mix.astype(f32),
        flat[1792:2048],
        flat[512:768],
        flat[768:1024],
        full_two.astype(f32),
        flat[2048:3072],
        full_narrow.astype(f32),
        flat[1792:2048],
    )


def solution(mesh):
    head_per_shard = mesh.shape["shard"] == HEADS and mesh.shape["rep"] == 4
    chosen = tensor_parallel if head_per_shard else per_device
    in_specs = (
        P(("rep", "shard"), None),
        P(("rep", "shard")),
        P(("rep", "shard")),
        P("shard"),
        P("shard"),
        P("shard", None),
        P("shard"),
        P("shard", None),
        P("shard"),
        P("shard"),
        P("shard"),
        P("shard", None),
        P("shard"),
        P("shard", None),
        P("shard"),
        P(("rep", "shard"), None),
    )
    out_specs = (
        P(("rep", "shard"), None),
        P(("rep", "shard"), None),
        P("shard"),
        P("shard"),
        P("shard", None),
        P("shard"),
        P("shard", None),
        P("shard"),
        P("shard"),
        P("shard"),
        P("shard", None),
        P("shard"),
        P("shard", None),
        P("shard"),
    )
    return jax.shard_map(
        chosen, mesh=mesh, in_specs=in_specs, out_specs=out_specs, check_vma=False
    )
```

```python
import math

import jax
import jax.numpy as jnp
from jax import lax
from jax.experimental import pallas as pl
from jax.experimental.pallas import tpu as pltpu
from jax.sharding import PartitionSpec as P

D = 2048
HEADS = 8
HEAD_DIM = 256
ROT = 64
FF = 8192


def layer_norm(values, gain, shift):
    center = values - jnp.mean(values, axis=-1, keepdims=True)
    spread = jnp.mean(center * center, axis=-1, keepdims=True)
    return center * lax.rsqrt(spread + 1e-05) * gain + shift


def angles(positions):
    freqs = 10000.0 ** (-(jnp.arange(ROT // 2, dtype=jnp.float32) * 2.0 / ROT))
    turned = positions.astype(jnp.float32)[..., None] * freqs
    return (jnp.cos(turned), jnp.sin(turned))


def rotary(values, cosine, sine):
    half = ROT // 2
    front = values[..., :half]
    back = values[..., half:ROT]
    return jnp.concatenate(
        [front * cosine - back * sine, back * cosine + front * sine, values[..., ROT:]], axis=-1
    )


def exact_gelu(values):
    return jax.nn.gelu(values, approximate=False)


def contract_rows(left, right):
    return lax.dot_general(
        left, right, (((0,), (0,)), ((), ())), preferred_element_type=jnp.float32
    )


def times_rows(left, piece):
    return lax.dot_general(
        left, piece, (((1,), (1,)), ((), ())), preferred_element_type=jnp.float32
    )


def weight_terms(left_one, left_two, left_mix, left_act, d_joint, d_widened, cotangent):

    def wide_term(start, count):
        return jnp.concatenate(
            [
                contract_rows(left_one, d_joint),
                contract_rows(left_two, d_widened),
                contract_rows(left_mix, cotangent),
            ],
            axis=1,
        )

    def down_term(start, count):
        return contract_rows(left_act, cotangent)

    return (wide_term, down_term)


def per_device(
    tokens,
    segment_ids,
    positions,
    first_gain,
    first_shift,
    project_weight,
    project_bias,
    mixing_weight,
    mixing_bias,
    second_gain,
    second_shift,
    widen_weight,
    widen_bias,
    narrow_weight,
    narrow_bias,
    cotangent,
):
    length = tokens.shape[0]
    shards = lax.axis_size("shard")
    gain_one, shift_one, gain_two, shift_two, joint_bias, mix_bias, wide_bias, narrow_full = (
        lax.all_gather(first_gain, "shard", axis=0, tiled=True),
        lax.all_gather(first_shift, "shard", axis=0, tiled=True),
        lax.all_gather(second_gain, "shard", axis=0, tiled=True),
        lax.all_gather(second_shift, "shard", axis=0, tiled=True),
        lax.all_gather(project_bias, "shard", axis=0, tiled=True),
        lax.all_gather(mixing_bias, "shard", axis=0, tiled=True),
        lax.all_gather(widen_bias, "shard", axis=0, tiled=True),
        lax.all_gather(narrow_bias, "shard", axis=0, tiled=True),
    )
    inputs = tokens.astype(jnp.float32)
    first_norm, first_pull = jax.vjp(layer_norm, inputs, gain_one, shift_one)
    second_norm, second_pull = jax.vjp(layer_norm, inputs, gain_two, shift_two)
    first = first_norm.astype(jnp.bfloat16)
    second = second_norm.astype(jnp.bfloat16)
    pieces = (
        lax.all_gather(project_weight, "shard", axis=0, tiled=True),
        lax.all_gather(widen_weight, "shard", axis=0, tiled=True),
    )
    part_one = jnp.dot(first, pieces[0], preferred_element_type=jnp.float32)
    part_two = jnp.dot(second, pieces[1], preferred_element_type=jnp.float32)
    joint = part_one + joint_bias
    widened = part_two + wide_bias
    shaped = joint.reshape(length, 3, HEADS, HEAD_DIM)
    cosine, sine = angles(positions)
    cosine = cosine[:, None, :]
    sine = sine[:, None, :]

    def place(query_in, key_in):
        return (rotary(query_in, cosine, sine) * HEAD_DIM ** (-0.5), rotary(key_in, cosine, sine))

    (query_turned, key_turned), rotate_pull = jax.vjp(place, shaped[:, 0], shaped[:, 1])
    query = query_turned.astype(jnp.bfloat16)
    keys = key_turned.astype(jnp.bfloat16)
    values = shaped[:, 2].astype(jnp.bfloat16)
    order = jnp.arange(length)
    allowed = ((segment_ids[:, None] == segment_ids[None, :]) & (order[:, None] >= order[None, :]))[
        None
    ]

    def masked_scores():
        raw = jnp.einsum("qhe,khe->hqk", query, keys, preferred_element_type=jnp.float32)
        return jnp.where(allowed, raw, -1e30)

    scores = masked_scores()
    highest = jnp.max(scores, axis=-1, keepdims=True)
    raised = jnp.exp(scores - highest)
    summed = jnp.sum(raised, axis=-1, keepdims=True)
    log_summed = highest + jnp.log(summed)
    weights = (raised / summed).astype(jnp.bfloat16)
    context = (
        jnp.einsum("hqk,khe->qhe", weights, values, preferred_element_type=jnp.float32)
        .reshape(length, D)
        .astype(jnp.bfloat16)
    )
    attention = (
        jnp.dot(
            context,
            lax.all_gather(mixing_weight, "shard", axis=0, tiled=True),
            preferred_element_type=jnp.float32,
        )
        + mix_bias
    )
    active_full, gelu_pull = jax.vjp(exact_gelu, widened)
    active = active_full.astype(jnp.bfloat16)
    mlp = (
        jnp.dot(
            active,
            lax.all_gather(narrow_weight, "shard", axis=0, tiled=True),
            preferred_element_type=jnp.float32,
        )
        + narrow_full
    )
    output = (inputs + attention + mlp).astype(jnp.bfloat16)

    def back_rows(piece):
        return times_rows(cotangent, piece)

    d_active = back_rows(lax.all_gather(narrow_weight, "shard", axis=0, tiled=True))
    d_widened = gelu_pull(d_active)[0].astype(jnp.bfloat16)
    d_context = back_rows(lax.all_gather(mixing_weight, "shard", axis=0, tiled=True))
    d_context = d_context.astype(jnp.bfloat16).reshape(length, HEADS, HEAD_DIM)
    again = jnp.exp(masked_scores() - log_summed)
    again_low = again.astype(jnp.bfloat16)
    d_weights = jnp.einsum("qhe,khe->hqk", d_context, values, preferred_element_type=jnp.float32)
    d_values = jnp.einsum("hqk,qhe->khe", again_low, d_context, preferred_element_type=jnp.float32)
    d_scores = (again * (d_weights - jnp.sum(d_weights * again, axis=-1, keepdims=True))).astype(
        jnp.bfloat16
    )
    d_query = jnp.einsum("hqk,khe->qhe", d_scores, keys, preferred_element_type=jnp.float32)
    d_keys = jnp.einsum("hqk,qhe->khe", d_scores, query, preferred_element_type=jnp.float32)
    d_query_in, d_key_in = rotate_pull((d_query, d_keys))
    d_joint = jnp.concatenate(
        [d_query_in.reshape(length, D), d_key_in.reshape(length, D), d_values.reshape(length, D)],
        axis=1,
    ).astype(jnp.bfloat16)
    pieces = lax.all_gather((project_weight, widen_weight), "shard", axis=0, tiled=True)
    stacked = jnp.concatenate(
        [times_rows(d_joint, pieces[0]), times_rows(d_widened, pieces[1])], axis=0
    )
    d_in_one, d_gain_one, d_shift_one = first_pull(stacked[:length])
    d_in_two, d_gain_two, d_shift_two = second_pull(stacked[length:])
    input_grad = (cotangent.astype(jnp.float32) + d_in_one + d_in_two).astype(jnp.bfloat16)
    sums = lax.psum(
        (
            d_gain_one,
            d_shift_one,
            d_gain_two,
            d_shift_two,
            jnp.sum(d_joint, axis=0, dtype=jnp.float32),
            jnp.sum(cotangent, axis=0, dtype=jnp.float32),
            jnp.sum(d_widened, axis=0, dtype=jnp.float32),
        ),
        ("rep", "shard"),
    )
    owner = lax.axis_index("shard")

    def own_part(vector):
        share = vector.shape[0] // shards
        return lax.dynamic_slice_in_dim(vector, owner * share, share)

    owned = [own_part(vector) for vector in sums]
    wide_term, down_term = weight_terms(
        first, second, context, active, d_joint, d_widened, cotangent
    )
    wide_part = lax.psum_scatter(
        wide_term(jnp.int32(0), lax.axis_size("shard") * (D // shards)).astype(jnp.bfloat16),
        "shard",
        scatter_dimension=0,
        tiled=True,
    ).astype(jnp.float32)
    down_part = lax.psum_scatter(
        down_term(jnp.int32(0), lax.axis_size("shard") * (FF // shards)).astype(jnp.bfloat16),
        "shard",
        scatter_dimension=0,
        tiled=True,
    ).astype(jnp.float32)
    wide_part, down_part = (
        lax.psum(wide_part.astype(jnp.bfloat16), "rep").astype(jnp.float32),
        lax.psum(down_part.astype(jnp.bfloat16), "rep").astype(jnp.float32),
    )
    return (
        output,
        input_grad,
        owned[0],
        owned[1],
        wide_part[:, : 3 * D],
        owned[4],
        wide_part[:, 3 * D + FF :],
        owned[5],
        owned[2],
        owned[3],
        wide_part[:, 3 * D : 3 * D + FF],
        owned[6],
        down_part,
        owned[5],
    )


MESH = pl.DeviceIdType.MESH
ANY = pl.BlockSpec(memory_space=pl.ANY)


def places():
    rep, me = lax.axis_index("rep"), lax.axis_index("shard")
    core, side = rep % 2, rep // 2
    col, line = me % 2, me // 2
    return rep, me, core, side, col, line


def greet(peers):
    barrier = pltpu.get_barrier_semaphore()
    for peer in peers:
        pl.semaphore_signal(barrier, inc=1, device_id=peer, device_id_type=MESH)
    pl.semaphore_wait(barrier, len(peers))


def remote(source, target, send, recv, device):
    return pltpu.make_async_remote_copy(
        src_ref=source,
        dst_ref=target,
        send_sem=send,
        recv_sem=recv,
        device_id=device,
        device_id_type=MESH,
    )


F32, BF16 = jnp.float32, jnp.bfloat16
CHUNK = 256


def turned(value, cosine, sine):
    near = value[:, :128]
    lane = lax.broadcasted_iota(jnp.int32, near.shape, 1)
    partner = jnp.where(
        lane < ROT // 2,
        pltpu.roll(near, 128 - ROT // 2, 1),
        pltpu.roll(near, ROT // 2, 1),
    )
    return jnp.concatenate([near * cosine + partner * sine, value[:, 128:]], axis=1)


def dot(left, right, dims=((1,), (0,))):
    return lax.dot_general(left, right, (dims, ((), ())), preferred_element_type=F32)


def forward_kernel(
    tok, cot, wide_one, wide_two, mix, narrow,
    gain_one, shift_one, gain_two, shift_two, mix_bias, narrow_bias, joint_bias, wide_bias,
    segments, positions,
    cot_all, tok_out, cols_one_out, cols_two_out, first_out, second_out,
    query_out, key_out, value_out, probs_out, context_out, active_out, slope_out,
    out_part, gains_out, bias_out,
    tok_all, cols_one, cols_two, mix_v, narrow_v, first, second, joint, query, key, value,
    probs, context, active, slope, partial, small, small_all, table,
    line_send, line_recv, col_send, col_recv,
    own_sem, piece_send, piece_recv, side_send, side_recv, core_send, core_recv,
    small_send, small_recv, load_sem, save_sem,
):
    rep, me, core, side, col, line = places()
    twin = rep + 1 - 2 * core
    across = rep + 2 - 4 * side
    twin_across = across + 1 - 2 * core
    other = me + 1 - 2 * col
    wide = cols_one.shape[1] // 3
    two_wide = cols_two.shape[1]
    rows = wide_one.shape[0]
    share = rows // 4
    length = tok.shape[0]
    width = tok.shape[1]

    offset = 0
    for ref in (gain_one, shift_one, gain_two, shift_two, mix_bias, narrow_bias, joint_bias,
                wide_bias, segments, positions):
        count = ref.shape[0]
        small[0:1, offset : offset + count] = ref[...].astype(F32)[None, :]
        offset += count

    greet(
        [(rep, (me + step) % 8) for step in range(1, 8)]
        + [(twin, me), (across, me)]
    )

    def along(which, array, gathered, direction, step):
        owner = line - direction * (step - 1)
        source = array if step == 1 else gathered.at[owner * 2 + col]
        lane = which * 6 + (0 if direction == 1 else 3) + step - 1
        return remote(
            source,
            gathered.at[owner * 2 + col],
            line_send.at[lane],
            line_recv.at[lane],
            (rep, (line + direction) * 2 + col),
        )

    def sends(direction, step):
        if direction == 1:
            return (line >= step - 1) & (line <= 2)
        return (line <= 4 - step) & (line >= 1)

    def gets(direction, step):
        if direction == 1:
            return line >= step
        return line <= 3 - step

    def sideways(which, array, gathered, direction, step):
        owner = line - direction * step
        source = array if step == 0 else gathered.at[owner * 2 + col]
        lane = which * 7 + (0 if direction == 1 else 3) + step
        return remote(
            source,
            gathered.at[owner * 2 + col],
            col_send.at[lane],
            col_recv.at[lane],
            (rep, other),
        )

    def from_other(which, gathered, direction, step):
        owner = line - direction * step
        lane = which * 7 + (0 if direction == 1 else 3) + step
        here = gathered.at[owner * 2 + 1 - col]
        return remote(here, here, col_send.at[lane], col_recv.at[lane], (rep, other))

    pairs = ((tok, tok_all), (cot, cot_all))
    turns = [(direction, step) for step in (1, 2, 3) for direction in (1, -1)]

    def begin(which):
        array, gathered = pairs[which]
        for direction in (1, -1):
            @pl.when(sends(direction, 1))
            def _(direction=direction):
                along(which, array, gathered, direction, 1).start()
        sideways(which, array, gathered, 1, 0).start()

    def pass_on(which, direction, step):
        array, gathered = pairs[which]

        @pl.when(gets(direction, step))
        def _():
            owner = line - direction * step
            lane = which * 6 + (0 if direction == 1 else 3) + step - 1
            here = gathered.at[owner * 2 + col]
            remote(
                here, here, line_send.at[lane], line_recv.at[lane], (rep, other)
            ).wait_recv()
            sideways(which, array, gathered, direction, step).start()

        if step < 3:
            @pl.when(sends(direction, step + 1))
            def _():
                along(which, array, gathered, direction, step + 1).start()

    def landed(which):
        gathered = pairs[which][1]
        for direction, step in turns:
            @pl.when(gets(direction, step))
            def _(direction=direction, step=step):
                from_other(which, gathered, direction, step).wait_recv()

        from_other(which, gathered, 1, 0).wait_recv()

    def sent(which):
        array, gathered = pairs[which]
        for direction, step in turns:
            @pl.when(sends(direction, step))
            def _(direction=direction, step=step):
                along(which, array, gathered, direction, step).wait_send()

            @pl.when(gets(direction, step))
            def _(direction=direction, step=step):
                sideways(which, array, gathered, direction, step).wait_send()

        sideways(which, array, gathered, 1, 0).wait_send()

    mine = pl.multiple_of(rep * share, share)

    def pieces(step):
        target = (me + step) % 8
        place = pl.ds(pl.multiple_of(me * rows + rep * share, share), share)
        out = []
        for part in range(3):
            out.append(
                remote(
                    wide_one.at[
                        pl.ds(mine, share),
                        pl.ds(pl.multiple_of((part * 8 + target) * wide, wide), wide),
                    ],
                    cols_one.at[place, pl.ds(part * wide, wide)],
                    piece_send.at[step - 1, part],
                    piece_recv.at[step - 1, part],
                    (rep, target),
                )
            )
        out.append(
            remote(
                wide_two.at[
                    pl.ds(mine, share),
                    pl.ds(pl.multiple_of(target * two_wide, two_wide), two_wide),
                ],
                cols_two.at[place, :],
                piece_send.at[step - 1, 3],
                piece_recv.at[step - 1, 3],
                (rep, target),
            )
        )
        return out

    def arrived(step):
        source = (me + 8 - step) % 8
        place = pl.ds(pl.multiple_of(source * rows + rep * share, share), share)
        here = [cols_one.at[place, pl.ds(part * wide, wide)] for part in range(3)]
        here.append(cols_two.at[place, :])
        return [
            remote(
                ref, ref, piece_send.at[step - 1, part], piece_recv.at[step - 1, part],
                (rep, source),
            )
            for part, ref in enumerate(here)
        ]

    def shares(step, quarter, send, recv, lane, device):
        source = (me + 8 - step) % 8
        place = pl.ds(pl.multiple_of(source * rows + quarter * share, share), share)
        return [
            remote(
                array.at[place, :], array.at[place, :],
                send.at[lane, step - 1, index], recv.at[lane, step - 1, index], device,
            )
            for index, array in enumerate((cols_one, cols_two))
        ]

    def little(step):
        return remote(
            small, small_all.at[me], small_send.at[step - 1], small_recv.at[step - 1],
            (rep, (me + step) % 8),
        )

    begin(0)
    for step in range(1, 8):
        little(step).start()
    for step in range(1, 8):
        for copy in pieces(step):
            copy.start()
    here = pl.ds(pl.multiple_of(me * rows, rows), rows)
    own = [
        pltpu.make_async_copy(tok, tok_all.at[me], own_sem.at[0]),
        pltpu.make_async_copy(cot, cot_all.at[me], own_sem.at[1]),
        pltpu.make_async_copy(small, small_all.at[me], own_sem.at[2]),
        pltpu.make_async_copy(
            wide_two.at[:, pl.ds(pl.multiple_of(me * two_wide, two_wide), two_wide)],
            cols_two.at[here, :],
            own_sem.at[3],
        ),
    ] + [
        pltpu.make_async_copy(
            wide_one.at[:, pl.ds(pl.multiple_of((part * 8 + me) * wide, wide), wide)],
            cols_one.at[here, pl.ds(part * wide, wide)],
            own_sem.at[4 + part],
        )
        for part in range(3)
    ]
    for copy in own:
        copy.start()
    loads = [
        pltpu.make_async_copy(mix, mix_v, load_sem.at[0]),
        pltpu.make_async_copy(narrow, narrow_v, load_sem.at[1]),
    ]
    for copy in loads:
        copy.start()
    for direction, step in turns:
        pass_on(0, direction, step)
    begin(1)
    for step in range(1, 8):
        source = (me + 8 - step) % 8
        remote(
            small_all.at[source], small_all.at[source], small_send.at[step - 1],
            small_recv.at[step - 1], (rep, source),
        ).wait_recv()
    own[0].wait()
    own[2].wait()
    for kind in range(6):
        for shard in range(8):
            table[kind : kind + 1, shard * 256 : shard * 256 + 256] = small_all[
                shard, :, kind * 256 : kind * 256 + 256
            ]
    for step in range(1, 8):
        for copy in arrived(step):
            copy.wait_recv()
        for copy in shares(step, rep, side_send, side_recv, 0, (across, me)):
            copy.start()
        for copy in shares(step, rep, core_send, core_recv, 0, (twin, me)):
            copy.start()
    landed(0)

    gains_one, shifts_one = table[0:1, :], table[1:2, :]
    gains_two, shifts_two = table[2:3, :], table[3:4, :]

    @pl.loop(0, 8 * length // 32)
    def _(index):
        block, part = index // (length // 32), index % (length // 32)
        at = pl.ds(pl.multiple_of(part * 32, 32), 32)
        raw = tok_all[block, at, :].astype(F32)
        center = raw - jnp.mean(raw, axis=-1, keepdims=True)
        spread = jnp.mean(center * center, axis=-1, keepdims=True)
        norm = center * lax.rsqrt(spread + 1e-05)
        there = pl.ds(pl.multiple_of(index * 32, 32), 32)
        first[there, :] = (norm * gains_one + shifts_one).astype(BF16)
        second[there, :] = (norm * gains_two + shifts_two).astype(BF16)

    saves = [
        pltpu.make_async_copy(tok_all, tok_out, save_sem.at[0]),
        pltpu.make_async_copy(first, first_out, save_sem.at[1]),
        pltpu.make_async_copy(second, second_out, save_sem.at[2]),
    ]
    for copy in saves:
        copy.start()

    for step in range(1, 8):
        for copy in shares(step, across, side_send, side_recv, 0, (across, me)):
            copy.wait_recv()
        for copy in shares(step, across, core_send, core_recv, 1, (twin, me)):
            copy.start()
    for step in range(1, 8):
        for copy in shares(step, twin, core_send, core_recv, 0, (twin, me)):
            copy.wait_recv()
    for step in range(1, 8):
        for copy in shares(step, twin_across, core_send, core_recv, 1, (twin, me)):
            copy.wait_recv()
    for copy in own[3:]:
        copy.wait()
    for copy in loads:
        copy.wait()
    late = [
        pltpu.make_async_copy(cols_one, cols_one_out, save_sem.at[3]),
        pltpu.make_async_copy(cols_two, cols_two_out, save_sem.at[4]),
    ]
    for copy in late:
        copy.start()
    saves += late

    for part in range(3):
        spot = part * 8 + me
        table[6:7, part * wide : (part + 1) * wide] = small_all[
            spot // 3, :, pl.ds(pl.multiple_of(1536 + (spot % 3) * 256, 256), 256)
        ]
    bias_row = table[6:7, 0 : 3 * wide]
    wide_row = small[0:1, 2304 : 2304 + two_wide]

    def project(start):
        at = pl.ds(start, CHUNK)
        for part in range(3):
            spot = slice(part * wide, (part + 1) * wide)
            joint[at, spot] = dot(first[at, :], cols_one[:, spot]) + bias_row[:, spot]
        for part in range(two_wide // 256):
            spot = slice(part * 256, (part + 1) * 256)
            value_now = dot(second[at, :], cols_two[:, spot]) + wide_row[:, spot]
            cdf = 0.5 * (1.0 + lax.erf(value_now * (0.5**0.5)))
            density = jnp.exp(-0.5 * value_now * value_now) * (0.5 / jnp.pi) ** 0.5
            active[at, spot] = (value_now * cdf).astype(BF16)
            slope[at, spot] = (cdf + value_now * density).astype(BF16)

    lane = lax.broadcasted_iota(jnp.int32, (1, 128), 1)
    frequency = jnp.where(
        lane < ROT,
        jnp.exp((lane % (ROT // 2)).astype(F32) * (-2.0 / ROT * math.log(10000.0))),
        0.0,
    )
    signs = jnp.where(lane < ROT // 2, -1.0, 1.0)
    tall = lax.broadcasted_iota(jnp.int32, (length, length), 0)
    flat = lax.broadcasted_iota(jnp.int32, (length, length), 1)
    ids_at = 2304 + two_wide

    def attend(block, start):
        at = pl.ds(start, length)
        ids = jnp.broadcast_to(small_all[block, :, ids_at : ids_at + 128], (length, length))
        spots = jnp.broadcast_to(
            small_all[block, :, ids_at + 128 : ids_at + 256], (length, length)
        )
        angle = spots.T * frequency
        cosine, sine = jnp.cos(angle), jnp.sin(angle) * signs
        query_now = (turned(joint[at, 0:wide], cosine, sine) * HEAD_DIM**-0.5).astype(BF16)
        key_now = turned(joint[at, wide : 2 * wide], cosine, sine).astype(BF16)
        value_now = joint[at, 2 * wide :].astype(BF16)
        scores = dot(query_now, key_now, ((1,), (1,)))
        allowed = (ids == ids.T) & (flat <= tall)
        scores = jnp.where(allowed, scores, -1e30)
        lifted = jnp.exp(scores - jnp.max(scores, axis=-1, keepdims=True))
        weights = lifted / jnp.sum(lifted, axis=-1, keepdims=True)
        query[at, :], key[at, :], value[at, :] = query_now, key_now, value_now
        probs[at, :] = weights
        context[at, :] = dot(weights.astype(BF16), value_now).astype(BF16)

    def finish(start):
        at = pl.ds(start, CHUNK)
        for part in range(width // 256):
            spot = slice(part * 256, (part + 1) * 256)
            partial[at, spot] = (
                dot(context[at, :], mix_v[:, spot]) + dot(active[at, :], narrow_v[:, spot])
            ).astype(BF16)

    pending = list(turns)
    for index in range(8 * length // CHUNK):
        project(index * CHUNK)
        for direction, step in pending[:1]:
            pass_on(1, direction, step)
        pending = pending[1:]
        for part in range(CHUNK // length):
            block = index * (CHUNK // length) + part
            attend(block, block * length)
        finish(index * CHUNK)
        for direction, step in pending[:1]:
            pass_on(1, direction, step)
        pending = pending[1:]
    for direction, step in pending:
        pass_on(1, direction, step)
    gains_out[...] = table[...]
    bias_out[...] = table[4:5, :] + table[5:6, :]
    late = [
        pltpu.make_async_copy(source, target, save_sem.at[5 + index])
        for index, (source, target) in enumerate(
            (
                (query, query_out), (key, key_out), (value, value_out), (probs, probs_out),
                (context, context_out), (active, active_out), (slope, slope_out),
                (partial, out_part),
            )
        )
    ]
    for copy in late:
        copy.start()
    saves += late

    sent(0)
    for step in range(1, 8):
        for copy in pieces(step):
            copy.wait_send()
        for copy in shares(step, rep, side_send, side_recv, 0, (across, me)):
            copy.wait_send()
        for copy in shares(step, rep, core_send, core_recv, 0, (twin, me)):
            copy.wait_send()
        for copy in shares(step, across, core_send, core_recv, 1, (twin, me)):
            copy.wait_send()
        little(step).wait_send()
    own[1].wait()
    for copy in saves:
        copy.wait()
    sent(1)
    landed(1)


def forward(tok, cot, wide_one, wide_two, mix, narrow, vectors):
    dma = pltpu.SemaphoreType.DMA
    length, width = tok.shape
    rows, one = wide_one.shape
    two = wide_two.shape[1]
    one, two = one // 8, two // 8
    total = 8 * length
    struct = jax.ShapeDtypeStruct
    vmem = pl.BlockSpec(memory_space=pltpu.VMEM)
    saved = [
        ((total, HEAD_DIM), BF16), ((total, HEAD_DIM), BF16), ((total, HEAD_DIM), BF16),
        ((total, length), F32), ((total, HEAD_DIM), BF16), ((total, two), BF16),
        ((total, two), BF16), ((total, width), BF16),
    ]
    packed = sum(v.shape[0] for v in vectors)
    return pl.pallas_call(
        forward_kernel,
        out_shape=(
            struct((8, length, width), BF16),
            struct((8, length, width), BF16),
            struct((rows * 8, one), BF16),
            struct((rows * 8, two), BF16),
            struct((total, width), BF16),
            struct((total, width), BF16),
        )
        + tuple(struct(*s) for s in saved)
        + (struct((8, width), F32), struct((1, width), F32)),
        in_specs=[ANY] * 6 + [vmem] * len(vectors),
        out_specs=(ANY,) * 14 + (vmem,) * 2,
        scratch_shapes=[
            pltpu.VMEM((8, length, width), BF16),
            pltpu.VMEM((rows * 8, one), BF16),
            pltpu.VMEM((rows * 8, two), BF16),
            pltpu.VMEM(mix.shape, BF16),
            pltpu.VMEM(narrow.shape, BF16),
            pltpu.VMEM((total, width), BF16),
            pltpu.VMEM((total, width), BF16),
            pltpu.VMEM((total, one), F32),
        ]
        + [pltpu.VMEM(*s) for s in saved]
        + [
            pltpu.VMEM((1, packed), F32),
            pltpu.VMEM((8, 1, packed), F32),
            pltpu.VMEM((8, width), F32),
            dma((12,)), dma((12,)), dma((14,)), dma((14,)),
            dma((7,)), dma((7, 4)), dma((7, 4)),
            dma((1, 7, 2)), dma((1, 7, 2)), dma((2, 7, 2)), dma((2, 7, 2)),
            dma((7,)), dma((7,)), dma((2,)), dma((13,)),
        ],
        compiler_params=pltpu.CompilerParams(
            collective_id=0, has_side_effects=True, vmem_limit_bytes=60 << 20
        ),
        name="forward",
    )(tok, cot, wide_one, wide_two, mix, narrow, *vectors)


def rows_loop(extent, chunk, body):
    @pl.loop(0, extent // chunk)
    def _(index):
        body(pl.ds(pl.multiple_of(index * chunk, chunk), chunk))


def add_two(target, left, right, chunk):
    def body(rows):
        target[rows, :] = (
            left[rows, :].astype(jnp.float32) + right[rows, :].astype(jnp.float32)
        ).astype(target.dtype)

    rows_loop(target.shape[0], chunk, body)


def add_three(target, left, right, third, chunk):
    def body(rows):
        target[rows, :] = (
            left[rows, :].astype(jnp.float32)
            + right[rows, :].astype(jnp.float32)
            + third[rows, :].astype(jnp.float32)
        ).astype(target.dtype)

    rows_loop(target.shape[0], chunk, body)


def gather_sums_kernel(
    out_part, in_part, one, two, mix, narrow, vec,
    out_sum, in_sum, one_full, two_full, mix_full, narrow_full, vec_full,
    loc_one, loc_two, loc_mix, loc_nar,
    core_one, core_two, core_mix, core_nar,
    side_one, side_two, side_mix, side_nar,
    loc_act, col_act, line_act, total, vec_loc, vec_got, vec_mid, vec_rep,
    load_sem, cs, cr, ss, sr, ys, yr, zs, zr, ps, pr, fs, fr, vs, vr, us, ur, ds_sem,
):
    rep, me, core, side, col, line = places()
    twin = rep + 1 - 2 * core
    across = rep + 2 - 4 * side
    diagonal = across + 1 - 2 * core
    other = me + 1 - 2 * col
    greet(
        [(rep, (me + step) % 8) for step in range(1, 8)]
        + [(twin, me), (across, me), (diagonal, me)]
    )
    grads = (
        (one, loc_one, core_one, side_one),
        (two, loc_two, core_two, side_two),
        (mix, loc_mix, core_mix, side_mix),
        (narrow, loc_nar, core_nar, side_nar),
    )
    acts = (out_part, in_part)

    def quarter_of(index, quarter):
        full = grads[index][0]
        return full.at[:, quarter] if index < 2 else full.at[quarter]

    def core_copy(index, slot):
        full, _, got, _ = grads[index]
        quarter = (across if slot == 0 else rep) + 1 - 2 * core
        return remote(
            quarter_of(index, quarter), got.at[slot], cs.at[index, slot], cr.at[index, slot],
            (twin, me),
        )

    def load(index, slot):
        full, local, _, _ = grads[index]
        quarter = across if slot == 0 else rep
        return pltpu.make_async_copy(
            quarter_of(index, quarter), local.at[slot], load_sem.at[index, slot]
        )

    def side_copy(index):
        _, local, _, got = grads[index]
        return remote(local.at[0], got, ss.at[index], sr.at[index], (across, me))

    def col_copy(index, step):
        target = (line + step) % 4
        return remote(
            acts[index].at[target * 2 + 1 - col], col_act.at[index, step],
            ys.at[index, step], yr.at[index, step], (rep, other),
        )

    def act_load(index, step):
        target = (line + step) % 4
        return pltpu.make_async_copy(
            acts[index].at[target * 2 + col], loc_act.at[index, step],
            load_sem.at[4 + index, step],
        )

    def line_copy(index, step):
        return remote(
            loc_act.at[index, step], line_act.at[index, step - 1],
            zs.at[index, step - 1], zr.at[index, step - 1],
            (rep, ((line + step) % 4) * 2 + col),
        )

    def vec_copy(step):
        target = (me + step) % 8
        return remote(
            vec.at[target], vec_got.at[step - 1], vs.at[step - 1], vr.at[step - 1],
            (rep, target),
        )

    def vec_share(step):
        target = (rep + step) % 4
        return remote(
            vec_mid, vec_rep.at[step - 1], us.at[step - 1], ur.at[step - 1],
            (target, me),
        )

    for index in (0, 1):
        for slot in (0, 1):
            core_copy(index, slot).start()
            load(index, slot).start()
    for index in (2, 3):
        for slot in (0, 1):
            core_copy(index, slot).start()
            load(index, slot).start()
    for step in range(1, 8):
        vec_copy(step).start()
    vec_load = pltpu.make_async_copy(vec.at[me], vec_loc, ds_sem.at[0])
    vec_load.start()
    for index in (0, 1):
        for step in (2, 1, 3, 0):
            col_copy(index, step).start()
            act_load(index, step).start()

    def flat(ref):
        if len(ref.shape) == 3:
            return [ref.at[i] for i in range(ref.shape[0])]
        return [ref]

    for index in range(4):
        _, local, got, _ = grads[index]
        core_copy(index, 0).wait_recv()
        load(index, 0).wait()
        for here, there in zip(flat(local.at[0]), flat(got.at[0])):
            add_two(here, here, there, 16)
        side_copy(index).start()

    for index in (0, 1):
        for step in (2, 1, 3):
            col_copy(index, step).wait_recv()
            act_load(index, step).wait()
            here = loc_act.at[index, step]
            add_two(here, here, col_act.at[index, step], 16)
            line_copy(index, step).start()

    vec_load.wait()
    for step in range(1, 8):
        vec_copy(step).wait_recv()
    running = vec_loc[...]
    for step in range(1, 8):
        running = running + vec_got[step - 1]
    vec_mid[...] = running
    for step in range(1, 4):
        vec_share(step).start()

    share_one = one_full.shape[0] // 4
    wide = loc_one.shape[3] // 3
    two_wide = loc_two.shape[3]
    my_rows = pl.ds(pl.multiple_of(rep * share_one, share_one), share_one)

    def whole(index):
        _, local, got, arrived = grads[index]
        core_copy(index, 1).wait_recv()
        load(index, 1).wait()
        side_copy(index).wait_recv()
        for here, there, far in zip(flat(local.at[1]), flat(got.at[1]), flat(arrived)):
            add_three(here, here, there, far, 16)

    def piece(index, step, part, source_shard, target_shard, local):
        if index == 0:
            return remote(
                local.at[:, pl.ds(part * wide, wide)],
                one_full.at[
                    my_rows,
                    pl.ds(pl.multiple_of((part * 8 + source_shard) * wide, wide), wide),
                ],
                ps.at[step, part], pr.at[step, part], (rep, target_shard),
            )
        return remote(
            local,
            two_full.at[
                my_rows, pl.ds(pl.multiple_of(source_shard * two_wide, two_wide), two_wide)
            ],
            ps.at[step, 3], pr.at[step, 3], (rep, target_shard),
        )

    def pieces(index, step, source_shard, target_shard):
        local = grads[index][1].at[1, target_shard]
        parts = range(3) if index == 0 else (0,)
        return [
            piece(index, step, part, source_shard, target_shard, local) for part in parts
        ]

    def own_pieces(index):
        if index == 0:
            return [
                pltpu.make_async_copy(
                    loc_one.at[1, me, :, pl.ds(part * wide, wide)],
                    one_full.at[
                        my_rows,
                        pl.ds(pl.multiple_of((part * 8 + me) * wide, wide), wide),
                    ],
                    ds_sem.at[1 + part],
                )
                for part in range(3)
            ]
        return [
            pltpu.make_async_copy(
                loc_two.at[1, me],
                two_full.at[
                    my_rows, pl.ds(pl.multiple_of(me * two_wide, two_wide), two_wide)
                ],
                ds_sem.at[4],
            )
        ]

    for index in (0, 1):
        whole(index)
        for step in range(1, 8):
            for copy in pieces(index, step, me, (me + step) % 8):
                copy.start()
        for copy in own_pieces(index):
            copy.start()

    fulls = (one_full, two_full, mix_full, narrow_full)

    def spot(index, quarter):
        count = fulls[index].shape[0] // 4
        return fulls[index].at[pl.ds(pl.multiple_of(quarter * count, count), count), :]

    def hand(index, lane, source, quarter, device):
        return remote(
            source, spot(index, quarter), fs.at[index, lane], fr.at[index, lane], device
        )

    own_full = []
    for index in (2, 3):
        whole(index)
        source = grads[index][1].at[1]
        hand(index, 0, source, rep, (across, me)).start()
        hand(index, 1, source, rep, (twin, me)).start()
        copy = pltpu.make_async_copy(source, spot(index, rep), ds_sem.at[3 + index])
        copy.start()
        own_full.append(copy)

    for index in (0, 1):
        for copy in own_pieces(index):
            copy.wait()
        for step in range(1, 8):
            source_shard = (me + 8 - step) % 8
            for copy in pieces(index, step, source_shard, me):
                copy.wait_recv()
        hand(index, 0, spot(index, rep), rep, (across, me)).start()
        hand(index, 1, spot(index, rep), rep, (twin, me)).start()

    for index in (0, 1):
        col_copy(index, 0).wait_recv()
        act_load(index, 0).wait()
        for step in range(1, 4):
            line_copy(index, step).wait_recv()

        def body(rows, index=index):
            value = loc_act[index, 0, rows, :].astype(jnp.float32)
            value = value + col_act[index, 0, rows, :].astype(jnp.float32)
            for step in range(3):
                value = value + line_act[index, step, rows, :].astype(jnp.float32)
            total[index, rows, :] = value

        rows_loop(total.shape[1], 16, body)
    outs = [
        pltpu.make_async_copy(total.at[0], out_sum, ds_sem.at[7]),
        pltpu.make_async_copy(total.at[1], in_sum, ds_sem.at[8]),
    ]
    for copy in outs:
        copy.start()

    for step in range(1, 4):
        vec_share(step).wait_recv()
    vec_full[...] = vec_mid[...] + vec_rep[0] + vec_rep[1] + vec_rep[2]

    for index in (2, 3, 0, 1):
        hand(index, 0, spot(index, across), across, (across, me)).wait_recv()
        hand(index, 2, spot(index, across), across, (twin, me)).start()
    for index in range(4):
        source = grads[index][1].at[1] if index > 1 else spot(index, rep)
        hand(index, 0, source, rep, (across, me)).wait_send()
        hand(index, 1, source, rep, (twin, me)).wait_send()
        hand(index, 1, spot(index, twin), twin, (twin, me)).wait_recv()
        hand(index, 2, spot(index, across), across, (twin, me)).wait_send()
        hand(index, 2, spot(index, diagonal), diagonal, (twin, me)).wait_recv()
        side_copy(index).wait_send()
        for slot in (0, 1):
            core_copy(index, slot).wait_send()
    for index in (0, 1):
        for step in range(1, 8):
            for copy in pieces(index, step, me, (me + step) % 8):
                copy.wait_send()
        for step in range(4):
            col_copy(index, step).wait_send()
            if step:
                line_copy(index, step).wait_send()
    for step in range(1, 8):
        vec_copy(step).wait_send()
    for step in range(1, 4):
        vec_share(step).wait_send()
    for copy in own_full + outs:
        copy.wait()


def gather_sums(out_part, in_part, one, two, mix, narrow, vec):
    dma = pltpu.SemaphoreType.DMA
    bf16, f32 = jnp.bfloat16, jnp.float32
    _, length, width = out_part.shape
    shards, _, share, one_wide = one.shape
    two_wide = two.shape[3]
    struct = jax.ShapeDtypeStruct
    grads = [(g.shape[0],) + g.shape[2:] for g in (one, two)]
    grads += [g.shape[1:] for g in (mix, narrow)]
    return pl.pallas_call(
        gather_sums_kernel,
        out_shape=(
            struct((length, width), f32),
            struct((length, width), f32),
            struct((4 * share, shards * one_wide), bf16),
            struct((4 * share, shards * two_wide), bf16),
            struct((4 * mix.shape[1], width), bf16),
            struct((4 * narrow.shape[1], width), bf16),
            struct(vec.shape[1:], f32),
        ),
        in_specs=[ANY] * 7,
        out_specs=(ANY,) * 6 + (pl.BlockSpec(memory_space=pltpu.VMEM),),
        scratch_shapes=[pltpu.VMEM((2,) + g, bf16) for g in grads]
        + [pltpu.VMEM((2,) + g, bf16) for g in grads]
        + [pltpu.VMEM(g, bf16) for g in grads]
        + [
            pltpu.VMEM((2, 4, length, width), bf16),
            pltpu.VMEM((2, 4, length, width), bf16),
            pltpu.VMEM((2, 3, length, width), bf16),
            pltpu.VMEM((2, length, width), f32),
            pltpu.VMEM(vec.shape[1:], f32),
            pltpu.VMEM((7,) + vec.shape[1:], f32),
            pltpu.VMEM(vec.shape[1:], f32),
            pltpu.VMEM((3,) + vec.shape[1:], f32),
            dma((6, 4)),
            dma((4, 2)), dma((4, 2)), dma((4,)), dma((4,)),
            dma((2, 4)), dma((2, 4)), dma((2, 3)), dma((2, 3)),
            dma((8, 4)), dma((8, 4)), dma((4, 3)), dma((4, 3)),
            dma((7,)), dma((7,)), dma((3,)), dma((3,)), dma((9,)),
        ],
        compiler_params=pltpu.CompilerParams(
            collective_id=1, has_side_effects=True, vmem_limit_bytes=56 << 20
        ),
        name="gather_sums",
    )(out_part, in_part, one, two, mix, narrow, vec)


def turn(values, cosine, sine, sign):
    half = ROT // 2
    front, back = values[..., :half], values[..., half:ROT]
    return jnp.concatenate(
        [
            front * cosine - sign * back * sine,
            back * cosine + sign * front * sine,
            values[..., ROT:],
        ],
        axis=-1,
    )


def matmul(left, right):
    return jnp.dot(left, right, preferred_element_type=jnp.float32)


def tensor_parallel(
    tokens,
    segment_ids,
    positions,
    first_gain,
    first_shift,
    project_weight,
    project_bias,
    mixing_weight,
    mixing_bias,
    second_gain,
    second_shift,
    widen_weight,
    widen_bias,
    narrow_weight,
    narrow_bias,
    cotangent,
):
    f32, bf16 = jnp.float32, jnp.bfloat16
    length = tokens.shape[0]
    me = lax.axis_index("shard")
    (
        cot_all, tok_all, cols_one, cols_two, first, second, query, keys, values, probs,
        context, active, slope, out_part, table, out_bias,
    ) = forward(
        tokens, cotangent, project_weight, widen_weight, mixing_weight, narrow_weight,
        (
            first_gain, first_shift, second_gain, second_shift, mixing_bias, narrow_bias,
            project_bias, widen_bias, segment_ids, positions,
        ),
    )
    gain_one, gain_two = table[0], table[2]
    inputs = tok_all.reshape(-1, D).astype(f32)
    center = inputs - jnp.mean(inputs, axis=-1, keepdims=True)
    scale = lax.rsqrt(jnp.mean(center * center, axis=-1, keepdims=True) + 1e-05)
    norm = center * scale
    cot = cot_all.reshape(-1, D)
    d_widened = (times_rows(cot, narrow_weight) * slope.astype(f32)).astype(bf16)
    shape = (8, length, HEAD_DIM)
    query, keys, values = (item.reshape(shape) for item in (query, keys, values))
    probs = probs.reshape(8, length, length)
    probs_low = probs.astype(bf16)
    places_all = lax.all_gather(positions, "shard", axis=0, tiled=True)
    cosine, sine = angles(places_all)

    def batched(left, right, dims):
        return lax.dot_general(
            left, right, (dims, ((0,), (0,))), preferred_element_type=f32
        )

    d_context = times_rows(cot, mixing_weight).astype(bf16).reshape(shape)
    d_probs = batched(d_context, values, ((2,), (2,)))
    d_values = batched(probs_low, d_context, ((1,), (1,)))
    d_scores = (
        probs * (d_probs - jnp.sum(d_probs * probs, axis=-1, keepdims=True))
    ).astype(bf16)
    d_query = batched(d_scores, keys, ((2,), (1,))).reshape(-1, HEAD_DIM)
    d_keys = batched(d_scores, query, ((1,), (1,))).reshape(-1, HEAD_DIM)
    d_joint = jnp.concatenate(
        [
            turn(d_query, cosine, sine, -1.0) * HEAD_DIM**-0.5,
            turn(d_keys, cosine, sine, -1.0),
            d_values.reshape(-1, HEAD_DIM),
        ],
        axis=1,
    ).astype(bf16)
    out_part = out_part.reshape(8, length, D)
    d_first = times_rows(d_joint, cols_one)
    d_second = times_rows(d_widened, cols_two)
    in_part = (d_first * gain_one + d_second * gain_two).astype(bf16)
    in_part = in_part.reshape(8, length, D)

    def quarters(array):
        return array.reshape(8, 4, -1, array.shape[1])

    grad_one = quarters(contract_rows(first, d_joint).astype(bf16))
    grad_two = quarters(contract_rows(second, d_widened).astype(bf16))
    grad_mix = contract_rows(context, cot).astype(bf16).reshape(4, -1, D)
    grad_narrow = contract_rows(active, cot).astype(bf16).reshape(4, -1, D)

    def at_own(array, count):
        zeros = jnp.zeros((8, count), f32)
        return lax.dynamic_update_slice(zeros, array.reshape(1, count), (me, 0))

    head_sums = jnp.sum(d_joint, axis=0, dtype=f32).reshape(3, 1, HEAD_DIM)
    head_sums = lax.dynamic_update_slice(
        jnp.zeros((3, HEADS, HEAD_DIM), f32), head_sums, (0, me, 0)
    )
    vec = jnp.concatenate(
        [
            jnp.sum(d_first * norm, axis=0).reshape(8, -1),
            jnp.sum(d_first, axis=0).reshape(8, -1),
            jnp.sum(d_second * norm, axis=0).reshape(8, -1),
            jnp.sum(d_second, axis=0).reshape(8, -1),
            head_sums.reshape(8, -1),
            jnp.sum(cotangent, axis=0, dtype=f32).reshape(8, -1),
            at_own(jnp.sum(d_widened, axis=0, dtype=f32), FF // 8),
        ],
        axis=1,
    ).reshape(8, 24, 128)

    out_sum, in_sum, full_one, full_two, full_mix, full_narrow, sums = gather_sums(
        out_part, in_part, grad_one, grad_two, grad_mix, grad_narrow, vec
    )
    own = tokens.astype(f32)
    own_center = own - jnp.mean(own, axis=-1, keepdims=True)
    own_scale = lax.rsqrt(
        jnp.mean(own_center * own_center, axis=-1, keepdims=True) + 1e-05
    )
    own_norm = own_center * own_scale
    output = (own + out_sum + out_bias).astype(bf16)
    pulled = own_scale * (
        in_sum
        - jnp.mean(in_sum, axis=-1, keepdims=True)
        - own_norm * jnp.mean(in_sum * own_norm, axis=-1, keepdims=True)
    )
    input_grad = (cotangent.astype(f32) + pulled).astype(bf16)
    flat = sums.reshape(-1)
    return (
        output,
        input_grad,
        flat[:256],
        flat[256:512],
        full_one.astype(f32),
        flat[1024:1792],
        full_mix.astype(f32),
        flat[1792:2048],
        flat[512:768],
        flat[768:1024],
        full_two.astype(f32),
        flat[2048:3072],
        full_narrow.astype(f32),
        flat[1792:2048],
    )


def solution(mesh):
    head_per_shard = mesh.shape["shard"] == HEADS and mesh.shape["rep"] == 4
    chosen = tensor_parallel if head_per_shard else per_device
    in_specs = (
        P(("rep", "shard"), None),
        P(("rep", "shard")),
        P(("rep", "shard")),
        P("shard"),
        P("shard"),
        P("shard", None),
        P("shard"),
        P("shard", None),
        P("shard"),
        P("shard"),
        P("shard"),
        P("shard", None),
        P("shard"),
        P("shard", None),
        P("shard"),
        P(("rep", "shard"), None),
    )
    out_specs = (
        P(("rep", "shard"), None),
        P(("rep", "shard"), None),
        P("shard"),
        P("shard"),
        P("shard", None),
        P("shard"),
        P("shard", None),
        P("shard"),
        P("shard"),
        P("shard"),
        P("shard", None),
        P("shard"),
        P("shard", None),
        P("shard"),
    )
    return jax.shard_map(
        chosen, mesh=mesh, in_specs=in_specs, out_specs=out_specs, check_vma=False
    )
```

```python
import math

import jax
import jax.numpy as jnp
from jax import lax
from jax.experimental import pallas as pl
from jax.experimental.pallas import tpu as pltpu
from jax.sharding import PartitionSpec as P

D = 2048
HEADS = 8
HEAD_DIM = 256
ROT = 64
FF = 8192


def layer_norm(values, gain, shift):
    center = values - jnp.mean(values, axis=-1, keepdims=True)
    spread = jnp.mean(center * center, axis=-1, keepdims=True)
    return center * lax.rsqrt(spread + 1e-05) * gain + shift


def angles(positions):
    freqs = 10000.0 ** (-(jnp.arange(ROT // 2, dtype=jnp.float32) * 2.0 / ROT))
    turned = positions.astype(jnp.float32)[..., None] * freqs
    return (jnp.cos(turned), jnp.sin(turned))


def rotary(values, cosine, sine):
    half = ROT // 2
    front = values[..., :half]
    back = values[..., half:ROT]
    return jnp.concatenate(
        [front * cosine - back * sine, back * cosine + front * sine, values[..., ROT:]], axis=-1
    )


def exact_gelu(values):
    return jax.nn.gelu(values, approximate=False)


def contract_rows(left, right):
    return lax.dot_general(
        left, right, (((0,), (0,)), ((), ())), preferred_element_type=jnp.float32
    )


def times_rows(left, piece):
    return lax.dot_general(
        left, piece, (((1,), (1,)), ((), ())), preferred_element_type=jnp.float32
    )


def weight_terms(left_one, left_two, left_mix, left_act, d_joint, d_widened, cotangent):

    def wide_term(start, count):
        return jnp.concatenate(
            [
                contract_rows(left_one, d_joint),
                contract_rows(left_two, d_widened),
                contract_rows(left_mix, cotangent),
            ],
            axis=1,
        )

    def down_term(start, count):
        return contract_rows(left_act, cotangent)

    return (wide_term, down_term)


def per_device(
    tokens,
    segment_ids,
    positions,
    first_gain,
    first_shift,
    project_weight,
    project_bias,
    mixing_weight,
    mixing_bias,
    second_gain,
    second_shift,
    widen_weight,
    widen_bias,
    narrow_weight,
    narrow_bias,
    cotangent,
):
    length = tokens.shape[0]
    shards = lax.axis_size("shard")
    gain_one, shift_one, gain_two, shift_two, joint_bias, mix_bias, wide_bias, narrow_full = (
        lax.all_gather(first_gain, "shard", axis=0, tiled=True),
        lax.all_gather(first_shift, "shard", axis=0, tiled=True),
        lax.all_gather(second_gain, "shard", axis=0, tiled=True),
        lax.all_gather(second_shift, "shard", axis=0, tiled=True),
        lax.all_gather(project_bias, "shard", axis=0, tiled=True),
        lax.all_gather(mixing_bias, "shard", axis=0, tiled=True),
        lax.all_gather(widen_bias, "shard", axis=0, tiled=True),
        lax.all_gather(narrow_bias, "shard", axis=0, tiled=True),
    )
    inputs = tokens.astype(jnp.float32)
    first_norm, first_pull = jax.vjp(layer_norm, inputs, gain_one, shift_one)
    second_norm, second_pull = jax.vjp(layer_norm, inputs, gain_two, shift_two)
    first = first_norm.astype(jnp.bfloat16)
    second = second_norm.astype(jnp.bfloat16)
    pieces = (
        lax.all_gather(project_weight, "shard", axis=0, tiled=True),
        lax.all_gather(widen_weight, "shard", axis=0, tiled=True),
    )
    part_one = jnp.dot(first, pieces[0], preferred_element_type=jnp.float32)
    part_two = jnp.dot(second, pieces[1], preferred_element_type=jnp.float32)
    joint = part_one + joint_bias
    widened = part_two + wide_bias
    shaped = joint.reshape(length, 3, HEADS, HEAD_DIM)
    cosine, sine = angles(positions)
    cosine = cosine[:, None, :]
    sine = sine[:, None, :]

    def place(query_in, key_in):
        return (rotary(query_in, cosine, sine) * HEAD_DIM ** (-0.5), rotary(key_in, cosine, sine))

    (query_turned, key_turned), rotate_pull = jax.vjp(place, shaped[:, 0], shaped[:, 1])
    query = query_turned.astype(jnp.bfloat16)
    keys = key_turned.astype(jnp.bfloat16)
    values = shaped[:, 2].astype(jnp.bfloat16)
    order = jnp.arange(length)
    allowed = ((segment_ids[:, None] == segment_ids[None, :]) & (order[:, None] >= order[None, :]))[
        None
    ]

    def masked_scores():
        raw = jnp.einsum("qhe,khe->hqk", query, keys, preferred_element_type=jnp.float32)
        return jnp.where(allowed, raw, -1e30)

    scores = masked_scores()
    highest = jnp.max(scores, axis=-1, keepdims=True)
    raised = jnp.exp(scores - highest)
    summed = jnp.sum(raised, axis=-1, keepdims=True)
    log_summed = highest + jnp.log(summed)
    weights = (raised / summed).astype(jnp.bfloat16)
    context = (
        jnp.einsum("hqk,khe->qhe", weights, values, preferred_element_type=jnp.float32)
        .reshape(length, D)
        .astype(jnp.bfloat16)
    )
    attention = (
        jnp.dot(
            context,
            lax.all_gather(mixing_weight, "shard", axis=0, tiled=True),
            preferred_element_type=jnp.float32,
        )
        + mix_bias
    )
    active_full, gelu_pull = jax.vjp(exact_gelu, widened)
    active = active_full.astype(jnp.bfloat16)
    mlp = (
        jnp.dot(
            active,
            lax.all_gather(narrow_weight, "shard", axis=0, tiled=True),
            preferred_element_type=jnp.float32,
        )
        + narrow_full
    )
    output = (inputs + attention + mlp).astype(jnp.bfloat16)

    def back_rows(piece):
        return times_rows(cotangent, piece)

    d_active = back_rows(lax.all_gather(narrow_weight, "shard", axis=0, tiled=True))
    d_widened = gelu_pull(d_active)[0].astype(jnp.bfloat16)
    d_context = back_rows(lax.all_gather(mixing_weight, "shard", axis=0, tiled=True))
    d_context = d_context.astype(jnp.bfloat16).reshape(length, HEADS, HEAD_DIM)
    again = jnp.exp(masked_scores() - log_summed)
    again_low = again.astype(jnp.bfloat16)
    d_weights = jnp.einsum("qhe,khe->hqk", d_context, values, preferred_element_type=jnp.float32)
    d_values = jnp.einsum("hqk,qhe->khe", again_low, d_context, preferred_element_type=jnp.float32)
    d_scores = (again * (d_weights - jnp.sum(d_weights * again, axis=-1, keepdims=True))).astype(
        jnp.bfloat16
    )
    d_query = jnp.einsum("hqk,khe->qhe", d_scores, keys, preferred_element_type=jnp.float32)
    d_keys = jnp.einsum("hqk,qhe->khe", d_scores, query, preferred_element_type=jnp.float32)
    d_query_in, d_key_in = rotate_pull((d_query, d_keys))
    d_joint = jnp.concatenate(
        [d_query_in.reshape(length, D), d_key_in.reshape(length, D), d_values.reshape(length, D)],
        axis=1,
    ).astype(jnp.bfloat16)
    pieces = lax.all_gather((project_weight, widen_weight), "shard", axis=0, tiled=True)
    stacked = jnp.concatenate(
        [times_rows(d_joint, pieces[0]), times_rows(d_widened, pieces[1])], axis=0
    )
    d_in_one, d_gain_one, d_shift_one = first_pull(stacked[:length])
    d_in_two, d_gain_two, d_shift_two = second_pull(stacked[length:])
    input_grad = (cotangent.astype(jnp.float32) + d_in_one + d_in_two).astype(jnp.bfloat16)
    sums = lax.psum(
        (
            d_gain_one,
            d_shift_one,
            d_gain_two,
            d_shift_two,
            jnp.sum(d_joint, axis=0, dtype=jnp.float32),
            jnp.sum(cotangent, axis=0, dtype=jnp.float32),
            jnp.sum(d_widened, axis=0, dtype=jnp.float32),
        ),
        ("rep", "shard"),
    )
    owner = lax.axis_index("shard")

    def own_part(vector):
        share = vector.shape[0] // shards
        return lax.dynamic_slice_in_dim(vector, owner * share, share)

    owned = [own_part(vector) for vector in sums]
    wide_term, down_term = weight_terms(
        first, second, context, active, d_joint, d_widened, cotangent
    )
    wide_part = lax.psum_scatter(
        wide_term(jnp.int32(0), lax.axis_size("shard") * (D // shards)).astype(jnp.bfloat16),
        "shard",
        scatter_dimension=0,
        tiled=True,
    ).astype(jnp.float32)
    down_part = lax.psum_scatter(
        down_term(jnp.int32(0), lax.axis_size("shard") * (FF // shards)).astype(jnp.bfloat16),
        "shard",
        scatter_dimension=0,
        tiled=True,
    ).astype(jnp.float32)
    wide_part, down_part = (
        lax.psum(wide_part.astype(jnp.bfloat16), "rep").astype(jnp.float32),
        lax.psum(down_part.astype(jnp.bfloat16), "rep").astype(jnp.float32),
    )
    return (
        output,
        input_grad,
        owned[0],
        owned[1],
        wide_part[:, : 3 * D],
        owned[4],
        wide_part[:, 3 * D + FF :],
        owned[5],
        owned[2],
        owned[3],
        wide_part[:, 3 * D : 3 * D + FF],
        owned[6],
        down_part,
        owned[5],
    )


MESH = pl.DeviceIdType.MESH
ANY = pl.BlockSpec(memory_space=pl.ANY)


def places():
    rep, me = lax.axis_index("rep"), lax.axis_index("shard")
    core, side = rep % 2, rep // 2
    col, line = me % 2, me // 2
    return rep, me, core, side, col, line


def greet(peers):
    barrier = pltpu.get_barrier_semaphore()
    for peer in peers:
        pl.semaphore_signal(barrier, inc=1, device_id=peer, device_id_type=MESH)
    pl.semaphore_wait(barrier, len(peers))


def remote(source, target, send, recv, device):
    return pltpu.make_async_remote_copy(
        src_ref=source,
        dst_ref=target,
        send_sem=send,
        recv_sem=recv,
        device_id=device,
        device_id_type=MESH,
    )


F32, BF16 = jnp.float32, jnp.bfloat16
CHUNK = 256


def turned(value, cosine, sine):
    near = value[:, :128]
    lane = lax.broadcasted_iota(jnp.int32, near.shape, 1)
    partner = jnp.where(
        lane < ROT // 2,
        pltpu.roll(near, 128 - ROT // 2, 1),
        pltpu.roll(near, ROT // 2, 1),
    )
    return jnp.concatenate([near * cosine + partner * sine, value[:, 128:]], axis=1)


def dot(left, right, dims=((1,), (0,))):
    return lax.dot_general(left, right, (dims, ((), ())), preferred_element_type=F32)


def forward_kernel(
    tok, cot, wide_one, wide_two, mix, narrow,
    gain_one, shift_one, gain_two, shift_two, mix_bias, narrow_bias, joint_bias, wide_bias,
    segments, positions,
    cot_all, norm_out, cols_one_out, cols_two_out, first_out, second_out,
    query_out, key_out, value_out, probs_out, context_out, active_out, slope_out,
    out_part, cosine_out, sine_out, gains_out, bias_out,
    tok_all, cols_one, cols_two, mix_v, narrow_v, norms, first, second, joint, query, key, value,
    probs, context, active, slope, partial, cosines, sines, small, small_all, table,
    line_send, line_recv, col_send, col_recv,
    own_sem, piece_send, piece_recv, side_send, side_recv, core_send, core_recv,
    small_send, small_recv, load_sem, save_sem,
):
    rep, me, core, side, col, line = places()
    twin = rep + 1 - 2 * core
    across = rep + 2 - 4 * side
    twin_across = across + 1 - 2 * core
    other = me + 1 - 2 * col
    wide = cols_one.shape[1] // 3
    two_wide = cols_two.shape[1]
    rows = wide_one.shape[0]
    share = rows // 4
    length = tok.shape[0]
    width = tok.shape[1]

    offset = 0
    for ref in (gain_one, shift_one, gain_two, shift_two, mix_bias, narrow_bias, joint_bias,
                wide_bias, segments, positions):
        count = ref.shape[0]
        small[0:1, offset : offset + count] = ref[...].astype(F32)[None, :]
        offset += count

    greet(
        [(rep, (me + step) % 8) for step in range(1, 8)]
        + [(twin, me), (across, me)]
    )

    def along(which, array, gathered, direction, step):
        owner = line - direction * (step - 1)
        source = array if step == 1 else gathered.at[owner * 2 + col]
        lane = which * 6 + (0 if direction == 1 else 3) + step - 1
        return remote(
            source,
            gathered.at[owner * 2 + col],
            line_send.at[lane],
            line_recv.at[lane],
            (rep, (line + direction) * 2 + col),
        )

    def sends(direction, step):
        if direction == 1:
            return (line >= step - 1) & (line <= 2)
        return (line <= 4 - step) & (line >= 1)

    def gets(direction, step):
        if direction == 1:
            return line >= step
        return line <= 3 - step

    def sideways(which, array, gathered, direction, step):
        owner = line - direction * step
        source = array if step == 0 else gathered.at[owner * 2 + col]
        lane = which * 7 + (0 if direction == 1 else 3) + step
        return remote(
            source,
            gathered.at[owner * 2 + col],
            col_send.at[lane],
            col_recv.at[lane],
            (rep, other),
        )

    def from_other(which, gathered, direction, step):
        owner = line - direction * step
        lane = which * 7 + (0 if direction == 1 else 3) + step
        here = gathered.at[owner * 2 + 1 - col]
        return remote(here, here, col_send.at[lane], col_recv.at[lane], (rep, other))

    pairs = ((tok, tok_all), (cot, cot_all))
    turns = [(direction, step) for step in (1, 2, 3) for direction in (1, -1)]

    def begin(which):
        array, gathered = pairs[which]
        for direction in (1, -1):
            @pl.when(sends(direction, 1))
            def _(direction=direction):
                along(which, array, gathered, direction, 1).start()
        sideways(which, array, gathered, 1, 0).start()

    def pass_on(which, direction, step):
        array, gathered = pairs[which]

        @pl.when(gets(direction, step))
        def _():
            owner = line - direction * step
            lane = which * 6 + (0 if direction == 1 else 3) + step - 1
            here = gathered.at[owner * 2 + col]
            remote(
                here, here, line_send.at[lane], line_recv.at[lane], (rep, other)
            ).wait_recv()
            sideways(which, array, gathered, direction, step).start()

        if step < 3:
            @pl.when(sends(direction, step + 1))
            def _():
                along(which, array, gathered, direction, step + 1).start()

    def landed(which):
        gathered = pairs[which][1]
        for direction, step in turns:
            @pl.when(gets(direction, step))
            def _(direction=direction, step=step):
                from_other(which, gathered, direction, step).wait_recv()

        from_other(which, gathered, 1, 0).wait_recv()

    def sent(which):
        array, gathered = pairs[which]
        for direction, step in turns:
            @pl.when(sends(direction, step))
            def _(direction=direction, step=step):
                along(which, array, gathered, direction, step).wait_send()

            @pl.when(gets(direction, step))
            def _(direction=direction, step=step):
                sideways(which, array, gathered, direction, step).wait_send()

        sideways(which, array, gathered, 1, 0).wait_send()

    mine = pl.multiple_of(rep * share, share)

    def pieces(step):
        target = (me + step) % 8
        place = pl.ds(pl.multiple_of(me * rows + rep * share, share), share)
        out = []
        for part in range(3):
            out.append(
                remote(
                    wide_one.at[
                        pl.ds(mine, share),
                        pl.ds(pl.multiple_of((part * 8 + target) * wide, wide), wide),
                    ],
                    cols_one.at[place, pl.ds(part * wide, wide)],
                    piece_send.at[step - 1, part],
                    piece_recv.at[step - 1, part],
                    (rep, target),
                )
            )
        out.append(
            remote(
                wide_two.at[
                    pl.ds(mine, share),
                    pl.ds(pl.multiple_of(target * two_wide, two_wide), two_wide),
                ],
                cols_two.at[place, :],
                piece_send.at[step - 1, 3],
                piece_recv.at[step - 1, 3],
                (rep, target),
            )
        )
        return out

    def arrived(step):
        source = (me + 8 - step) % 8
        place = pl.ds(pl.multiple_of(source * rows + rep * share, share), share)
        here = [cols_one.at[place, pl.ds(part * wide, wide)] for part in range(3)]
        here.append(cols_two.at[place, :])
        return [
            remote(
                ref, ref, piece_send.at[step - 1, part], piece_recv.at[step - 1, part],
                (rep, source),
            )
            for part, ref in enumerate(here)
        ]

    def shares(step, quarter, send, recv, lane, device):
        source = (me + 8 - step) % 8
        place = pl.ds(pl.multiple_of(source * rows + quarter * share, share), share)
        return [
            remote(
                array.at[place, :], array.at[place, :],
                send.at[lane, step - 1, index], recv.at[lane, step - 1, index], device,
            )
            for index, array in enumerate((cols_one, cols_two))
        ]

    def little(step):
        return remote(
            small, small_all.at[me], small_send.at[step - 1], small_recv.at[step - 1],
            (rep, (me + step) % 8),
        )

    begin(0)
    for step in range(1, 8):
        little(step).start()
    for step in range(1, 8):
        for copy in pieces(step):
            copy.start()
    here = pl.ds(pl.multiple_of(me * rows, rows), rows)
    own = [
        pltpu.make_async_copy(tok, tok_all.at[me], own_sem.at[0]),
        pltpu.make_async_copy(cot, cot_all.at[me], own_sem.at[1]),
        pltpu.make_async_copy(small, small_all.at[me], own_sem.at[2]),
        pltpu.make_async_copy(
            wide_two.at[:, pl.ds(pl.multiple_of(me * two_wide, two_wide), two_wide)],
            cols_two.at[here, :],
            own_sem.at[3],
        ),
    ] + [
        pltpu.make_async_copy(
            wide_one.at[:, pl.ds(pl.multiple_of((part * 8 + me) * wide, wide), wide)],
            cols_one.at[here, pl.ds(part * wide, wide)],
            own_sem.at[4 + part],
        )
        for part in range(3)
    ]
    for copy in own:
        copy.start()
    loads = [
        pltpu.make_async_copy(mix, mix_v, load_sem.at[0]),
        pltpu.make_async_copy(narrow, narrow_v, load_sem.at[1]),
    ]
    for copy in loads:
        copy.start()
    for direction, step in turns:
        pass_on(0, direction, step)
    begin(1)
    for step in range(1, 8):
        source = (me + 8 - step) % 8
        remote(
            small_all.at[source], small_all.at[source], small_send.at[step - 1],
            small_recv.at[step - 1], (rep, source),
        ).wait_recv()
    own[0].wait()
    own[2].wait()
    for kind in range(6):
        for shard in range(8):
            table[kind : kind + 1, shard * 256 : shard * 256 + 256] = small_all[
                shard, :, kind * 256 : kind * 256 + 256
            ]
    for step in range(1, 8):
        for copy in arrived(step):
            copy.wait_recv()
        for copy in shares(step, rep, side_send, side_recv, 0, (across, me)):
            copy.start()
        for copy in shares(step, rep, core_send, core_recv, 0, (twin, me)):
            copy.start()
    landed(0)

    gains_one, shifts_one = table[0:1, :], table[1:2, :]
    gains_two, shifts_two = table[2:3, :], table[3:4, :]

    @pl.loop(0, 8 * length // 32)
    def _(index):
        block, part = index // (length // 32), index % (length // 32)
        at = pl.ds(pl.multiple_of(part * 32, 32), 32)
        raw = tok_all[block, at, :].astype(F32)
        center = raw - jnp.mean(raw, axis=-1, keepdims=True)
        spread = jnp.mean(center * center, axis=-1, keepdims=True)
        norm = center * lax.rsqrt(spread + 1e-05)
        there = pl.ds(pl.multiple_of(index * 32, 32), 32)
        norms[there, :] = norm.astype(BF16)
        first[there, :] = (norm * gains_one + shifts_one).astype(BF16)
        second[there, :] = (norm * gains_two + shifts_two).astype(BF16)

    saves = [
        pltpu.make_async_copy(norms, norm_out, save_sem.at[0]),
        pltpu.make_async_copy(first, first_out, save_sem.at[1]),
        pltpu.make_async_copy(second, second_out, save_sem.at[2]),
    ]
    for copy in saves:
        copy.start()

    for step in range(1, 8):
        for copy in shares(step, across, side_send, side_recv, 0, (across, me)):
            copy.wait_recv()
        for copy in shares(step, across, core_send, core_recv, 1, (twin, me)):
            copy.start()
    for step in range(1, 8):
        for copy in shares(step, twin, core_send, core_recv, 0, (twin, me)):
            copy.wait_recv()
    for step in range(1, 8):
        for copy in shares(step, twin_across, core_send, core_recv, 1, (twin, me)):
            copy.wait_recv()
    for copy in own[3:]:
        copy.wait()
    for copy in loads:
        copy.wait()
    late = [
        pltpu.make_async_copy(cols_one, cols_one_out, save_sem.at[3]),
        pltpu.make_async_copy(cols_two, cols_two_out, save_sem.at[4]),
    ]
    for copy in late:
        copy.start()
    saves += late

    for part in range(3):
        spot = part * 8 + me
        table[6:7, part * wide : (part + 1) * wide] = small_all[
            spot // 3, :, pl.ds(pl.multiple_of(1536 + (spot % 3) * 256, 256), 256)
        ]
    bias_row = table[6:7, 0 : 3 * wide]
    wide_row = small[0:1, 2304 : 2304 + two_wide]

    def project(start):
        at = pl.ds(start, CHUNK)
        for part in range(3):
            spot = slice(part * wide, (part + 1) * wide)
            joint[at, spot] = dot(first[at, :], cols_one[:, spot]) + bias_row[:, spot]
        for part in range(two_wide // 256):
            spot = slice(part * 256, (part + 1) * 256)
            value_now = dot(second[at, :], cols_two[:, spot]) + wide_row[:, spot]
            cdf = 0.5 * (1.0 + lax.erf(value_now * (0.5**0.5)))
            density = jnp.exp(-0.5 * value_now * value_now) * (0.5 / jnp.pi) ** 0.5
            active[at, spot] = (value_now * cdf).astype(BF16)
            slope[at, spot] = (cdf + value_now * density).astype(BF16)

    lane = lax.broadcasted_iota(jnp.int32, (1, 128), 1)
    frequency = jnp.where(
        lane < ROT,
        jnp.exp((lane % (ROT // 2)).astype(F32) * (-2.0 / ROT * math.log(10000.0))),
        0.0,
    )
    signs = jnp.where(lane < ROT // 2, -1.0, 1.0)
    tall = lax.broadcasted_iota(jnp.int32, (length, length), 0)
    flat = lax.broadcasted_iota(jnp.int32, (length, length), 1)
    ids_at = 2304 + two_wide

    def attend(block, start):
        at = pl.ds(start, length)
        ids = jnp.broadcast_to(small_all[block, :, ids_at : ids_at + 128], (length, length))
        spots = jnp.broadcast_to(
            small_all[block, :, ids_at + 128 : ids_at + 256], (length, length)
        )
        angle = spots.T * frequency
        cosine, sine = jnp.cos(angle), jnp.sin(angle) * signs
        query_now = (turned(joint[at, 0:wide], cosine, sine) * HEAD_DIM**-0.5).astype(BF16)
        key_now = turned(joint[at, wide : 2 * wide], cosine, sine).astype(BF16)
        value_now = joint[at, 2 * wide :].astype(BF16)
        scores = dot(query_now, key_now, ((1,), (1,)))
        allowed = (ids == ids.T) & (flat <= tall)
        scores = jnp.where(allowed, scores, -1e30)
        lifted = jnp.exp(scores - jnp.max(scores, axis=-1, keepdims=True))
        weights = lifted / jnp.sum(lifted, axis=-1, keepdims=True)
        cosines[at, :], sines[at, :] = cosine, sine
        query[at, :], key[at, :], value[at, :] = query_now, key_now, value_now
        probs[at, :] = weights
        context[at, :] = dot(weights.astype(BF16), value_now).astype(BF16)

    def finish(start):
        at = pl.ds(start, CHUNK)
        for part in range(width // 256):
            spot = slice(part * 256, (part + 1) * 256)
            partial[at, spot] = (
                dot(context[at, :], mix_v[:, spot]) + dot(active[at, :], narrow_v[:, spot])
            ).astype(BF16)

    pending = list(turns)
    for index in range(8 * length // CHUNK):
        project(index * CHUNK)
        for direction, step in pending[:1]:
            pass_on(1, direction, step)
        pending = pending[1:]
        for part in range(CHUNK // length):
            block = index * (CHUNK // length) + part
            attend(block, block * length)
        finish(index * CHUNK)
        for direction, step in pending[:1]:
            pass_on(1, direction, step)
        pending = pending[1:]
    for direction, step in pending:
        pass_on(1, direction, step)
    gains_out[...] = table[...]
    bias_out[...] = table[4:5, :] + table[5:6, :]
    late = [
        pltpu.make_async_copy(source, target, save_sem.at[5 + index])
        for index, (source, target) in enumerate(
            (
                (query, query_out), (key, key_out), (value, value_out), (probs, probs_out),
                (context, context_out), (active, active_out), (slope, slope_out),
                (partial, out_part), (cosines, cosine_out), (sines, sine_out),
            )
        )
    ]
    for copy in late:
        copy.start()
    saves += late

    sent(0)
    for step in range(1, 8):
        for copy in pieces(step):
            copy.wait_send()
        for copy in shares(step, rep, side_send, side_recv, 0, (across, me)):
            copy.wait_send()
        for copy in shares(step, rep, core_send, core_recv, 0, (twin, me)):
            copy.wait_send()
        for copy in shares(step, across, core_send, core_recv, 1, (twin, me)):
            copy.wait_send()
        little(step).wait_send()
    own[1].wait()
    for copy in saves:
        copy.wait()
    sent(1)
    landed(1)


def forward(tok, cot, wide_one, wide_two, mix, narrow, vectors):
    dma = pltpu.SemaphoreType.DMA
    length, width = tok.shape
    rows, one = wide_one.shape
    two = wide_two.shape[1]
    one, two = one // 8, two // 8
    total = 8 * length
    struct = jax.ShapeDtypeStruct
    vmem = pl.BlockSpec(memory_space=pltpu.VMEM)
    saved = [
        ((total, HEAD_DIM), BF16), ((total, HEAD_DIM), BF16), ((total, HEAD_DIM), BF16),
        ((total, length), F32), ((total, HEAD_DIM), BF16), ((total, two), BF16),
        ((total, two), BF16), ((total, width), BF16), ((total, length), F32),
        ((total, length), F32),
    ]
    packed = sum(v.shape[0] for v in vectors)
    return pl.pallas_call(
        forward_kernel,
        out_shape=(
            struct((8, length, width), BF16),
            struct((total, width), BF16),
            struct((rows * 8, one), BF16),
            struct((rows * 8, two), BF16),
            struct((total, width), BF16),
            struct((total, width), BF16),
        )
        + tuple(struct(*s) for s in saved)
        + (struct((8, width), F32), struct((1, width), F32)),
        in_specs=[ANY] * 6 + [vmem] * len(vectors),
        out_specs=(ANY,) * 16 + (vmem,) * 2,
        scratch_shapes=[
            pltpu.VMEM((8, length, width), BF16),
            pltpu.VMEM((rows * 8, one), BF16),
            pltpu.VMEM((rows * 8, two), BF16),
            pltpu.VMEM(mix.shape, BF16),
            pltpu.VMEM(narrow.shape, BF16),
            pltpu.VMEM((total, width), BF16),
            pltpu.VMEM((total, width), BF16),
            pltpu.VMEM((total, width), BF16),
            pltpu.VMEM((total, one), F32),
        ]
        + [pltpu.VMEM(*s) for s in saved]
        + [
            pltpu.VMEM((1, packed), F32),
            pltpu.VMEM((8, 1, packed), F32),
            pltpu.VMEM((8, width), F32),
            dma((12,)), dma((12,)), dma((14,)), dma((14,)),
            dma((7,)), dma((7, 4)), dma((7, 4)),
            dma((1, 7, 2)), dma((1, 7, 2)), dma((2, 7, 2)), dma((2, 7, 2)),
            dma((7,)), dma((7,)), dma((2,)), dma((15,)),
        ],
        compiler_params=pltpu.CompilerParams(
            collective_id=0, has_side_effects=True, vmem_limit_bytes=60 << 20
        ),
        name="forward",
    )(tok, cot, wide_one, wide_two, mix, narrow, *vectors)


def backward_kernel(
    cot_all, norm_all, first, second, cols_one, cols_two, mix, narrow,
    query_all, key_all, value_all, probs_all, context_all, active_all, slope_all,
    cosine_all, sine_all, out_part, table,
    out_sum, in_sum, one_full, two_full, mix_full, narrow_full, vec_full,
    grad_one, grad_two, grad_mix, grad_nar,
    core_one, core_two, core_mix, core_nar,
    side_one, side_two, side_mix, side_nar,
    cot, pair, duo, wide, d_widened, mix_v, query, key, value, probs, context, d_context,
    d_joint, cosine, sine, own_act, col_act, line_act, total, sums,
    vec, vec_got, vec_mid, vec_rep,
    load_sem, act_sem, cs, cr, ss, sr, ys, yr, zs, zr, ps, pr, fs, fr, vs, vr, us, ur, ds_sem,
):
    rep, me, core, side, col, line = places()
    twin = rep + 1 - 2 * core
    across = rep + 2 - 4 * side
    diagonal = across + 1 - 2 * core
    other = me + 1 - 2 * col
    length = out_sum.shape[0]
    width = out_sum.shape[1]
    tokens = wide.shape[0]
    half = width // 2
    two_wide = d_widened.shape[1]
    one_wide = d_joint.shape[1]
    part_wide = one_wide // 3
    share = grad_one.shape[2]
    greet(
        [(rep, (me + step) % 8) for step in range(1, 8)]
        + [(twin, me), (across, me), (diagonal, me)]
    )
    grads = (
        (grad_one, core_one, side_one),
        (grad_two, core_two, side_two),
        (grad_mix, core_mix, side_mix),
        (grad_nar, core_nar, side_nar),
    )

    def core_copy(index, slot):
        full, got, _ = grads[index]
        quarter = (across if slot == 0 else rep) + 1 - 2 * core
        return remote(
            full.at[quarter], got.at[slot], cs.at[index, slot], cr.at[index, slot],
            (twin, me),
        )

    def side_copy(index):
        full, _, got = grads[index]
        return remote(full.at[across], got, ss.at[index], sr.at[index], (across, me))

    def block_rows(target, column):
        return pl.ds(pl.multiple_of((target * 2 + column) * length, length), length)

    def col_copy(index, step):
        target = (line + step) % 4
        if index == 0:
            source = out_part.at[block_rows(target, 1 - col), :]
        else:
            source = wide.at[block_rows(target, 1 - col), :]
        return remote(
            source, col_act.at[index, step], ys.at[index, step], yr.at[index, step],
            (rep, other),
        )

    def own_block(index, step):
        if index == 0:
            return own_act.at[step]
        return wide.at[block_rows((line + step) % 4, col), :]

    def own_load(step):
        return pltpu.make_async_copy(
            out_part.at[block_rows((line + step) % 4, col), :], own_act.at[step],
            act_sem.at[step],
        )

    def line_copy(index, step):
        return remote(
            own_block(index, step), line_act.at[index, step - 1],
            zs.at[index, step - 1], zr.at[index, step - 1],
            (rep, ((line + step) % 4) * 2 + col),
        )

    def vec_copy(step):
        target = (me + step) % 8
        return remote(
            vec.at[target], vec_got.at[step - 1], vs.at[step - 1], vr.at[step - 1],
            (rep, target),
        )

    def vec_share(step):
        return remote(
            vec_mid, vec_rep.at[step - 1], us.at[step - 1], ur.at[step - 1],
            ((rep + step) % 4, me),
        )

    def load(source, target, lane):
        copy = pltpu.make_async_copy(source, target, load_sem.at[lane])
        copy.start()
        return copy

    active, slope = duo.at[pl.ds(0, tokens), :], duo.at[pl.ds(tokens, tokens), :]
    got_cot = load(cot_all, cot, 0)
    got_active = load(active_all, active, 1)
    got_context = load(context_all, context, 2)
    for step in (2, 1, 3, 0):
        col_copy(0, step).start()
    got_narrow = [
        load(narrow.at[:, pl.ds(0, half)], pair.at[pl.ds(0, two_wide), :], 3),
        load(narrow.at[:, pl.ds(half, half)], pair.at[pl.ds(two_wide, two_wide), :], 4),
    ]
    got_slope = load(slope_all, slope, 5)
    got_second = load(second, wide, 6)
    got_mix = load(mix, mix_v, 7)
    got_heads = [
        load(query_all, query, 8), load(key_all, key, 9), load(value_all, value, 10),
        load(probs_all, probs, 11), load(cosine_all, cosine, 12), load(sine_all, sine, 13),
    ]
    for step in range(4):
        own_load(step).start()
    vec[...] = jnp.zeros_like(vec)
    sums[...] = jnp.zeros_like(sums)

    def add_two(target, left, right):
        target[...] = (left[...].astype(F32) + right[...].astype(F32)).astype(BF16)

    def chunks(refs, function):
        shape = refs[0].shape
        if len(shape) == 3:
            per = shape[1] // 16

            @pl.loop(0, shape[0] * per)
            def _(index):
                at = pl.ds(pl.multiple_of((index % per) * 16, 16), 16)
                function(*[ref.at[index // per, at, :] for ref in refs])
        else:

            @pl.loop(0, shape[0] // 16)
            def _(index):
                at = pl.ds(pl.multiple_of(index * 16, 16), 16)
                function(*[ref.at[at, :] for ref in refs])

    def send_across(index):
        full, got, _ = grads[index]
        core_copy(index, 0).wait_recv()
        here = full.at[across]
        chunks((here, got.at[0]), lambda left, right: add_two(left, left, right))
        side_copy(index).start()

    got_active.wait()
    got_cot.wait()

    def narrow_quarter(quarter):
        at = pl.ds(pl.multiple_of(quarter * 256, 256), 256)
        for part in range(width // 512):
            spot = pl.ds(part * 512, 512)
            grad_nar[quarter, :, spot] = dot(
                active[:, at], cot[:, spot], ((0,), (0,))
            ).astype(BF16)

    @pl.loop(0, 2)
    def _(slot):
        narrow_quarter(jnp.where(slot == 0, diagonal, twin))

    core_copy(3, 0).start()
    core_copy(3, 1).start()

    @pl.loop(0, 2)
    def _(slot):
        narrow_quarter(jnp.where(slot == 0, across, rep))

    send_across(3)
    got_context.wait()
    for part in range(width // 512):
        spot = pl.ds(part * 512, 512)
        found = dot(context[...], cot[:, spot], ((0,), (0,))).astype(BF16)
        for quarter in range(4):
            grad_mix[quarter, :, spot] = found[quarter * share : (quarter + 1) * share]
    core_copy(2, 0).start()
    core_copy(2, 1).start()

    for copy in got_narrow:
        copy.wait()
    got_slope.wait()

    @pl.loop(0, tokens // 256)
    def _(index):
        at = pl.ds(pl.multiple_of(index * 256, 256), 256)
        for part in range(two_wide // 256):
            spot = pl.ds(part * 256, 256)
            low, high = pl.ds(part * 256, 256), pl.ds(two_wide + part * 256, 256)
            found = dot(cot[at, 0:half], pair[low, :], ((1,), (1,)))
            found = found + dot(cot[at, half:width], pair[high, :], ((1,), (1,)))
            found = (found * slope[at, spot].astype(F32)).astype(BF16)
            d_widened[at, spot] = found
            sums[5:6, spot] = sums[5:6, spot] + jnp.sum(
                found.astype(F32), axis=0, keepdims=True
            )

    got_cols = [load(cols_two, pair, 3)]
    send_across(2)
    got_second.wait()

    @pl.loop(0, 8)
    def _(shard):
        at = pl.ds(pl.multiple_of(shard * 256, 256), 256)
        for part in range(two_wide // 512):
            spot = pl.ds(part * 512, 512)
            found = dot(wide[:, at], d_widened[:, spot], ((0,), (0,))).astype(BF16)
            for quarter in range(4):
                grad_two[quarter, shard, :, spot] = found[
                    quarter * share : (quarter + 1) * share
                ]

    core_copy(1, 0).start()
    core_copy(1, 1).start()
    got_first = load(first, wide, 6)
    got_cols.append(load(cols_one, duo.at[:, pl.ds(0, one_wide)], 1))

    got_mix.wait()
    for copy in got_heads:
        copy.wait()

    @pl.loop(0, tokens // 256)
    def _(index):
        at = pl.ds(pl.multiple_of(index * 256, 256), 256)
        d_context[at, :] = dot(cot[at, :], mix_v[...], ((1,), (1,))).astype(BF16)

    @pl.loop(0, length // 16)
    def _(index):
        at = pl.ds(pl.multiple_of(me * length + index * 16, 16), 16)
        sums[4:5, :] = sums[4:5, :] + jnp.sum(
            cot[at, :].astype(F32), axis=0, keepdims=True
        )

    got_norm = load(norm_all, cot, 0)
    send_across(1)

    @pl.loop(0, 8)
    def _(block):
        at = pl.ds(pl.multiple_of(block * length, length), length)
        weights = probs[at, :]
        pull = d_context[at, :]
        d_weights = dot(pull, value[at, :], ((1,), (1,)))
        d_value = dot(weights.astype(BF16), pull, ((0,), (0,)))
        inner = jnp.sum(d_weights * weights, axis=-1, keepdims=True)
        d_scores = (weights * (d_weights - inner)).astype(BF16)
        d_query = dot(d_scores, key[at, :])
        d_key = dot(d_scores, query[at, :], ((0,), (0,)))
        turn_by, back = cosine[at, :], -sine[at, :]
        pieces = (
            turned(d_query, turn_by, back) * HEAD_DIM**-0.5,
            turned(d_key, turn_by, back),
            d_value,
        )
        for part, piece in enumerate(pieces):
            low = piece.astype(BF16)
            spot = slice(part * part_wide, (part + 1) * part_wide)
            d_joint[at, spot] = low
            sums[6:7, spot] = sums[6:7, spot] + jnp.sum(
                low.astype(F32), axis=0, keepdims=True
            )

    got_first.wait()

    @pl.loop(0, 8)
    def _(shard):
        at = pl.ds(pl.multiple_of(shard * 256, 256), 256)
        for part in range(3):
            spot = pl.ds(part * part_wide, part_wide)
            found = dot(wide[:, at], d_joint[:, spot], ((0,), (0,))).astype(BF16)
            for quarter in range(4):
                grad_one[quarter, shard, :, spot] = found[
                    quarter * share : (quarter + 1) * share
                ]

    core_copy(0, 0).start()
    core_copy(0, 1).start()
    send_across(0)

    def send_along(index, step):
        col_copy(index, step).wait_recv()
        if index == 0:
            own_load(step).wait()
        chunks(
            (own_block(index, step), col_act.at[index, step]),
            lambda left, right: add_two(left, left, right),
        )
        line_copy(index, step).start()

    for step in (2, 1, 3):
        send_along(0, step)

    for copy in got_cols:
        copy.wait()
    got_norm.wait()

    for step in (2, 1, 3, 0):
        start = ((line + step) % 4) * 2 * length

        @pl.loop(0, width // 256)
        def _(index, start=start):
            at = pl.ds(pl.multiple_of(start, 2 * length), 2 * length)
            spot = pl.ds(pl.multiple_of(index * 256, 256), 256)
            d_one = dot(d_joint[at, :], duo[spot, 0:one_wide], ((1,), (1,)))
            d_two = dot(d_widened[at, :], pair[spot, :], ((1,), (1,)))
            now = cot[at, spot].astype(F32)
            rows = (d_one * now, d_one, d_two * now, d_two)
            for place, piece in enumerate(rows):
                sums[place : place + 1, spot] = sums[place : place + 1, spot] + jnp.sum(
                    piece, axis=0, keepdims=True
                )
            wide[at, spot] = (d_one * table[0:1, spot] + d_two * table[2:3, spot]).astype(
                BF16
            )

        col_copy(1, step).start()

    for shard in range(8):
        for place in range(5):
            start = place * 256 if place < 4 else 1792
            vec[shard, :, start : start + 256] = sums[
                place : place + 1, shard * 256 : (shard + 1) * 256
            ]
    vec[me, :, 2048:3072] = sums[5:6, 0:two_wide]
    for part in range(3):
        place = part * 8 + me
        start = pl.multiple_of(1024 + (place % 3) * 256, 256)
        vec[place // 3, :, pl.ds(start, 256)] = sums[
            6:7, part * part_wide : (part + 1) * part_wide
        ]
    for step in range(1, 8):
        vec_copy(step).start()

    my_rows = pl.ds(pl.multiple_of(rep * share, share), share)

    def whole(index):
        full, got, arrived = grads[index]
        core_copy(index, 1).wait_recv()
        side_copy(index).wait_recv()

        def add(left, right, far):
            left[...] = (
                left[...].astype(F32) + right[...].astype(F32) + far[...].astype(F32)
            ).astype(BF16)

        chunks((full.at[rep], got.at[1], arrived), add)

    def pieces(index, step, source_shard, target_shard):
        local = grads[index][0].at[rep, target_shard]
        if index == 1:
            at = pl.ds(pl.multiple_of(source_shard * two_wide, two_wide), two_wide)
            return [
                remote(
                    local, two_full.at[my_rows, at], ps.at[step, 3], pr.at[step, 3],
                    (rep, target_shard),
                )
            ]
        out = []
        for part in range(3):
            start = pl.multiple_of((part * 8 + source_shard) * part_wide, part_wide)
            out.append(
                remote(
                    local.at[:, pl.ds(part * part_wide, part_wide)],
                    one_full.at[my_rows, pl.ds(start, part_wide)],
                    ps.at[step, part], pr.at[step, part], (rep, target_shard),
                )
            )
        return out

    def own_pieces(index):
        local = grads[index][0].at[rep, me]
        if index == 1:
            at = pl.ds(pl.multiple_of(me * two_wide, two_wide), two_wide)
            return [pltpu.make_async_copy(local, two_full.at[my_rows, at], ds_sem.at[3])]
        out = []
        for part in range(3):
            start = pl.multiple_of((part * 8 + me) * part_wide, part_wide)
            out.append(
                pltpu.make_async_copy(
                    local.at[:, pl.ds(part * part_wide, part_wide)],
                    one_full.at[my_rows, pl.ds(start, part_wide)],
                    ds_sem.at[part],
                )
            )
        return out

    for index in (1, 0):
        whole(index)
        for step in range(1, 8):
            for copy in pieces(index, step, me, (me + step) % 8):
                copy.start()
        for copy in own_pieces(index):
            copy.start()

    fulls = (one_full, two_full, mix_full, narrow_full)

    def spot_of(index, quarter):
        count = fulls[index].shape[0] // 4
        return fulls[index].at[pl.ds(pl.multiple_of(quarter * count, count), count), :]

    def hand(index, lane, source, quarter, device):
        return remote(
            source, spot_of(index, quarter), fs.at[index, lane], fr.at[index, lane], device
        )

    own_full = []
    for index in (3, 2):
        whole(index)
        source = grads[index][0].at[rep]
        hand(index, 0, source, rep, (across, me)).start()
        hand(index, 1, source, rep, (twin, me)).start()
        copy = pltpu.make_async_copy(source, spot_of(index, rep), ds_sem.at[2 + index])
        copy.start()
        own_full.append(copy)

    for step in (2, 1, 3):
        send_along(1, step)

    for step in range(1, 8):
        vec_copy(step).wait_recv()
    running = vec[me]
    for step in range(1, 8):
        running = running + vec_got[step - 1]
    vec_mid[...] = running
    for step in range(1, 4):
        vec_share(step).start()

    for index in (1, 0):
        for copy in own_pieces(index):
            copy.wait()
        for step in range(1, 8):
            for copy in pieces(index, step, (me + 8 - step) % 8, me):
                copy.wait_recv()
        hand(index, 0, spot_of(index, rep), rep, (across, me)).start()
        hand(index, 1, spot_of(index, rep), rep, (twin, me)).start()

    for index in (0, 1):
        col_copy(index, 0).wait_recv()
        if index == 0:
            own_load(0).wait()
        for step in range(1, 4):
            line_copy(index, step).wait_recv()
        base = own_block(index, 0)

        @pl.loop(0, length // 16)
        def _(place, index=index, base=base):
            at = pl.ds(pl.multiple_of(place * 16, 16), 16)
            found = base[at, :].astype(F32) + col_act[index, 0, at, :].astype(F32)
            for step in range(3):
                found = found + line_act[index, step, at, :].astype(F32)
            total[at, :] = found

        copy = pltpu.make_async_copy(total, (out_sum, in_sum)[index], ds_sem.at[6])
        copy.start()
        copy.wait()

    for step in range(1, 4):
        vec_share(step).wait_recv()
    vec_full[...] = vec_mid[...] + vec_rep[0] + vec_rep[1] + vec_rep[2]

    for index in (3, 2, 1, 0):
        hand(index, 0, spot_of(index, across), across, (across, me)).wait_recv()
        hand(index, 2, spot_of(index, across), across, (twin, me)).start()
    for index in range(4):
        source = grads[index][0].at[rep] if index > 1 else spot_of(index, rep)
        hand(index, 0, source, rep, (across, me)).wait_send()
        hand(index, 1, source, rep, (twin, me)).wait_send()
        hand(index, 1, spot_of(index, twin), twin, (twin, me)).wait_recv()
        hand(index, 2, spot_of(index, across), across, (twin, me)).wait_send()
        hand(index, 2, spot_of(index, diagonal), diagonal, (twin, me)).wait_recv()
        side_copy(index).wait_send()
        for slot in (0, 1):
            core_copy(index, slot).wait_send()
    for index in (0, 1):
        for step in range(1, 8):
            for copy in pieces(index, step, me, (me + step) % 8):
                copy.wait_send()
        for step in range(4):
            col_copy(index, step).wait_send()
            if step:
                line_copy(index, step).wait_send()
    for step in range(1, 8):
        vec_copy(step).wait_send()
    for step in range(1, 4):
        vec_share(step).wait_send()
    for copy in own_full:
        copy.wait()


def backward(
    cot_all, norm, first, second, cols_one, cols_two, mix, narrow,
    heads, context, active, slope, cosine, sine, out_part, table,
):
    dma = pltpu.SemaphoreType.DMA
    struct = jax.ShapeDtypeStruct
    vmem = pl.BlockSpec(memory_space=pltpu.VMEM)
    tokens, width = cot_all.shape
    length = tokens // 8
    one, two = cols_one.shape[1], cols_two.shape[1]
    share = width // 32
    quarters = [
        (8, share, one), (8, share, two), (mix.shape[0] // 4, width),
        (narrow.shape[0] // 4, width),
    ]
    lanes = 4 * width // 8 + one + width // 8 + two
    return pl.pallas_call(
        backward_kernel,
        out_shape=(
            struct((length, width), F32),
            struct((length, width), F32),
            struct((4 * share, 8 * one), BF16),
            struct((4 * share, 8 * two), BF16),
            struct(mix.shape, BF16),
            struct(narrow.shape, BF16),
            struct((1, lanes), F32),
        ),
        in_specs=[ANY] * 18 + [vmem],
        out_specs=(ANY,) * 6 + (vmem,),
        scratch_shapes=[pltpu.VMEM((4,) + q, BF16) for q in quarters]
        + [pltpu.VMEM((2,) + q, BF16) for q in quarters]
        + [pltpu.VMEM(q, BF16) for q in quarters]
        + [
            pltpu.VMEM((tokens, width), BF16),
            pltpu.VMEM((width, two), BF16),
            pltpu.VMEM((2 * tokens, two), BF16),
            pltpu.VMEM((tokens, width), BF16),
            pltpu.VMEM((tokens, two), BF16),
            pltpu.VMEM(mix.shape, BF16),
        ]
        + [pltpu.VMEM(h.shape, h.dtype) for h in heads]
        + [
            pltpu.VMEM(context.shape, BF16),
            pltpu.VMEM(context.shape, BF16),
            pltpu.VMEM((tokens, one), BF16),
            pltpu.VMEM(cosine.shape, F32),
            pltpu.VMEM(sine.shape, F32),
            pltpu.VMEM((4, length, width), BF16),
            pltpu.VMEM((2, 4, length, width), BF16),
            pltpu.VMEM((2, 3, length, width), BF16),
            pltpu.VMEM((length, width), F32),
            pltpu.VMEM((8, width), F32),
            pltpu.VMEM((8, 1, lanes), F32),
            pltpu.VMEM((7, 1, lanes), F32),
            pltpu.VMEM((1, lanes), F32),
            pltpu.VMEM((3, 1, lanes), F32),
            dma((14,)), dma((4,)),
            dma((4, 2)), dma((4, 2)), dma((4,)), dma((4,)),
            dma((2, 4)), dma((2, 4)), dma((2, 3)), dma((2, 3)),
            dma((8, 4)), dma((8, 4)), dma((4, 3)), dma((4, 3)),
            dma((7,)), dma((7,)), dma((3,)), dma((3,)), dma((7,)),
        ],
        compiler_params=pltpu.CompilerParams(
            collective_id=1, has_side_effects=True, vmem_limit_bytes=60 << 20
        ),
        name="backward",
    )(
        cot_all, norm, first, second, cols_one, cols_two, mix, narrow,
        *heads, context, active, slope, cosine, sine, out_part, table,
    )


def tensor_parallel(
    tokens,
    segment_ids,
    positions,
    first_gain,
    first_shift,
    project_weight,
    project_bias,
    mixing_weight,
    mixing_bias,
    second_gain,
    second_shift,
    widen_weight,
    widen_bias,
    narrow_weight,
    narrow_bias,
    cotangent,
):
    (
        cot_all, norm, cols_one, cols_two, first, second, query, keys, values, probs,
        context, active, slope, out_part, cosine, sine, table, out_bias,
    ) = forward(
        tokens, cotangent, project_weight, widen_weight, mixing_weight, narrow_weight,
        (
            first_gain, first_shift, second_gain, second_shift, mixing_bias, narrow_bias,
            project_bias, widen_bias, segment_ids, positions,
        ),
    )
    out_sum, in_sum, full_one, full_two, full_mix, full_narrow, sums = backward(
        cot_all.reshape(-1, D), norm, first, second, cols_one, cols_two, mixing_weight,
        narrow_weight, (query, keys, values, probs), context, active, slope, cosine, sine,
        out_part, table,
    )
    own = tokens.astype(F32)
    own_center = own - jnp.mean(own, axis=-1, keepdims=True)
    own_scale = lax.rsqrt(
        jnp.mean(own_center * own_center, axis=-1, keepdims=True) + 1e-05
    )
    own_norm = own_center * own_scale
    output = (own + out_sum + out_bias).astype(BF16)
    pulled = own_scale * (
        in_sum
        - jnp.mean(in_sum, axis=-1, keepdims=True)
        - own_norm * jnp.mean(in_sum * own_norm, axis=-1, keepdims=True)
    )
    input_grad = (cotangent.astype(F32) + pulled).astype(BF16)
    flat = sums.reshape(-1)
    return (
        output,
        input_grad,
        flat[:256],
        flat[256:512],
        full_one.astype(F32),
        flat[1024:1792],
        full_mix.astype(F32),
        flat[1792:2048],
        flat[512:768],
        flat[768:1024],
        full_two.astype(F32),
        flat[2048:3072],
        full_narrow.astype(F32),
        flat[1792:2048],
    )


def solution(mesh):
    head_per_shard = mesh.shape["shard"] == HEADS and mesh.shape["rep"] == 4
    chosen = tensor_parallel if head_per_shard else per_device
    in_specs = (
        P(("rep", "shard"), None),
        P(("rep", "shard")),
        P(("rep", "shard")),
        P("shard"),
        P("shard"),
        P("shard", None),
        P("shard"),
        P("shard", None),
        P("shard"),
        P("shard"),
        P("shard"),
        P("shard", None),
        P("shard"),
        P("shard", None),
        P("shard"),
        P(("rep", "shard"), None),
    )
    out_specs = (
        P(("rep", "shard"), None),
        P(("rep", "shard"), None),
        P("shard"),
        P("shard"),
        P("shard", None),
        P("shard"),
        P("shard", None),
        P("shard"),
        P("shard"),
        P("shard"),
        P("shard", None),
        P("shard"),
        P("shard", None),
        P("shard"),
    )
    return jax.shard_map(
        chosen, mesh=mesh, in_specs=in_specs, out_specs=out_specs, check_vma=False
    )
```

```python
import math

import jax
import jax.numpy as jnp
from jax import lax
from jax.experimental import pallas as pl
from jax.experimental.pallas import tpu as pltpu
from jax.sharding import PartitionSpec as P

D = 2048
HEADS = 8
HEAD_DIM = 256
ROT = 64
FF = 8192


def layer_norm(values, gain, shift):
    center = values - jnp.mean(values, axis=-1, keepdims=True)
    spread = jnp.mean(center * center, axis=-1, keepdims=True)
    return center * lax.rsqrt(spread + 1e-05) * gain + shift


def angles(positions):
    freqs = 10000.0 ** (-(jnp.arange(ROT // 2, dtype=jnp.float32) * 2.0 / ROT))
    turned = positions.astype(jnp.float32)[..., None] * freqs
    return (jnp.cos(turned), jnp.sin(turned))


def rotary(values, cosine, sine):
    half = ROT // 2
    front = values[..., :half]
    back = values[..., half:ROT]
    return jnp.concatenate(
        [front * cosine - back * sine, back * cosine + front * sine, values[..., ROT:]], axis=-1
    )


def exact_gelu(values):
    return jax.nn.gelu(values, approximate=False)


def contract_rows(left, right):
    return lax.dot_general(
        left, right, (((0,), (0,)), ((), ())), preferred_element_type=jnp.float32
    )


def times_rows(left, piece):
    return lax.dot_general(
        left, piece, (((1,), (1,)), ((), ())), preferred_element_type=jnp.float32
    )


def weight_terms(left_one, left_two, left_mix, left_act, d_joint, d_widened, cotangent):

    def wide_term(start, count):
        return jnp.concatenate(
            [
                contract_rows(left_one, d_joint),
                contract_rows(left_two, d_widened),
                contract_rows(left_mix, cotangent),
            ],
            axis=1,
        )

    def down_term(start, count):
        return contract_rows(left_act, cotangent)

    return (wide_term, down_term)


def per_device(
    tokens,
    segment_ids,
    positions,
    first_gain,
    first_shift,
    project_weight,
    project_bias,
    mixing_weight,
    mixing_bias,
    second_gain,
    second_shift,
    widen_weight,
    widen_bias,
    narrow_weight,
    narrow_bias,
    cotangent,
):
    length = tokens.shape[0]
    shards = lax.axis_size("shard")
    gain_one, shift_one, gain_two, shift_two, joint_bias, mix_bias, wide_bias, narrow_full = (
        lax.all_gather(first_gain, "shard", axis=0, tiled=True),
        lax.all_gather(first_shift, "shard", axis=0, tiled=True),
        lax.all_gather(second_gain, "shard", axis=0, tiled=True),
        lax.all_gather(second_shift, "shard", axis=0, tiled=True),
        lax.all_gather(project_bias, "shard", axis=0, tiled=True),
        lax.all_gather(mixing_bias, "shard", axis=0, tiled=True),
        lax.all_gather(widen_bias, "shard", axis=0, tiled=True),
        lax.all_gather(narrow_bias, "shard", axis=0, tiled=True),
    )
    inputs = tokens.astype(jnp.float32)
    first_norm, first_pull = jax.vjp(layer_norm, inputs, gain_one, shift_one)
    second_norm, second_pull = jax.vjp(layer_norm, inputs, gain_two, shift_two)
    first = first_norm.astype(jnp.bfloat16)
    second = second_norm.astype(jnp.bfloat16)
    pieces = (
        lax.all_gather(project_weight, "shard", axis=0, tiled=True),
        lax.all_gather(widen_weight, "shard", axis=0, tiled=True),
    )
    part_one = jnp.dot(first, pieces[0], preferred_element_type=jnp.float32)
    part_two = jnp.dot(second, pieces[1], preferred_element_type=jnp.float32)
    joint = part_one + joint_bias
    widened = part_two + wide_bias
    shaped = joint.reshape(length, 3, HEADS, HEAD_DIM)
    cosine, sine = angles(positions)
    cosine = cosine[:, None, :]
    sine = sine[:, None, :]

    def place(query_in, key_in):
        return (rotary(query_in, cosine, sine) * HEAD_DIM ** (-0.5), rotary(key_in, cosine, sine))

    (query_turned, key_turned), rotate_pull = jax.vjp(place, shaped[:, 0], shaped[:, 1])
    query = query_turned.astype(jnp.bfloat16)
    keys = key_turned.astype(jnp.bfloat16)
    values = shaped[:, 2].astype(jnp.bfloat16)
    order = jnp.arange(length)
    allowed = ((segment_ids[:, None] == segment_ids[None, :]) & (order[:, None] >= order[None, :]))[
        None
    ]

    def masked_scores():
        raw = jnp.einsum("qhe,khe->hqk", query, keys, preferred_element_type=jnp.float32)
        return jnp.where(allowed, raw, -1e30)

    scores = masked_scores()
    highest = jnp.max(scores, axis=-1, keepdims=True)
    raised = jnp.exp(scores - highest)
    summed = jnp.sum(raised, axis=-1, keepdims=True)
    log_summed = highest + jnp.log(summed)
    weights = (raised / summed).astype(jnp.bfloat16)
    context = (
        jnp.einsum("hqk,khe->qhe", weights, values, preferred_element_type=jnp.float32)
        .reshape(length, D)
        .astype(jnp.bfloat16)
    )
    attention = (
        jnp.dot(
            context,
            lax.all_gather(mixing_weight, "shard", axis=0, tiled=True),
            preferred_element_type=jnp.float32,
        )
        + mix_bias
    )
    active_full, gelu_pull = jax.vjp(exact_gelu, widened)
    active = active_full.astype(jnp.bfloat16)
    mlp = (
        jnp.dot(
            active,
            lax.all_gather(narrow_weight, "shard", axis=0, tiled=True),
            preferred_element_type=jnp.float32,
        )
        + narrow_full
    )
    output = (inputs + attention + mlp).astype(jnp.bfloat16)

    def back_rows(piece):
        return times_rows(cotangent, piece)

    d_active = back_rows(lax.all_gather(narrow_weight, "shard", axis=0, tiled=True))
    d_widened = gelu_pull(d_active)[0].astype(jnp.bfloat16)
    d_context = back_rows(lax.all_gather(mixing_weight, "shard", axis=0, tiled=True))
    d_context = d_context.astype(jnp.bfloat16).reshape(length, HEADS, HEAD_DIM)
    again = jnp.exp(masked_scores() - log_summed)
    again_low = again.astype(jnp.bfloat16)
    d_weights = jnp.einsum("qhe,khe->hqk", d_context, values, preferred_element_type=jnp.float32)
    d_values = jnp.einsum("hqk,qhe->khe", again_low, d_context, preferred_element_type=jnp.float32)
    d_scores = (again * (d_weights - jnp.sum(d_weights * again, axis=-1, keepdims=True))).astype(
        jnp.bfloat16
    )
    d_query = jnp.einsum("hqk,khe->qhe", d_scores, keys, preferred_element_type=jnp.float32)
    d_keys = jnp.einsum("hqk,qhe->khe", d_scores, query, preferred_element_type=jnp.float32)
    d_query_in, d_key_in = rotate_pull((d_query, d_keys))
    d_joint = jnp.concatenate(
        [d_query_in.reshape(length, D), d_key_in.reshape(length, D), d_values.reshape(length, D)],
        axis=1,
    ).astype(jnp.bfloat16)
    pieces = lax.all_gather((project_weight, widen_weight), "shard", axis=0, tiled=True)
    stacked = jnp.concatenate(
        [times_rows(d_joint, pieces[0]), times_rows(d_widened, pieces[1])], axis=0
    )
    d_in_one, d_gain_one, d_shift_one = first_pull(stacked[:length])
    d_in_two, d_gain_two, d_shift_two = second_pull(stacked[length:])
    input_grad = (cotangent.astype(jnp.float32) + d_in_one + d_in_two).astype(jnp.bfloat16)
    sums = lax.psum(
        (
            d_gain_one,
            d_shift_one,
            d_gain_two,
            d_shift_two,
            jnp.sum(d_joint, axis=0, dtype=jnp.float32),
            jnp.sum(cotangent, axis=0, dtype=jnp.float32),
            jnp.sum(d_widened, axis=0, dtype=jnp.float32),
        ),
        ("rep", "shard"),
    )
    owner = lax.axis_index("shard")

    def own_part(vector):
        share = vector.shape[0] // shards
        return lax.dynamic_slice_in_dim(vector, owner * share, share)

    owned = [own_part(vector) for vector in sums]
    wide_term, down_term = weight_terms(
        first, second, context, active, d_joint, d_widened, cotangent
    )
    wide_part = lax.psum_scatter(
        wide_term(jnp.int32(0), lax.axis_size("shard") * (D // shards)).astype(jnp.bfloat16),
        "shard",
        scatter_dimension=0,
        tiled=True,
    ).astype(jnp.float32)
    down_part = lax.psum_scatter(
        down_term(jnp.int32(0), lax.axis_size("shard") * (FF // shards)).astype(jnp.bfloat16),
        "shard",
        scatter_dimension=0,
        tiled=True,
    ).astype(jnp.float32)
    wide_part, down_part = (
        lax.psum(wide_part.astype(jnp.bfloat16), "rep").astype(jnp.float32),
        lax.psum(down_part.astype(jnp.bfloat16), "rep").astype(jnp.float32),
    )
    return (
        output,
        input_grad,
        owned[0],
        owned[1],
        wide_part[:, : 3 * D],
        owned[4],
        wide_part[:, 3 * D + FF :],
        owned[5],
        owned[2],
        owned[3],
        wide_part[:, 3 * D : 3 * D + FF],
        owned[6],
        down_part,
        owned[5],
    )


MESH = pl.DeviceIdType.MESH
ANY = pl.BlockSpec(memory_space=pl.ANY)


def places():
    rep, me = lax.axis_index("rep"), lax.axis_index("shard")
    core, side = rep % 2, rep // 2
    col, line = me % 2, me // 2
    return rep, me, core, side, col, line


def greet(peers):
    barrier = pltpu.get_barrier_semaphore()
    for peer in peers:
        pl.semaphore_signal(barrier, inc=1, device_id=peer, device_id_type=MESH)
    pl.semaphore_wait(barrier, len(peers))


def remote(source, target, send, recv, device):
    return pltpu.make_async_remote_copy(
        src_ref=source,
        dst_ref=target,
        send_sem=send,
        recv_sem=recv,
        device_id=device,
        device_id_type=MESH,
    )


F32, BF16 = jnp.float32, jnp.bfloat16
CHUNK = 256


def turned(value, cosine, sine):
    near = value[:, :128]
    lane = lax.broadcasted_iota(jnp.int32, near.shape, 1)
    partner = jnp.where(
        lane < ROT // 2,
        pltpu.roll(near, 128 - ROT // 2, 1),
        pltpu.roll(near, ROT // 2, 1),
    )
    return jnp.concatenate([near * cosine + partner * sine, value[:, 128:]], axis=1)


def dot(left, right, dims=((1,), (0,))):
    return lax.dot_general(left, right, (dims, ((), ())), preferred_element_type=F32)


def forward_kernel(
    tok, cot, wide_one, wide_two, mix, narrow,
    gain_one, shift_one, gain_two, shift_two, mix_bias, narrow_bias, joint_bias, wide_bias,
    segments, positions,
    cot_all, norm_out, cols_one_out, cols_two_out, first_out, second_out,
    query_out, key_out, value_out, probs_out, context_out, active_out, slope_out,
    out_part, cosine_out, sine_out, gains_out, bias_out,
    tok_all, cols_one, cols_two, mix_v, narrow_v, norms, first, second, joint, query, key, value,
    probs, context, active, slope, partial, cosines, sines, small, small_all, table,
    line_send, line_recv, col_send, col_recv,
    own_sem, piece_send, piece_recv, side_send, side_recv, core_send, core_recv,
    small_send, small_recv, load_sem, save_sem,
):
    rep, me, core, side, col, line = places()
    twin = rep + 1 - 2 * core
    across = rep + 2 - 4 * side
    twin_across = across + 1 - 2 * core
    other = me + 1 - 2 * col
    wide = cols_one.shape[1] // 3
    two_wide = cols_two.shape[1]
    rows = wide_one.shape[0]
    share = rows // 4
    length = tok.shape[0]
    width = tok.shape[1]

    offset = 0
    for ref in (gain_one, shift_one, gain_two, shift_two, mix_bias, narrow_bias, joint_bias,
                wide_bias, segments, positions):
        count = ref.shape[0]
        small[0:1, offset : offset + count] = ref[...].astype(F32)[None, :]
        offset += count

    greet(
        [(rep, (me + step) % 8) for step in range(1, 8)]
        + [(twin, me), (across, me)]
    )

    def along(which, array, gathered, direction, step):
        owner = line - direction * (step - 1)
        source = array if step == 1 else gathered.at[owner * 2 + col]
        lane = which * 6 + (0 if direction == 1 else 3) + step - 1
        return remote(
            source,
            gathered.at[owner * 2 + col],
            line_send.at[lane],
            line_recv.at[lane],
            (rep, (line + direction) * 2 + col),
        )

    def sends(direction, step):
        if direction == 1:
            return (line >= step - 1) & (line <= 2)
        return (line <= 4 - step) & (line >= 1)

    def gets(direction, step):
        if direction == 1:
            return line >= step
        return line <= 3 - step

    def sideways(which, array, gathered, direction, step):
        owner = line - direction * step
        source = array if step == 0 else gathered.at[owner * 2 + col]
        lane = which * 7 + (0 if direction == 1 else 3) + step
        return remote(
            source,
            gathered.at[owner * 2 + col],
            col_send.at[lane],
            col_recv.at[lane],
            (rep, other),
        )

    def from_other(which, gathered, direction, step):
        owner = line - direction * step
        lane = which * 7 + (0 if direction == 1 else 3) + step
        here = gathered.at[owner * 2 + 1 - col]
        return remote(here, here, col_send.at[lane], col_recv.at[lane], (rep, other))

    pairs = ((tok, tok_all), (cot, cot_all))
    turns = [(direction, step) for step in (1, 2, 3) for direction in (1, -1)]

    def begin(which):
        array, gathered = pairs[which]
        for direction in (1, -1):
            @pl.when(sends(direction, 1))
            def _(direction=direction):
                along(which, array, gathered, direction, 1).start()
        sideways(which, array, gathered, 1, 0).start()

    def pass_on(which, direction, step):
        array, gathered = pairs[which]

        @pl.when(gets(direction, step))
        def _():
            owner = line - direction * step
            lane = which * 6 + (0 if direction == 1 else 3) + step - 1
            here = gathered.at[owner * 2 + col]
            remote(
                here, here, line_send.at[lane], line_recv.at[lane], (rep, other)
            ).wait_recv()
            sideways(which, array, gathered, direction, step).start()

        if step < 3:
            @pl.when(sends(direction, step + 1))
            def _():
                along(which, array, gathered, direction, step + 1).start()

    def landed(which):
        gathered = pairs[which][1]
        for direction, step in turns:
            @pl.when(gets(direction, step))
            def _(direction=direction, step=step):
                from_other(which, gathered, direction, step).wait_recv()

        from_other(which, gathered, 1, 0).wait_recv()

    def sent(which):
        array, gathered = pairs[which]
        for direction, step in turns:
            @pl.when(sends(direction, step))
            def _(direction=direction, step=step):
                along(which, array, gathered, direction, step).wait_send()

            @pl.when(gets(direction, step))
            def _(direction=direction, step=step):
                sideways(which, array, gathered, direction, step).wait_send()

        sideways(which, array, gathered, 1, 0).wait_send()

    mine = pl.multiple_of(rep * share, share)

    def pieces(step):
        target = (me + step) % 8
        place = pl.ds(pl.multiple_of(me * rows + rep * share, share), share)
        out = []
        for part in range(3):
            out.append(
                remote(
                    wide_one.at[
                        pl.ds(mine, share),
                        pl.ds(pl.multiple_of((part * 8 + target) * wide, wide), wide),
                    ],
                    cols_one.at[place, pl.ds(part * wide, wide)],
                    piece_send.at[step - 1, part],
                    piece_recv.at[step - 1, part],
                    (rep, target),
                )
            )
        out.append(
            remote(
                wide_two.at[
                    pl.ds(mine, share),
                    pl.ds(pl.multiple_of(target * two_wide, two_wide), two_wide),
                ],
                cols_two.at[place, :],
                piece_send.at[step - 1, 3],
                piece_recv.at[step - 1, 3],
                (rep, target),
            )
        )
        return out

    def arrived(step):
        source = (me + 8 - step) % 8
        place = pl.ds(pl.multiple_of(source * rows + rep * share, share), share)
        here = [cols_one.at[place, pl.ds(part * wide, wide)] for part in range(3)]
        here.append(cols_two.at[place, :])
        return [
            remote(
                ref, ref, piece_send.at[step - 1, part], piece_recv.at[step - 1, part],
                (rep, source),
            )
            for part, ref in enumerate(here)
        ]

    def shares(step, quarter, send, recv, lane, device):
        source = (me + 8 - step) % 8
        place = pl.ds(pl.multiple_of(source * rows + quarter * share, share), share)
        return [
            remote(
                array.at[place, :], array.at[place, :],
                send.at[lane, step - 1, index], recv.at[lane, step - 1, index], device,
            )
            for index, array in enumerate((cols_one, cols_two))
        ]

    def little(step):
        return remote(
            small, small_all.at[me], small_send.at[step - 1], small_recv.at[step - 1],
            (rep, (me + step) % 8),
        )

    here = pl.ds(pl.multiple_of(me * rows, rows), rows)
    own = [
        pltpu.make_async_copy(tok, tok_all.at[me], own_sem.at[0]),
        pltpu.make_async_copy(cot, cot_all.at[me], own_sem.at[1]),
        pltpu.make_async_copy(small, small_all.at[me], own_sem.at[2]),
        pltpu.make_async_copy(
            wide_two.at[:, pl.ds(pl.multiple_of(me * two_wide, two_wide), two_wide)],
            cols_two.at[here, :],
            own_sem.at[3],
        ),
    ] + [
        pltpu.make_async_copy(
            wide_one.at[:, pl.ds(pl.multiple_of((part * 8 + me) * wide, wide), wide)],
            cols_one.at[here, pl.ds(part * wide, wide)],
            own_sem.at[4 + part],
        )
        for part in range(3)
    ]
    loads = [
        pltpu.make_async_copy(mix, mix_v, load_sem.at[0]),
        pltpu.make_async_copy(narrow, narrow_v, load_sem.at[1]),
    ]

    def send_small():
        for step in range(1, 8):
            little(step).start()

    def send_pieces(*steps):
        for step in steps:
            for copy in pieces(step):
                copy.start()

    def load_own():
        for copy in own + loads:
            copy.start()

    def take_small():
        for step in range(1, 8):
            source = (me + 8 - step) % 8
            remote(
                small_all.at[source], small_all.at[source], small_send.at[step - 1],
                small_recv.at[step - 1], (rep, source),
            ).wait_recv()
        own[2].wait()
        for kind in range(6):
            for shard in range(8):
                table[kind : kind + 1, shard * 256 : shard * 256 + 256] = small_all[
                    shard, :, kind * 256 : kind * 256 + 256
                ]
        for part in range(3):
            spot = part * 8 + me
            table[6:7, part * wide : (part + 1) * wide] = small_all[
                spot // 3, :, pl.ds(pl.multiple_of(1536 + (spot % 3) * 256, 256), 256)
            ]
        gains_out[...] = table[...]
        bias_out[...] = table[4:5, :] + table[5:6, :]

    def relay(*steps):
        for step in steps:
            for copy in arrived(step):
                copy.wait_recv()
            for copy in shares(step, rep, side_send, side_recv, 0, (across, me)):
                copy.start()
            for copy in shares(step, rep, core_send, core_recv, 0, (twin, me)):
                copy.start()

    def relay_across(*steps):
        for step in steps:
            for copy in shares(step, across, side_send, side_recv, 0, (across, me)):
                copy.wait_recv()
            for copy in shares(step, across, core_send, core_recv, 1, (twin, me)):
                copy.start()

    def take_weights():
        for step in range(1, 8):
            for copy in shares(step, twin, core_send, core_recv, 0, (twin, me)):
                copy.wait_recv()
        for step in range(1, 8):
            for copy in shares(step, twin_across, core_send, core_recv, 1, (twin, me)):
                copy.wait_recv()
        for copy in own[3:]:
            copy.wait()
        for copy in loads:
            copy.wait()
        save((cols_one, cols_one_out), (cols_two, cols_two_out))

    saves = []

    def save(*items):
        for source, target in items:
            copy = pltpu.make_async_copy(source, target, save_sem.at[len(saves)])
            copy.start()
            saves.append(copy)

    def norm_all():
        gains_one, shifts_one = table[0:1, :], table[1:2, :]
        gains_two, shifts_two = table[2:3, :], table[3:4, :]

        @pl.loop(0, 8 * length // 32)
        def _(index):
            block, part = index // (length // 32), index % (length // 32)
            at = pl.ds(pl.multiple_of(part * 32, 32), 32)
            raw = tok_all[block, at, :].astype(F32)
            center = raw - jnp.mean(raw, axis=-1, keepdims=True)
            spread = jnp.mean(center * center, axis=-1, keepdims=True)
            norm = center * lax.rsqrt(spread + 1e-05)
            there = pl.ds(pl.multiple_of(index * 32, 32), 32)
            norms[there, :] = norm.astype(BF16)
            first[there, :] = (norm * gains_one + shifts_one).astype(BF16)
            second[there, :] = (norm * gains_two + shifts_two).astype(BF16)

        save((norms, norm_out), (first, first_out), (second, second_out))

    def project(index):
        bias_row = table[6:7, 0 : 3 * wide]
        wide_row = small[0:1, 2304 : 2304 + two_wide]
        at = pl.ds(index * CHUNK, CHUNK)
        for part in range(3):
            spot = slice(part * wide, (part + 1) * wide)
            joint[at, spot] = dot(first[at, :], cols_one[:, spot]) + bias_row[:, spot]
        for part in range(two_wide // 256):
            spot = slice(part * 256, (part + 1) * 256)
            value_now = dot(second[at, :], cols_two[:, spot]) + wide_row[:, spot]
            cdf = 0.5 * (1.0 + lax.erf(value_now * (0.5**0.5)))
            density = jnp.exp(-0.5 * value_now * value_now) * (0.5 / jnp.pi) ** 0.5
            active[at, spot] = (value_now * cdf).astype(BF16)
            slope[at, spot] = (cdf + value_now * density).astype(BF16)

    lane = lax.broadcasted_iota(jnp.int32, (1, 128), 1)
    frequency = jnp.where(
        lane < ROT,
        jnp.exp((lane % (ROT // 2)).astype(F32) * (-2.0 / ROT * math.log(10000.0))),
        0.0,
    )
    signs = jnp.where(lane < ROT // 2, -1.0, 1.0)
    tall = lax.broadcasted_iota(jnp.int32, (length, length), 0)
    flat = lax.broadcasted_iota(jnp.int32, (length, length), 1)
    ids_at = 2304 + two_wide

    def attend(block):
        at = pl.ds(block * length, length)
        ids = jnp.broadcast_to(small_all[block, :, ids_at : ids_at + 128], (length, length))
        spots = jnp.broadcast_to(
            small_all[block, :, ids_at + 128 : ids_at + 256], (length, length)
        )
        angle = spots.T * frequency
        cosine, sine = jnp.cos(angle), jnp.sin(angle) * signs
        query_now = (turned(joint[at, 0:wide], cosine, sine) * HEAD_DIM**-0.5).astype(BF16)
        key_now = turned(joint[at, wide : 2 * wide], cosine, sine).astype(BF16)
        value_now = joint[at, 2 * wide :].astype(BF16)
        scores = dot(query_now, key_now, ((1,), (1,)))
        allowed = (ids == ids.T) & (flat <= tall)
        scores = jnp.where(allowed, scores, -1e30)
        lifted = jnp.exp(scores - jnp.max(scores, axis=-1, keepdims=True))
        weights = lifted / jnp.sum(lifted, axis=-1, keepdims=True)
        cosines[at, :], sines[at, :] = cosine, sine
        query[at, :], key[at, :], value[at, :] = query_now, key_now, value_now
        probs[at, :] = weights
        context[at, :] = dot(weights.astype(BF16), value_now).astype(BF16)

    def finish(index):
        at = pl.ds(index * CHUNK, CHUNK)
        for part in range(width // 256):
            spot = slice(part * 256, (part + 1) * 256)
            partial[at, spot] = (
                dot(context[at, :], mix_v[:, spot]) + dot(active[at, :], narrow_v[:, spot])
            ).astype(BF16)

    def save_all():
        save(
            (query, query_out), (key, key_out), (value, value_out), (probs, probs_out),
            (context, context_out), (active, active_out), (slope, slope_out),
            (partial, out_part), (cosines, cosine_out), (sines, sine_out),
        )

    begin(0)
    send_small()
    load_own()
    pass_on(0, 1, 1)
    pass_on(0, -1, 1)
    send_pieces(1,7,2,6)
    pass_on(0, 1, 2)
    pass_on(0, -1, 2)
    send_pieces(3,5,4)
    pass_on(0, 1, 3)
    pass_on(0, -1, 3)
    relay(1,7)
    begin(1)
    take_small()
    own[0].wait()
    relay(2,6)
    landed(0)
    norm_all()
    relay(3,5,4)
    pass_on(1, 1, 1)
    pass_on(1, -1, 1)
    relay_across(1,7,2,6,3,5,4)
    pass_on(1, 1, 2)
    pass_on(1, -1, 2)
    take_weights()
    project(0)
    pass_on(1, 1, 3)
    pass_on(1, -1, 3)
    attend(0)
    attend(1)
    finish(0)
    project(1)
    attend(2)
    attend(3)
    finish(1)
    project(2)
    attend(4)
    attend(5)
    finish(2)
    project(3)
    attend(6)
    attend(7)
    finish(3)
    save_all()
    sent(0)
    for step in range(1, 8):
        for copy in pieces(step):
            copy.wait_send()
        for copy in shares(step, rep, side_send, side_recv, 0, (across, me)):
            copy.wait_send()
        for copy in shares(step, rep, core_send, core_recv, 0, (twin, me)):
            copy.wait_send()
        for copy in shares(step, across, core_send, core_recv, 1, (twin, me)):
            copy.wait_send()
        little(step).wait_send()
    own[1].wait()
    for copy in saves:
        copy.wait()
    sent(1)
    landed(1)


def forward(tok, cot, wide_one, wide_two, mix, narrow, vectors):
    dma = pltpu.SemaphoreType.DMA
    length, width = tok.shape
    rows, one = wide_one.shape
    two = wide_two.shape[1]
    one, two = one // 8, two // 8
    total = 8 * length
    struct = jax.ShapeDtypeStruct
    vmem = pl.BlockSpec(memory_space=pltpu.VMEM)
    saved = [
        ((total, HEAD_DIM), BF16), ((total, HEAD_DIM), BF16), ((total, HEAD_DIM), BF16),
        ((total, length), F32), ((total, HEAD_DIM), BF16), ((total, two), BF16),
        ((total, two), BF16), ((total, width), BF16), ((total, length), F32),
        ((total, length), F32),
    ]
    packed = sum(v.shape[0] for v in vectors)
    return pl.pallas_call(
        forward_kernel,
        out_shape=(
            struct((8, length, width), BF16),
            struct((total, width), BF16),
            struct((rows * 8, one), BF16),
            struct((rows * 8, two), BF16),
            struct((total, width), BF16),
            struct((total, width), BF16),
        )
        + tuple(struct(*s) for s in saved)
        + (struct((8, width), F32), struct((1, width), F32)),
        in_specs=[ANY] * 6 + [vmem] * len(vectors),
        out_specs=(ANY,) * 16 + (vmem,) * 2,
        scratch_shapes=[
            pltpu.VMEM((8, length, width), BF16),
            pltpu.VMEM((rows * 8, one), BF16),
            pltpu.VMEM((rows * 8, two), BF16),
            pltpu.VMEM(mix.shape, BF16),
            pltpu.VMEM(narrow.shape, BF16),
            pltpu.VMEM((total, width), BF16),
            pltpu.VMEM((total, width), BF16),
            pltpu.VMEM((total, width), BF16),
            pltpu.VMEM((total, one), F32),
        ]
        + [pltpu.VMEM(*s) for s in saved]
        + [
            pltpu.VMEM((1, packed), F32),
            pltpu.VMEM((8, 1, packed), F32),
            pltpu.VMEM((8, width), F32),
            dma((12,)), dma((12,)), dma((14,)), dma((14,)),
            dma((7,)), dma((7, 4)), dma((7, 4)),
            dma((1, 7, 2)), dma((1, 7, 2)), dma((2, 7, 2)), dma((2, 7, 2)),
            dma((7,)), dma((7,)), dma((2,)), dma((15,)),
        ],
        compiler_params=pltpu.CompilerParams(
            collective_id=0, has_side_effects=True, vmem_limit_bytes=60 << 20
        ),
        name="forward",
    )(tok, cot, wide_one, wide_two, mix, narrow, *vectors)


def backward_kernel(
    cot_all, norm_all, first, second, cols_one, cols_two, mix, narrow,
    query_all, key_all, value_all, probs_all, context_all, active_all, slope_all,
    cosine_all, sine_all, out_part, table,
    out_sum, in_sum, one_full, two_full, mix_full, narrow_full, vec_full,
    grad_one, grad_two, grad_mix, grad_nar,
    core_one, core_two, core_mix, core_nar,
    side_one, side_two, side_mix, side_nar,
    cot, pair, duo, wide, d_widened, mix_v, query, key, value, probs, context, d_context,
    d_joint, cosine, sine, own_act, col_act, line_act, total, sums,
    vec, vec_got, vec_mid, vec_rep,
    load_sem, act_sem, cs, cr, ss, sr, ys, yr, zs, zr, ps, pr, fs, fr, vs, vr, us, ur, ds_sem,
):
    rep, me, core, side, col, line = places()
    twin = rep + 1 - 2 * core
    across = rep + 2 - 4 * side
    diagonal = across + 1 - 2 * core
    other = me + 1 - 2 * col
    length = out_sum.shape[0]
    width = out_sum.shape[1]
    tokens = wide.shape[0]
    half = width // 2
    two_wide = d_widened.shape[1]
    one_wide = d_joint.shape[1]
    part_wide = one_wide // 3
    share = grad_one.shape[2]
    greet(
        [(rep, (me + step) % 8) for step in range(1, 8)]
        + [(twin, me), (across, me), (diagonal, me)]
    )
    grads = (
        (grad_one, core_one, side_one),
        (grad_two, core_two, side_two),
        (grad_mix, core_mix, side_mix),
        (grad_nar, core_nar, side_nar),
    )

    def core_copy(index, slot):
        full, got, _ = grads[index]
        quarter = (across if slot == 0 else rep) + 1 - 2 * core
        return remote(
            full.at[quarter], got.at[slot], cs.at[index, slot], cr.at[index, slot],
            (twin, me),
        )

    def side_copy(index):
        full, _, got = grads[index]
        return remote(full.at[across], got, ss.at[index], sr.at[index], (across, me))

    inner = (line == 1) | (line == 2)

    def target_of(step):
        if step == 0:
            return 3 * ((line + 1) % 2)
        if step == 1:
            return (line + 2) % 4
        if step == 2:
            return 1 + line % 2
        return line

    def block_rows(target, column):
        return pl.ds(pl.multiple_of((target * 2 + column) * length, length), length)

    def col_copy(index, step):
        target = target_of(step)
        if index == 0:
            source = out_part.at[block_rows(target, 1 - col), :]
        else:
            source = wide.at[block_rows(target, 1 - col), :]
        return remote(
            source, col_act.at[index, step], ys.at[index, step], yr.at[index, step],
            (rep, other),
        )

    def own_block(index, step):
        if index == 0:
            return own_act.at[step]
        return wide.at[block_rows(target_of(step), col), :]

    def own_load(step):
        return pltpu.make_async_copy(
            out_part.at[block_rows(target_of(step), col), :], own_act.at[step],
            act_sem.at[step],
        )

    def line_copy(index, step):
        slot = jnp.where(inner, (2, 3, 3)[step], step)
        goal = jnp.where(inner, target_of(step), 1 + line // 2)
        return remote(
            own_block(index, step), line_act.at[index, slot], zs.at[index, step],
            zr.at[index, slot], (rep, goal * 2 + col),
        )

    def came(index, slot):
        here = line_act.at[index, slot]
        return here, remote(here, here, zs.at[index, 0], zr.at[index, slot], (rep, other))

    def vec_copy(step):
        target = (me + step) % 8
        return remote(
            vec.at[target], vec_got.at[step - 1], vs.at[step - 1], vr.at[step - 1],
            (rep, target),
        )

    def vec_share(step):
        return remote(
            vec_mid, vec_rep.at[step - 1], us.at[step - 1], ur.at[step - 1],
            ((rep + step) % 4, me),
        )

    def load(source, target, lane):
        copy = pltpu.make_async_copy(source, target, load_sem.at[lane])
        copy.start()
        return copy

    active, slope = duo.at[pl.ds(0, tokens), :], duo.at[pl.ds(tokens, tokens), :]
    got_cot = load(cot_all, cot, 0)
    got_active = load(active_all, active, 1)
    got_context = load(context_all, context, 2)
    for step in range(4):
        col_copy(0, step).start()
    got_narrow = [
        load(narrow.at[:, pl.ds(0, half)], pair.at[pl.ds(0, two_wide), :], 3),
        load(narrow.at[:, pl.ds(half, half)], pair.at[pl.ds(two_wide, two_wide), :], 4),
    ]
    got_slope = load(slope_all, slope, 5)
    got_second = load(second, wide, 6)
    got_mix = load(mix, mix_v, 7)
    got_heads = [
        load(query_all, query, 8), load(key_all, key, 9), load(value_all, value, 10),
        load(probs_all, probs, 11), load(cosine_all, cosine, 12), load(sine_all, sine, 13),
    ]
    for step in range(4):
        own_load(step).start()
    vec[...] = jnp.zeros_like(vec)
    sums[...] = jnp.zeros_like(sums)

    def add_two(target, left, right):
        target[...] = (left[...].astype(F32) + right[...].astype(F32)).astype(BF16)

    def chunks(refs, function):
        shape = refs[0].shape
        if len(shape) == 3:
            per = shape[1] // 16

            @pl.loop(0, shape[0] * per)
            def _(index):
                at = pl.ds(pl.multiple_of((index % per) * 16, 16), 16)
                function(*[ref.at[index // per, at, :] for ref in refs])
        else:

            @pl.loop(0, shape[0] // 16)
            def _(index):
                at = pl.ds(pl.multiple_of(index * 16, 16), 16)
                function(*[ref.at[at, :] for ref in refs])

    def across_sum(index):
        full, got, _ = grads[index]
        core_copy(index, 0).wait_recv()
        here = full.at[across]
        chunks((here, got.at[0]), lambda left, right: add_two(left, left, right))
        side_copy(index).start()

    def trade(index, slot):
        core_copy(index, slot).start()

    def wait(*copies):
        for copy in copies:
            copy.wait()

    def narrow_grad(order):
        quarter = (diagonal, twin, across, rep)[order]
        at = pl.ds(pl.multiple_of(quarter * 256, 256), 256)
        for part in range(width // 512):
            spot = pl.ds(part * 512, 512)
            grad_nar[quarter, :, spot] = dot(
                active[:, at], cot[:, spot], ((0,), (0,))
            ).astype(BF16)

    def mix_grad():
        for part in range(width // 512):
            spot = pl.ds(part * 512, 512)
            found = dot(context[...], cot[:, spot], ((0,), (0,))).astype(BF16)
            for quarter in range(4):
                grad_mix[quarter, :, spot] = found[quarter * share : (quarter + 1) * share]

    def through_gelu(low_index, high_index):
        @pl.loop(low_index, high_index)
        def _(index):
            at = pl.ds(pl.multiple_of(index * 256, 256), 256)
            for part in range(two_wide // 256):
                spot = pl.ds(part * 256, 256)
                low, high = pl.ds(part * 256, 256), pl.ds(two_wide + part * 256, 256)
                found = dot(cot[at, 0:half], pair[low, :], ((1,), (1,)))
                found = found + dot(cot[at, half:width], pair[high, :], ((1,), (1,)))
                found = (found * slope[at, spot].astype(F32)).astype(BF16)
                d_widened[at, spot] = found
                sums[5:6, spot] = sums[5:6, spot] + jnp.sum(
                    found.astype(F32), axis=0, keepdims=True
                )

    def wide_grad(low_index, high_index):
        @pl.loop(low_index, high_index)
        def _(shard):
            at = pl.ds(pl.multiple_of(shard * 256, 256), 256)
            for part in range(two_wide // 512):
                spot = pl.ds(part * 512, 512)
                found = dot(wide[:, at], d_widened[:, spot], ((0,), (0,))).astype(BF16)
                for quarter in range(4):
                    grad_two[quarter, shard, :, spot] = found[
                        quarter * share : (quarter + 1) * share
                    ]

    def through_mix():
        @pl.loop(0, tokens // 256)
        def _(index):
            at = pl.ds(pl.multiple_of(index * 256, 256), 256)
            d_context[at, :] = dot(cot[at, :], mix_v[...], ((1,), (1,))).astype(BF16)

        @pl.loop(0, length // 16)
        def _(index):
            at = pl.ds(pl.multiple_of(me * length + index * 16, 16), 16)
            sums[4:5, :] = sums[4:5, :] + jnp.sum(
                cot[at, :].astype(F32), axis=0, keepdims=True
            )

    def attend_back(low_index, high_index):
        @pl.loop(low_index, high_index)
        def _(block):
            at = pl.ds(pl.multiple_of(block * length, length), length)
            weights = probs[at, :]
            pull = d_context[at, :]
            d_weights = dot(pull, value[at, :], ((1,), (1,)))
            d_value = dot(weights.astype(BF16), pull, ((0,), (0,)))
            inner = jnp.sum(d_weights * weights, axis=-1, keepdims=True)
            d_scores = (weights * (d_weights - inner)).astype(BF16)
            d_query = dot(d_scores, key[at, :])
            d_key = dot(d_scores, query[at, :], ((0,), (0,)))
            turn_by, back = cosine[at, :], -sine[at, :]
            pieces = (
                turned(d_query, turn_by, back) * HEAD_DIM**-0.5,
                turned(d_key, turn_by, back),
                d_value,
            )
            for part, piece in enumerate(pieces):
                low = piece.astype(BF16)
                spot = slice(part * part_wide, (part + 1) * part_wide)
                d_joint[at, spot] = low
                sums[6:7, spot] = sums[6:7, spot] + jnp.sum(
                    low.astype(F32), axis=0, keepdims=True
                )

    def project_grad(low_index, high_index):
        @pl.loop(low_index, high_index)
        def _(shard):
            at = pl.ds(pl.multiple_of(shard * 256, 256), 256)
            for part in range(3):
                spot = pl.ds(part * part_wide, part_wide)
                found = dot(wide[:, at], d_joint[:, spot], ((0,), (0,))).astype(BF16)
                for quarter in range(4):
                    grad_one[quarter, shard, :, spot] = found[
                        quarter * share : (quarter + 1) * share
                    ]

    def send_along(index, step):
        col_copy(index, step).wait_recv()
        if index == 0:
            own_load(step).wait()
        here = own_block(index, step)

        def add(left, right):
            chunks((left, right), lambda one, two: add_two(one, one, two))

        add(here, col_act.at[index, step])

        if step > 0:
            @pl.when(inner)
            def _():
                there, copy = came(index, step - 1)
                copy.wait_recv()
                add(here, there)

        line_copy(index, step).start()

    def input_part(step):
        start = target_of(step) * 2 * length

        @pl.loop(0, width // 256)
        def _(index, start=start):
            at = pl.ds(pl.multiple_of(start, 2 * length), 2 * length)
            spot = pl.ds(pl.multiple_of(index * 256, 256), 256)
            d_one = dot(d_joint[at, :], duo[spot, 0:one_wide], ((1,), (1,)))
            d_two = dot(d_widened[at, :], pair[spot, :], ((1,), (1,)))
            now = cot[at, spot].astype(F32)
            rows = (d_one * now, d_one, d_two * now, d_two)
            for place, piece in enumerate(rows):
                sums[place : place + 1, spot] = sums[place : place + 1, spot] + jnp.sum(
                    piece, axis=0, keepdims=True
                )
            wide[at, spot] = (d_one * table[0:1, spot] + d_two * table[2:3, spot]).astype(
                BF16
            )

        col_copy(1, step).start()

    def send_sums():
        for shard in range(8):
            for place in range(5):
                start = place * 256 if place < 4 else 1792
                vec[shard, :, start : start + 256] = sums[
                    place : place + 1, shard * 256 : (shard + 1) * 256
                ]
        vec[me, :, 2048:3072] = sums[5:6, 0:two_wide]
        for part in range(3):
            place = part * 8 + me
            start = pl.multiple_of(1024 + (place % 3) * 256, 256)
            vec[place // 3, :, pl.ds(start, 256)] = sums[
                6:7, part * part_wide : (part + 1) * part_wide
            ]
        for step in range(1, 8):
            vec_copy(step).start()

    my_rows = pl.ds(pl.multiple_of(rep * share, share), share)

    def whole(index):
        full, got, arrived = grads[index]
        core_copy(index, 1).wait_recv()
        side_copy(index).wait_recv()

        def add(left, right, far):
            left[...] = (
                left[...].astype(F32) + right[...].astype(F32) + far[...].astype(F32)
            ).astype(BF16)

        chunks((full.at[rep], got.at[1], arrived), add)

    def pieces(index, step, source_shard, target_shard):
        local = grads[index][0].at[rep, target_shard]
        if index == 1:
            at = pl.ds(pl.multiple_of(source_shard * two_wide, two_wide), two_wide)
            return [
                remote(
                    local, two_full.at[my_rows, at], ps.at[step, 3], pr.at[step, 3],
                    (rep, target_shard),
                )
            ]
        out = []
        for part in range(3):
            start = pl.multiple_of((part * 8 + source_shard) * part_wide, part_wide)
            out.append(
                remote(
                    local.at[:, pl.ds(part * part_wide, part_wide)],
                    one_full.at[my_rows, pl.ds(start, part_wide)],
                    ps.at[step, part], pr.at[step, part], (rep, target_shard),
                )
            )
        return out

    def own_pieces(index):
        local = grads[index][0].at[rep, me]
        if index == 1:
            at = pl.ds(pl.multiple_of(me * two_wide, two_wide), two_wide)
            return [pltpu.make_async_copy(local, two_full.at[my_rows, at], ds_sem.at[3])]
        out = []
        for part in range(3):
            start = pl.multiple_of((part * 8 + me) * part_wide, part_wide)
            out.append(
                pltpu.make_async_copy(
                    local.at[:, pl.ds(part * part_wide, part_wide)],
                    one_full.at[my_rows, pl.ds(start, part_wide)],
                    ds_sem.at[part],
                )
            )
        return out

    fulls = (one_full, two_full, mix_full, narrow_full)

    def spot_of(index, quarter):
        count = fulls[index].shape[0] // 4
        return fulls[index].at[pl.ds(pl.multiple_of(quarter * count, count), count), :]

    def hand(index, lane, source, quarter, device):
        return remote(
            source, spot_of(index, quarter), fs.at[index, lane], fr.at[index, lane], device
        )

    own_full = []

    def scatter(index, *steps):
        for step in steps:
            for copy in pieces(index, step, me, (me + step) % 8):
                copy.start()
        for copy in own_pieces(index):
            copy.start()

    def hand_out(index):
        source = grads[index][0].at[rep]
        hand(index, 0, source, rep, (across, me)).start()
        hand(index, 1, source, rep, (twin, me)).start()
        copy = pltpu.make_async_copy(source, spot_of(index, rep), ds_sem.at[2 + index])
        copy.start()
        own_full.append(copy)

    def share_sums():
        for step in range(1, 8):
            vec_copy(step).wait_recv()
        running = vec[me]
        for step in range(1, 8):
            running = running + vec_got[step - 1]
        vec_mid[...] = running
        for step in range(1, 4):
            vec_share(step).start()

    def hand_on(index):
        for copy in own_pieces(index):
            copy.wait()
        for step in range(1, 8):
            for copy in pieces(index, step, (me + 8 - step) % 8, me):
                copy.wait_recv()
        hand(index, 0, spot_of(index, rep), rep, (across, me)).start()
        hand(index, 1, spot_of(index, rep), rep, (twin, me)).start()

    def end_sum(index):
        col_copy(index, 3).wait_recv()
        if index == 0:
            own_load(3).wait()
        here = own_block(index, 3)

        def add(left, right):
            left[...] = left[...] + right[...].astype(F32)

        def begin(left, right, both):
            both[...] = left[...].astype(F32) + right[...].astype(F32)

        chunks((here, col_act.at[index, 3], total), begin)

        for slot in (2, 3):
            there, copy = came(index, slot)
            copy.wait_recv()
            chunks((total, there), add)
        copy = pltpu.make_async_copy(total, (out_sum, in_sum)[index], ds_sem.at[6])
        copy.start()
        copy.wait()

    def end_vec():
        for step in range(1, 4):
            vec_share(step).wait_recv()
        vec_full[...] = vec_mid[...] + vec_rep[0] + vec_rep[1] + vec_rep[2]

    def hand_twin(index):
        hand(index, 0, spot_of(index, across), across, (across, me)).wait_recv()
        hand(index, 2, spot_of(index, across), across, (twin, me)).start()

    wait(got_active, got_cot)
    narrow_grad(0)
    trade(3, 0)
    narrow_grad(1)
    trade(3, 1)
    narrow_grad(2)
    across_sum(3)
    narrow_grad(3)
    wait(got_context)
    mix_grad()
    trade(2, 0)
    trade(2, 1)
    wait(*got_narrow, got_slope)
    through_gelu(0, 4)
    got_cols = [load(cols_two, pair, 3)]
    across_sum(2)
    wait(got_second)
    send_along(0, 0)
    wide_grad(0, 8)
    trade(1, 0)
    trade(1, 1)
    got_first = load(first, wide, 6)
    got_cols.append(load(cols_one, duo.at[:, pl.ds(0, one_wide)], 1))
    wait(got_mix, *got_heads)
    through_mix()
    got_norm = load(norm_all, cot, 0)
    across_sum(1)
    send_along(0, 1)
    attend_back(0, 8)
    wait(got_first)
    project_grad(0, 8)
    trade(0, 0)
    trade(0, 1)
    across_sum(0)
    wait(*got_cols, got_norm)
    send_along(0, 2)
    input_part(0)
    input_part(1)
    input_part(2)
    input_part(3)
    send_sums()
    whole(1)
    scatter(1, 1,7,2,6,3,5,4)
    send_along(1, 0)
    whole(0)
    scatter(0, 1,7,2,6,3,5,4)
    whole(3)
    hand_out(3)
    whole(2)
    hand_out(2)
    send_along(1, 1)
    end_sum(0)
    hand_on(1)
    send_along(1, 2)
    share_sums()
    hand_on(0)
    end_sum(1)
    end_vec()
    hand_twin(3)
    hand_twin(2)
    hand_twin(1)
    hand_twin(0)
    for index in range(4):
        source = grads[index][0].at[rep] if index > 1 else spot_of(index, rep)
        hand(index, 0, source, rep, (across, me)).wait_send()
        hand(index, 1, source, rep, (twin, me)).wait_send()
        hand(index, 1, spot_of(index, twin), twin, (twin, me)).wait_recv()
        hand(index, 2, spot_of(index, across), across, (twin, me)).wait_send()
        hand(index, 2, spot_of(index, diagonal), diagonal, (twin, me)).wait_recv()
        side_copy(index).wait_send()
        for slot in (0, 1):
            core_copy(index, slot).wait_send()
    for index in (0, 1):
        for step in range(1, 8):
            for copy in pieces(index, step, me, (me + step) % 8):
                copy.wait_send()
        for step in range(4):
            col_copy(index, step).wait_send()
            if step < 3:
                line_copy(index, step).wait_send()
    for step in range(1, 8):
        vec_copy(step).wait_send()
    for step in range(1, 4):
        vec_share(step).wait_send()
    for copy in own_full:
        copy.wait()


def backward(
    cot_all, norm, first, second, cols_one, cols_two, mix, narrow,
    heads, context, active, slope, cosine, sine, out_part, table,
):
    dma = pltpu.SemaphoreType.DMA
    struct = jax.ShapeDtypeStruct
    vmem = pl.BlockSpec(memory_space=pltpu.VMEM)
    tokens, width = cot_all.shape
    length = tokens // 8
    one, two = cols_one.shape[1], cols_two.shape[1]
    share = width // 32
    quarters = [
        (8, share, one), (8, share, two), (mix.shape[0] // 4, width),
        (narrow.shape[0] // 4, width),
    ]
    lanes = 4 * width // 8 + one + width // 8 + two
    return pl.pallas_call(
        backward_kernel,
        out_shape=(
            struct((length, width), F32),
            struct((length, width), F32),
            struct((4 * share, 8 * one), BF16),
            struct((4 * share, 8 * two), BF16),
            struct(mix.shape, BF16),
            struct(narrow.shape, BF16),
            struct((1, lanes), F32),
        ),
        in_specs=[ANY] * 18 + [vmem],
        out_specs=(ANY,) * 6 + (vmem,),
        scratch_shapes=[pltpu.VMEM((4,) + q, BF16) for q in quarters]
        + [pltpu.VMEM((2,) + q, BF16) for q in quarters]
        + [pltpu.VMEM(q, BF16) for q in quarters]
        + [
            pltpu.VMEM((tokens, width), BF16),
            pltpu.VMEM((width, two), BF16),
            pltpu.VMEM((2 * tokens, two), BF16),
            pltpu.VMEM((tokens, width), BF16),
            pltpu.VMEM((tokens, two), BF16),
            pltpu.VMEM(mix.shape, BF16),
        ]
        + [pltpu.VMEM(h.shape, h.dtype) for h in heads]
        + [
            pltpu.VMEM(context.shape, BF16),
            pltpu.VMEM(context.shape, BF16),
            pltpu.VMEM((tokens, one), BF16),
            pltpu.VMEM(cosine.shape, F32),
            pltpu.VMEM(sine.shape, F32),
            pltpu.VMEM((4, length, width), BF16),
            pltpu.VMEM((2, 4, length, width), BF16),
            pltpu.VMEM((2, 4, length, width), BF16),
            pltpu.VMEM((length, width), F32),
            pltpu.VMEM((8, width), F32),
            pltpu.VMEM((8, 1, lanes), F32),
            pltpu.VMEM((7, 1, lanes), F32),
            pltpu.VMEM((1, lanes), F32),
            pltpu.VMEM((3, 1, lanes), F32),
            dma((14,)), dma((4,)),
            dma((4, 2)), dma((4, 2)), dma((4,)), dma((4,)),
            dma((2, 4)), dma((2, 4)), dma((2, 3)), dma((2, 4)),
            dma((8, 4)), dma((8, 4)), dma((4, 3)), dma((4, 3)),
            dma((7,)), dma((7,)), dma((3,)), dma((3,)), dma((7,)),
        ],
        compiler_params=pltpu.CompilerParams(
            collective_id=1, has_side_effects=True, vmem_limit_bytes=60 << 20
        ),
        name="backward",
    )(
        cot_all, norm, first, second, cols_one, cols_two, mix, narrow,
        *heads, context, active, slope, cosine, sine, out_part, table,
    )


def tensor_parallel(
    tokens,
    segment_ids,
    positions,
    first_gain,
    first_shift,
    project_weight,
    project_bias,
    mixing_weight,
    mixing_bias,
    second_gain,
    second_shift,
    widen_weight,
    widen_bias,
    narrow_weight,
    narrow_bias,
    cotangent,
):
    (
        cot_all, norm, cols_one, cols_two, first, second, query, keys, values, probs,
        context, active, slope, out_part, cosine, sine, table, out_bias,
    ) = forward(
        tokens, cotangent, project_weight, widen_weight, mixing_weight, narrow_weight,
        (
            first_gain, first_shift, second_gain, second_shift, mixing_bias, narrow_bias,
            project_bias, widen_bias, segment_ids, positions,
        ),
    )
    out_sum, in_sum, full_one, full_two, full_mix, full_narrow, sums = backward(
        cot_all.reshape(-1, D), norm, first, second, cols_one, cols_two, mixing_weight,
        narrow_weight, (query, keys, values, probs), context, active, slope, cosine, sine,
        out_part, table,
    )
    own = tokens.astype(F32)
    own_center = own - jnp.mean(own, axis=-1, keepdims=True)
    own_scale = lax.rsqrt(
        jnp.mean(own_center * own_center, axis=-1, keepdims=True) + 1e-05
    )
    own_norm = own_center * own_scale
    output = (own + out_sum + out_bias).astype(BF16)
    pulled = own_scale * (
        in_sum
        - jnp.mean(in_sum, axis=-1, keepdims=True)
        - own_norm * jnp.mean(in_sum * own_norm, axis=-1, keepdims=True)
    )
    input_grad = (cotangent.astype(F32) + pulled).astype(BF16)
    flat = sums.reshape(-1)
    return (
        output,
        input_grad,
        flat[:256],
        flat[256:512],
        full_one.astype(F32),
        flat[1024:1792],
        full_mix.astype(F32),
        flat[1792:2048],
        flat[512:768],
        flat[768:1024],
        full_two.astype(F32),
        flat[2048:3072],
        full_narrow.astype(F32),
        flat[1792:2048],
    )


def solution(mesh):
    head_per_shard = mesh.shape["shard"] == HEADS and mesh.shape["rep"] == 4
    chosen = tensor_parallel if head_per_shard else per_device
    in_specs = (
        P(("rep", "shard"), None),
        P(("rep", "shard")),
        P(("rep", "shard")),
        P("shard"),
        P("shard"),
        P("shard", None),
        P("shard"),
        P("shard", None),
        P("shard"),
        P("shard"),
        P("shard"),
        P("shard", None),
        P("shard"),
        P("shard", None),
        P("shard"),
        P(("rep", "shard"), None),
    )
    out_specs = (
        P(("rep", "shard"), None),
        P(("rep", "shard"), None),
        P("shard"),
        P("shard"),
        P("shard", None),
        P("shard"),
        P("shard", None),
        P("shard"),
        P("shard"),
        P("shard"),
        P("shard", None),
        P("shard"),
        P("shard", None),
        P("shard"),
    )
    return jax.shard_map(
        chosen, mesh=mesh, in_specs=in_specs, out_specs=out_specs, check_vma=False
    )
```

```python
import math

import jax
import jax.numpy as jnp
from jax import lax
from jax.experimental import pallas as pl
from jax.experimental.pallas import tpu as pltpu
from jax.sharding import PartitionSpec as P

D = 2048
HEADS = 8
HEAD_DIM = 256
ROT = 64
FF = 8192


def layer_norm(values, gain, shift):
    center = values - jnp.mean(values, axis=-1, keepdims=True)
    spread = jnp.mean(center * center, axis=-1, keepdims=True)
    return center * lax.rsqrt(spread + 1e-05) * gain + shift


def angles(positions):
    freqs = 10000.0 ** (-(jnp.arange(ROT // 2, dtype=jnp.float32) * 2.0 / ROT))
    turned = positions.astype(jnp.float32)[..., None] * freqs
    return (jnp.cos(turned), jnp.sin(turned))


def rotary(values, cosine, sine):
    half = ROT // 2
    front = values[..., :half]
    back = values[..., half:ROT]
    return jnp.concatenate(
        [front * cosine - back * sine, back * cosine + front * sine, values[..., ROT:]], axis=-1
    )


def exact_gelu(values):
    return jax.nn.gelu(values, approximate=False)


def contract_rows(left, right):
    return lax.dot_general(
        left, right, (((0,), (0,)), ((), ())), preferred_element_type=jnp.float32
    )


def times_rows(left, piece):
    return lax.dot_general(
        left, piece, (((1,), (1,)), ((), ())), preferred_element_type=jnp.float32
    )


def weight_terms(left_one, left_two, left_mix, left_act, d_joint, d_widened, cotangent):

    def wide_term(start, count):
        return jnp.concatenate(
            [
                contract_rows(left_one, d_joint),
                contract_rows(left_two, d_widened),
                contract_rows(left_mix, cotangent),
            ],
            axis=1,
        )

    def down_term(start, count):
        return contract_rows(left_act, cotangent)

    return (wide_term, down_term)


def per_device(
    tokens,
    segment_ids,
    positions,
    first_gain,
    first_shift,
    project_weight,
    project_bias,
    mixing_weight,
    mixing_bias,
    second_gain,
    second_shift,
    widen_weight,
    widen_bias,
    narrow_weight,
    narrow_bias,
    cotangent,
):
    length = tokens.shape[0]
    shards = lax.axis_size("shard")
    gain_one, shift_one, gain_two, shift_two, joint_bias, mix_bias, wide_bias, narrow_full = (
        lax.all_gather(first_gain, "shard", axis=0, tiled=True),
        lax.all_gather(first_shift, "shard", axis=0, tiled=True),
        lax.all_gather(second_gain, "shard", axis=0, tiled=True),
        lax.all_gather(second_shift, "shard", axis=0, tiled=True),
        lax.all_gather(project_bias, "shard", axis=0, tiled=True),
        lax.all_gather(mixing_bias, "shard", axis=0, tiled=True),
        lax.all_gather(widen_bias, "shard", axis=0, tiled=True),
        lax.all_gather(narrow_bias, "shard", axis=0, tiled=True),
    )
    inputs = tokens.astype(jnp.float32)
    first_norm, first_pull = jax.vjp(layer_norm, inputs, gain_one, shift_one)
    second_norm, second_pull = jax.vjp(layer_norm, inputs, gain_two, shift_two)
    first = first_norm.astype(jnp.bfloat16)
    second = second_norm.astype(jnp.bfloat16)
    pieces = (
        lax.all_gather(project_weight, "shard", axis=0, tiled=True),
        lax.all_gather(widen_weight, "shard", axis=0, tiled=True),
    )
    part_one = jnp.dot(first, pieces[0], preferred_element_type=jnp.float32)
    part_two = jnp.dot(second, pieces[1], preferred_element_type=jnp.float32)
    joint = part_one + joint_bias
    widened = part_two + wide_bias
    shaped = joint.reshape(length, 3, HEADS, HEAD_DIM)
    cosine, sine = angles(positions)
    cosine = cosine[:, None, :]
    sine = sine[:, None, :]

    def place(query_in, key_in):
        return (rotary(query_in, cosine, sine) * HEAD_DIM ** (-0.5), rotary(key_in, cosine, sine))

    (query_turned, key_turned), rotate_pull = jax.vjp(place, shaped[:, 0], shaped[:, 1])
    query = query_turned.astype(jnp.bfloat16)
    keys = key_turned.astype(jnp.bfloat16)
    values = shaped[:, 2].astype(jnp.bfloat16)
    order = jnp.arange(length)
    allowed = ((segment_ids[:, None] == segment_ids[None, :]) & (order[:, None] >= order[None, :]))[
        None
    ]

    def masked_scores():
        raw = jnp.einsum("qhe,khe->hqk", query, keys, preferred_element_type=jnp.float32)
        return jnp.where(allowed, raw, -1e30)

    scores = masked_scores()
    highest = jnp.max(scores, axis=-1, keepdims=True)
    raised = jnp.exp(scores - highest)
    summed = jnp.sum(raised, axis=-1, keepdims=True)
    log_summed = highest + jnp.log(summed)
    weights = (raised / summed).astype(jnp.bfloat16)
    context = (
        jnp.einsum("hqk,khe->qhe", weights, values, preferred_element_type=jnp.float32)
        .reshape(length, D)
        .astype(jnp.bfloat16)
    )
    attention = (
        jnp.dot(
            context,
            lax.all_gather(mixing_weight, "shard", axis=0, tiled=True),
            preferred_element_type=jnp.float32,
        )
        + mix_bias
    )
    active_full, gelu_pull = jax.vjp(exact_gelu, widened)
    active = active_full.astype(jnp.bfloat16)
    mlp = (
        jnp.dot(
            active,
            lax.all_gather(narrow_weight, "shard", axis=0, tiled=True),
            preferred_element_type=jnp.float32,
        )
        + narrow_full
    )
    output = (inputs + attention + mlp).astype(jnp.bfloat16)

    def back_rows(piece):
        return times_rows(cotangent, piece)

    d_active = back_rows(lax.all_gather(narrow_weight, "shard", axis=0, tiled=True))
    d_widened = gelu_pull(d_active)[0].astype(jnp.bfloat16)
    d_context = back_rows(lax.all_gather(mixing_weight, "shard", axis=0, tiled=True))
    d_context = d_context.astype(jnp.bfloat16).reshape(length, HEADS, HEAD_DIM)
    again = jnp.exp(masked_scores() - log_summed)
    again_low = again.astype(jnp.bfloat16)
    d_weights = jnp.einsum("qhe,khe->hqk", d_context, values, preferred_element_type=jnp.float32)
    d_values = jnp.einsum("hqk,qhe->khe", again_low, d_context, preferred_element_type=jnp.float32)
    d_scores = (again * (d_weights - jnp.sum(d_weights * again, axis=-1, keepdims=True))).astype(
        jnp.bfloat16
    )
    d_query = jnp.einsum("hqk,khe->qhe", d_scores, keys, preferred_element_type=jnp.float32)
    d_keys = jnp.einsum("hqk,qhe->khe", d_scores, query, preferred_element_type=jnp.float32)
    d_query_in, d_key_in = rotate_pull((d_query, d_keys))
    d_joint = jnp.concatenate(
        [d_query_in.reshape(length, D), d_key_in.reshape(length, D), d_values.reshape(length, D)],
        axis=1,
    ).astype(jnp.bfloat16)
    pieces = lax.all_gather((project_weight, widen_weight), "shard", axis=0, tiled=True)
    stacked = jnp.concatenate(
        [times_rows(d_joint, pieces[0]), times_rows(d_widened, pieces[1])], axis=0
    )
    d_in_one, d_gain_one, d_shift_one = first_pull(stacked[:length])
    d_in_two, d_gain_two, d_shift_two = second_pull(stacked[length:])
    input_grad = (cotangent.astype(jnp.float32) + d_in_one + d_in_two).astype(jnp.bfloat16)
    sums = lax.psum(
        (
            d_gain_one,
            d_shift_one,
            d_gain_two,
            d_shift_two,
            jnp.sum(d_joint, axis=0, dtype=jnp.float32),
            jnp.sum(cotangent, axis=0, dtype=jnp.float32),
            jnp.sum(d_widened, axis=0, dtype=jnp.float32),
        ),
        ("rep", "shard"),
    )
    owner = lax.axis_index("shard")

    def own_part(vector):
        share = vector.shape[0] // shards
        return lax.dynamic_slice_in_dim(vector, owner * share, share)

    owned = [own_part(vector) for vector in sums]
    wide_term, down_term = weight_terms(
        first, second, context, active, d_joint, d_widened, cotangent
    )
    wide_part = lax.psum_scatter(
        wide_term(jnp.int32(0), lax.axis_size("shard") * (D // shards)).astype(jnp.bfloat16),
        "shard",
        scatter_dimension=0,
        tiled=True,
    ).astype(jnp.float32)
    down_part = lax.psum_scatter(
        down_term(jnp.int32(0), lax.axis_size("shard") * (FF // shards)).astype(jnp.bfloat16),
        "shard",
        scatter_dimension=0,
        tiled=True,
    ).astype(jnp.float32)
    wide_part, down_part = (
        lax.psum(wide_part.astype(jnp.bfloat16), "rep").astype(jnp.float32),
        lax.psum(down_part.astype(jnp.bfloat16), "rep").astype(jnp.float32),
    )
    return (
        output,
        input_grad,
        owned[0],
        owned[1],
        wide_part[:, : 3 * D],
        owned[4],
        wide_part[:, 3 * D + FF :],
        owned[5],
        owned[2],
        owned[3],
        wide_part[:, 3 * D : 3 * D + FF],
        owned[6],
        down_part,
        owned[5],
    )


MESH = pl.DeviceIdType.MESH
ANY = pl.BlockSpec(memory_space=pl.ANY)


def places():
    rep, me = lax.axis_index("rep"), lax.axis_index("shard")
    core, side = rep % 2, rep // 2
    col, line = me % 2, me // 2
    return rep, me, core, side, col, line


def greet(peers):
    barrier = pltpu.get_barrier_semaphore()
    for peer in peers:
        pl.semaphore_signal(barrier, inc=1, device_id=peer, device_id_type=MESH)
    pl.semaphore_wait(barrier, len(peers))


def remote(source, target, send, recv, device):
    return pltpu.make_async_remote_copy(
        src_ref=source,
        dst_ref=target,
        send_sem=send,
        recv_sem=recv,
        device_id=device,
        device_id_type=MESH,
    )


F32, BF16 = jnp.float32, jnp.bfloat16
CHUNK = 256


def turned(value, cosine, sine):
    near = value[:, :128]
    lane = lax.broadcasted_iota(jnp.int32, near.shape, 1)
    partner = jnp.where(
        lane < ROT // 2,
        pltpu.roll(near, 128 - ROT // 2, 1),
        pltpu.roll(near, ROT // 2, 1),
    )
    return jnp.concatenate([near * cosine + partner * sine, value[:, 128:]], axis=1)


def dot(left, right, dims=((1,), (0,))):
    return lax.dot_general(left, right, (dims, ((), ())), preferred_element_type=F32)


def forward_kernel(
    tok, cot, wide_one, wide_two, mix, narrow,
    gain_one, shift_one, gain_two, shift_two, mix_bias, narrow_bias, joint_bias, wide_bias,
    segments, positions,
    cot_all, norm_out, cols_one_out, cols_two_out, first_out, second_out,
    query_out, key_out, value_out, probs_out, context_out, active_out, slope_out,
    out_part, cosine_out, sine_out, gains_out, bias_out,
    tok_all, cols_one, cols_two, mix_v, narrow_v, norms, first, second, joint, query, key, value,
    probs, context, active, slope, partial, cosines, sines, small, small_all, table,
    line_send, line_recv, col_send, col_recv,
    own_sem, piece_send, piece_recv, side_send, side_recv, core_send, core_recv,
    small_send, small_recv, load_sem, save_sem,
):
    rep, me, core, side, col, line = places()
    twin = rep + 1 - 2 * core
    across = rep + 2 - 4 * side
    twin_across = across + 1 - 2 * core
    other = me + 1 - 2 * col
    wide = cols_one.shape[1] // 3
    two_wide = cols_two.shape[1]
    rows = wide_one.shape[0]
    share = rows // 4
    length = tok.shape[0]
    width = tok.shape[1]

    offset = 0
    for ref in (gain_one, shift_one, gain_two, shift_two, mix_bias, narrow_bias, joint_bias,
                wide_bias, segments, positions):
        count = ref.shape[0]
        small[0:1, offset : offset + count] = ref[...].astype(F32)[None, :]
        offset += count

    greet(
        [(rep, (me + step) % 8) for step in range(1, 8)]
        + [(twin, me), (across, me)]
    )

    def along(which, direction, step):
        array, gathered, part = pairs[which]
        owner = line - direction * (step - 1)
        there = gathered.at[owner * 2 + col, part, :]
        source = array.at[part, :] if step == 1 else there
        lane = which * 6 + (0 if direction == 1 else 3) + step - 1
        return remote(
            source,
            there,
            line_send.at[lane],
            line_recv.at[lane],
            (rep, (line + direction) * 2 + col),
        )

    def sends(direction, step):
        if direction == 1:
            return (line >= step - 1) & (line <= 2)
        return (line <= 4 - step) & (line >= 1)

    def gets(direction, step):
        if direction == 1:
            return line >= step
        return line <= 3 - step

    def sideways(which, direction, step):
        array, gathered, part = pairs[which]
        owner = line - direction * step
        there = gathered.at[owner * 2 + col, part, :]
        source = array.at[part, :] if step == 0 else there
        lane = which * 7 + (0 if direction == 1 else 3) + step
        return remote(
            source,
            there,
            col_send.at[lane],
            col_recv.at[lane],
            (rep, other),
        )

    def from_other(which, direction, step):
        _, gathered, part = pairs[which]
        owner = line - direction * step
        lane = which * 7 + (0 if direction == 1 else 3) + step
        here = gathered.at[owner * 2 + 1 - col, part, :]
        return remote(here, here, col_send.at[lane], col_recv.at[lane], (rep, other))

    halves = (pl.ds(0, length // 2), pl.ds(length // 2, length // 2))
    pairs = [
        (array, gathered, part)
        for array, gathered in ((tok, tok_all), (cot, cot_all))
        for part in halves
    ]
    turns = [(direction, step) for step in (1, 2, 3) for direction in (1, -1)]

    def begin(which):
        for direction in (1, -1):
            @pl.when(sends(direction, 1))
            def _(direction=direction):
                along(which, direction, 1).start()
        sideways(which, 1, 0).start()

    def pass_on(which, direction, step):
        _, gathered, part = pairs[which]

        @pl.when(gets(direction, step))
        def _():
            owner = line - direction * step
            lane = which * 6 + (0 if direction == 1 else 3) + step - 1
            here = gathered.at[owner * 2 + col, part, :]
            remote(
                here, here, line_send.at[lane], line_recv.at[lane], (rep, other)
            ).wait_recv()
            sideways(which, direction, step).start()

        if step < 3:
            @pl.when(sends(direction, step + 1))
            def _():
                along(which, direction, step + 1).start()

    def landed(which):
        for direction, step in turns:
            @pl.when(gets(direction, step))
            def _(direction=direction, step=step):
                from_other(which, direction, step).wait_recv()

        from_other(which, 1, 0).wait_recv()

    def sent(which):
        for direction, step in turns:
            @pl.when(sends(direction, step))
            def _(direction=direction, step=step):
                along(which, direction, step).wait_send()

            @pl.when(gets(direction, step))
            def _(direction=direction, step=step):
                sideways(which, direction, step).wait_send()

        sideways(which, 1, 0).wait_send()

    mine = pl.multiple_of(rep * share, share)

    def pieces(step):
        target = (me + step) % 8
        place = pl.ds(pl.multiple_of(me * rows + rep * share, share), share)
        out = []
        for part in range(3):
            out.append(
                remote(
                    wide_one.at[
                        pl.ds(mine, share),
                        pl.ds(pl.multiple_of((part * 8 + target) * wide, wide), wide),
                    ],
                    cols_one.at[place, pl.ds(part * wide, wide)],
                    piece_send.at[step - 1, part],
                    piece_recv.at[step - 1, part],
                    (rep, target),
                )
            )
        out.append(
            remote(
                wide_two.at[
                    pl.ds(mine, share),
                    pl.ds(pl.multiple_of(target * two_wide, two_wide), two_wide),
                ],
                cols_two.at[place, :],
                piece_send.at[step - 1, 3],
                piece_recv.at[step - 1, 3],
                (rep, target),
            )
        )
        return out

    def arrived(step):
        source = (me + 8 - step) % 8
        place = pl.ds(pl.multiple_of(source * rows + rep * share, share), share)
        here = [cols_one.at[place, pl.ds(part * wide, wide)] for part in range(3)]
        here.append(cols_two.at[place, :])
        return [
            remote(
                ref, ref, piece_send.at[step - 1, part], piece_recv.at[step - 1, part],
                (rep, source),
            )
            for part, ref in enumerate(here)
        ]

    def shares(step, quarter, send, recv, lane, device):
        source = (me + 8 - step) % 8
        place = pl.ds(pl.multiple_of(source * rows + quarter * share, share), share)
        return [
            remote(
                array.at[place, :], array.at[place, :],
                send.at[lane, step - 1, index], recv.at[lane, step - 1, index], device,
            )
            for index, array in enumerate((cols_one, cols_two))
        ]

    def little(step):
        return remote(
            small, small_all.at[me], small_send.at[step - 1], small_recv.at[step - 1],
            (rep, (me + step) % 8),
        )

    here = pl.ds(pl.multiple_of(me * rows, rows), rows)
    own = [
        pltpu.make_async_copy(tok, tok_all.at[me], own_sem.at[0]),
        pltpu.make_async_copy(cot, cot_all.at[me], own_sem.at[1]),
        pltpu.make_async_copy(small, small_all.at[me], own_sem.at[2]),
        pltpu.make_async_copy(
            wide_two.at[:, pl.ds(pl.multiple_of(me * two_wide, two_wide), two_wide)],
            cols_two.at[here, :],
            own_sem.at[3],
        ),
    ] + [
        pltpu.make_async_copy(
            wide_one.at[:, pl.ds(pl.multiple_of((part * 8 + me) * wide, wide), wide)],
            cols_one.at[here, pl.ds(part * wide, wide)],
            own_sem.at[4 + part],
        )
        for part in range(3)
    ]
    loads = [
        pltpu.make_async_copy(mix, mix_v, load_sem.at[0]),
        pltpu.make_async_copy(narrow, narrow_v, load_sem.at[1]),
    ]

    def send_small():
        for step in range(1, 8):
            little(step).start()

    def send_pieces(*steps):
        for step in steps:
            for copy in pieces(step):
                copy.start()

    def load_own():
        for copy in own + loads:
            copy.start()

    def take_small():
        for step in range(1, 8):
            source = (me + 8 - step) % 8
            remote(
                small_all.at[source], small_all.at[source], small_send.at[step - 1],
                small_recv.at[step - 1], (rep, source),
            ).wait_recv()
        own[2].wait()
        for kind in range(6):
            for shard in range(8):
                table[kind : kind + 1, shard * 256 : shard * 256 + 256] = small_all[
                    shard, :, kind * 256 : kind * 256 + 256
                ]
        for part in range(3):
            spot = part * 8 + me
            table[6:7, part * wide : (part + 1) * wide] = small_all[
                spot // 3, :, pl.ds(pl.multiple_of(1536 + (spot % 3) * 256, 256), 256)
            ]
        gains_out[...] = table[...]
        bias_out[...] = table[4:5, :] + table[5:6, :]

    def relay(*steps):
        for step in steps:
            for copy in arrived(step):
                copy.wait_recv()
            for copy in shares(step, rep, side_send, side_recv, 0, (across, me)):
                copy.start()
            for copy in shares(step, rep, core_send, core_recv, 0, (twin, me)):
                copy.start()

    def relay_across(*steps):
        for step in steps:
            for copy in shares(step, across, side_send, side_recv, 0, (across, me)):
                copy.wait_recv()
            for copy in shares(step, across, core_send, core_recv, 1, (twin, me)):
                copy.start()

    def take_weights():
        for step in range(1, 8):
            for copy in shares(step, twin, core_send, core_recv, 0, (twin, me)):
                copy.wait_recv()
        for step in range(1, 8):
            for copy in shares(step, twin_across, core_send, core_recv, 1, (twin, me)):
                copy.wait_recv()
        for copy in own[3:]:
            copy.wait()
        for copy in loads:
            copy.wait()
        save((cols_one, cols_one_out), (cols_two, cols_two_out))

    saves = []

    def save(*items):
        for source, target in items:
            copy = pltpu.make_async_copy(source, target, save_sem.at[len(saves)])
            copy.start()
            saves.append(copy)

    def norm_all():
        gains_one, shifts_one = table[0:1, :], table[1:2, :]
        gains_two, shifts_two = table[2:3, :], table[3:4, :]

        @pl.loop(0, 8 * length // 32)
        def _(index):
            block, part = index // (length // 32), index % (length // 32)
            at = pl.ds(pl.multiple_of(part * 32, 32), 32)
            raw = tok_all[block, at, :].astype(F32)
            center = raw - jnp.mean(raw, axis=-1, keepdims=True)
            spread = jnp.mean(center * center, axis=-1, keepdims=True)
            norm = center * lax.rsqrt(spread + 1e-05)
            there = pl.ds(pl.multiple_of(index * 32, 32), 32)
            norms[there, :] = norm.astype(BF16)
            first[there, :] = (norm * gains_one + shifts_one).astype(BF16)
            second[there, :] = (norm * gains_two + shifts_two).astype(BF16)

        save((norms, norm_out), (first, first_out), (second, second_out))

    def project(index):
        bias_row = table[6:7, 0 : 3 * wide]
        wide_row = small[0:1, 2304 : 2304 + two_wide]
        at = pl.ds(index * CHUNK, CHUNK)
        for part in range(3):
            spot = slice(part * wide, (part + 1) * wide)
            joint[at, spot] = dot(first[at, :], cols_one[:, spot]) + bias_row[:, spot]
        for part in range(two_wide // 256):
            spot = slice(part * 256, (part + 1) * 256)
            value_now = dot(second[at, :], cols_two[:, spot]) + wide_row[:, spot]
            cdf = 0.5 * (1.0 + lax.erf(value_now * (0.5**0.5)))
            density = jnp.exp(-0.5 * value_now * value_now) * (0.5 / jnp.pi) ** 0.5
            active[at, spot] = (value_now * cdf).astype(BF16)
            slope[at, spot] = (cdf + value_now * density).astype(BF16)

    lane = lax.broadcasted_iota(jnp.int32, (1, 128), 1)
    frequency = jnp.where(
        lane < ROT,
        jnp.exp((lane % (ROT // 2)).astype(F32) * (-2.0 / ROT * math.log(10000.0))),
        0.0,
    )
    signs = jnp.where(lane < ROT // 2, -1.0, 1.0)
    tall = lax.broadcasted_iota(jnp.int32, (length, length), 0)
    flat = lax.broadcasted_iota(jnp.int32, (length, length), 1)
    ids_at = 2304 + two_wide

    def attend(block):
        at = pl.ds(block * length, length)
        ids = jnp.broadcast_to(small_all[block, :, ids_at : ids_at + 128], (length, length))
        spots = jnp.broadcast_to(
            small_all[block, :, ids_at + 128 : ids_at + 256], (length, length)
        )
        angle = spots.T * frequency
        cosine, sine = jnp.cos(angle), jnp.sin(angle) * signs
        query_now = (turned(joint[at, 0:wide], cosine, sine) * HEAD_DIM**-0.5).astype(BF16)
        key_now = turned(joint[at, wide : 2 * wide], cosine, sine).astype(BF16)
        value_now = joint[at, 2 * wide :].astype(BF16)
        scores = dot(query_now, key_now, ((1,), (1,)))
        allowed = (ids == ids.T) & (flat <= tall)
        scores = jnp.where(allowed, scores, -1e30)
        lifted = jnp.exp(scores - jnp.max(scores, axis=-1, keepdims=True))
        weights = lifted / jnp.sum(lifted, axis=-1, keepdims=True)
        cosines[at, :], sines[at, :] = cosine, sine
        query[at, :], key[at, :], value[at, :] = query_now, key_now, value_now
        probs[at, :] = weights
        context[at, :] = dot(weights.astype(BF16), value_now).astype(BF16)

    def finish(index):
        at = pl.ds(index * CHUNK, CHUNK)
        for part in range(width // 256):
            spot = slice(part * 256, (part + 1) * 256)
            partial[at, spot] = (
                dot(context[at, :], mix_v[:, spot]) + dot(active[at, :], narrow_v[:, spot])
            ).astype(BF16)

    def save_all():
        save(
            (query, query_out), (key, key_out), (value, value_out), (probs, probs_out),
            (context, context_out), (active, active_out), (slope, slope_out),
            (partial, out_part), (cosines, cosine_out), (sines, sine_out),
        )

    begin(0)
    begin(1)
    send_small()
    load_own()
    pass_on(0, 1, 1)
    pass_on(0, -1, 1)
    send_pieces(1,7)
    pass_on(1, 1, 1)
    pass_on(1, -1, 1)
    send_pieces(2,6)
    pass_on(0, 1, 2)
    pass_on(0, -1, 2)
    pass_on(1, 1, 2)
    pass_on(1, -1, 2)
    send_pieces(3,5,4)
    pass_on(0, 1, 3)
    pass_on(0, -1, 3)
    pass_on(1, 1, 3)
    pass_on(1, -1, 3)
    relay(1,7)
    begin(2)
    begin(3)
    take_small()
    own[0].wait()
    relay(2,6,3,5,4)
    landed(0)
    landed(1)
    norm_all()
    pass_on(2, 1, 1)
    pass_on(2, -1, 1)
    pass_on(3, 1, 1)
    pass_on(3, -1, 1)
    relay_across(1,7,2,6,3,5,4)
    pass_on(2, 1, 2)
    pass_on(2, -1, 2)
    pass_on(3, 1, 2)
    pass_on(3, -1, 2)
    take_weights()
    project(0)
    pass_on(2, 1, 3)
    pass_on(2, -1, 3)
    pass_on(3, 1, 3)
    pass_on(3, -1, 3)
    attend(0)
    attend(1)
    finish(0)
    project(1)
    attend(2)
    attend(3)
    finish(1)
    project(2)
    attend(4)
    attend(5)
    finish(2)
    project(3)
    attend(6)
    attend(7)
    finish(3)
    save_all()
    sent(0)
    sent(1)
    for step in range(1, 8):
        for copy in pieces(step):
            copy.wait_send()
        for copy in shares(step, rep, side_send, side_recv, 0, (across, me)):
            copy.wait_send()
        for copy in shares(step, rep, core_send, core_recv, 0, (twin, me)):
            copy.wait_send()
        for copy in shares(step, across, core_send, core_recv, 1, (twin, me)):
            copy.wait_send()
        little(step).wait_send()
    own[1].wait()
    for copy in saves:
        copy.wait()
    sent(2)
    sent(3)
    landed(2)
    landed(3)


def forward(tok, cot, wide_one, wide_two, mix, narrow, vectors):
    dma = pltpu.SemaphoreType.DMA
    length, width = tok.shape
    rows, one = wide_one.shape
    two = wide_two.shape[1]
    one, two = one // 8, two // 8
    total = 8 * length
    struct = jax.ShapeDtypeStruct
    vmem = pl.BlockSpec(memory_space=pltpu.VMEM)
    saved = [
        ((total, HEAD_DIM), BF16), ((total, HEAD_DIM), BF16), ((total, HEAD_DIM), BF16),
        ((total, length), F32), ((total, HEAD_DIM), BF16), ((total, two), BF16),
        ((total, two), BF16), ((total, width), BF16), ((total, length), F32),
        ((total, length), F32),
    ]
    packed = sum(v.shape[0] for v in vectors)
    return pl.pallas_call(
        forward_kernel,
        out_shape=(
            struct((8, length, width), BF16),
            struct((total, width), BF16),
            struct((rows * 8, one), BF16),
            struct((rows * 8, two), BF16),
            struct((total, width), BF16),
            struct((total, width), BF16),
        )
        + tuple(struct(*s) for s in saved)
        + (struct((8, width), F32), struct((1, width), F32)),
        in_specs=[ANY] * 6 + [vmem] * len(vectors),
        out_specs=(ANY,) * 16 + (vmem,) * 2,
        scratch_shapes=[
            pltpu.VMEM((8, length, width), BF16),
            pltpu.VMEM((rows * 8, one), BF16),
            pltpu.VMEM((rows * 8, two), BF16),
            pltpu.VMEM(mix.shape, BF16),
            pltpu.VMEM(narrow.shape, BF16),
            pltpu.VMEM((total, width), BF16),
            pltpu.VMEM((total, width), BF16),
            pltpu.VMEM((total, width), BF16),
            pltpu.VMEM((total, one), F32),
        ]
        + [pltpu.VMEM(*s) for s in saved]
        + [
            pltpu.VMEM((1, packed), F32),
            pltpu.VMEM((8, 1, packed), F32),
            pltpu.VMEM((8, width), F32),
            dma((24,)), dma((24,)), dma((28,)), dma((28,)),
            dma((7,)), dma((7, 4)), dma((7, 4)),
            dma((1, 7, 2)), dma((1, 7, 2)), dma((2, 7, 2)), dma((2, 7, 2)),
            dma((7,)), dma((7,)), dma((2,)), dma((15,)),
        ],
        compiler_params=pltpu.CompilerParams(
            collective_id=0, has_side_effects=True, vmem_limit_bytes=60 << 20
        ),
        name="forward",
    )(tok, cot, wide_one, wide_two, mix, narrow, *vectors)


def backward_kernel(
    cot_all, norm_all, first, second, cols_one, cols_two, mix, narrow,
    query_all, key_all, value_all, probs_all, context_all, active_all, slope_all,
    cosine_all, sine_all, out_part, table,
    out_sum, in_sum, one_full, two_full, mix_full, narrow_full, vec_full,
    grad_one, grad_two, grad_mix, grad_nar,
    core_one, core_two, core_mix, core_nar,
    side_one, side_two, side_mix, side_nar,
    cot, pair, duo, wide, d_widened, mix_v, query, key, value, probs, context, d_context,
    d_joint, cosine, sine, own_act, col_act, line_act, total, sums,
    vec, vec_got, vec_mid, vec_rep,
    load_sem, act_sem, cs, cr, ss, sr, ys, yr, zs, zr, ps, pr, fs, fr, vs, vr, us, ur, ds_sem,
):
    rep, me, core, side, col, line = places()
    twin = rep + 1 - 2 * core
    across = rep + 2 - 4 * side
    diagonal = across + 1 - 2 * core
    other = me + 1 - 2 * col
    length = out_sum.shape[0]
    width = out_sum.shape[1]
    tokens = wide.shape[0]
    half = width // 2
    two_wide = d_widened.shape[1]
    one_wide = d_joint.shape[1]
    part_wide = one_wide // 3
    share = grad_one.shape[2]
    greet(
        [(rep, (me + step) % 8) for step in range(1, 8)]
        + [(twin, me), (across, me), (diagonal, me)]
    )
    grads = (
        (grad_one, core_one, side_one),
        (grad_two, core_two, side_two),
        (grad_mix, core_mix, side_mix),
        (grad_nar, core_nar, side_nar),
    )

    def core_copy(index, slot):
        full, got, _ = grads[index]
        quarter = (across if slot == 0 else rep) + 1 - 2 * core
        return remote(
            full.at[quarter], got.at[slot], cs.at[index, slot], cr.at[index, slot],
            (twin, me),
        )

    def side_copy(index):
        full, _, got = grads[index]
        return remote(full.at[across], got, ss.at[index], sr.at[index], (across, me))

    inner = (line == 1) | (line == 2)

    def target_of(step):
        if step == 0:
            return 3 * ((line + 1) % 2)
        if step == 1:
            return (line + 2) % 4
        if step == 2:
            return 1 + line % 2
        return line

    def block_rows(target, column):
        return pl.ds(pl.multiple_of((target * 2 + column) * length, length), length)

    def col_copy(index, step):
        target = target_of(step)
        if index == 0:
            source = out_part.at[block_rows(target, 1 - col), :]
        else:
            source = wide.at[block_rows(target, 1 - col), :]
        return remote(
            source, col_act.at[index, step], ys.at[index, step], yr.at[index, step],
            (rep, other),
        )

    def own_block(index, step):
        if index == 0:
            return own_act.at[step]
        return wide.at[block_rows(target_of(step), col), :]

    def own_load(step):
        return pltpu.make_async_copy(
            out_part.at[block_rows(target_of(step), col), :], own_act.at[step],
            act_sem.at[step],
        )

    def line_copy(index, step):
        slot = jnp.where(inner, (2, 3, 3)[step], step)
        goal = jnp.where(inner, target_of(step), 1 + line // 2)
        return remote(
            own_block(index, step), line_act.at[index, slot], zs.at[index, step],
            zr.at[index, slot], (rep, goal * 2 + col),
        )

    def came(index, slot):
        here = line_act.at[index, slot]
        return here, remote(here, here, zs.at[index, 0], zr.at[index, slot], (rep, other))

    def vec_copy(step):
        target = (me + step) % 8
        return remote(
            vec.at[target], vec_got.at[step - 1], vs.at[step - 1], vr.at[step - 1],
            (rep, target),
        )

    def vec_share(step):
        return remote(
            vec_mid, vec_rep.at[step - 1], us.at[step - 1], ur.at[step - 1],
            ((rep + step) % 4, me),
        )

    def load(source, target, lane):
        copy = pltpu.make_async_copy(source, target, load_sem.at[lane])
        copy.start()
        return copy

    active, slope = duo.at[pl.ds(0, tokens), :], duo.at[pl.ds(tokens, tokens), :]
    got_cot = load(cot_all, cot, 0)
    got_active = load(active_all, active, 1)
    got_context = load(context_all, context, 2)
    for step in range(4):
        col_copy(0, step).start()
    got_narrow = [
        load(narrow.at[:, pl.ds(0, half)], pair.at[pl.ds(0, two_wide), :], 3),
        load(narrow.at[:, pl.ds(half, half)], pair.at[pl.ds(two_wide, two_wide), :], 4),
    ]
    got_slope = load(slope_all, slope, 5)
    got_second = load(second, wide, 6)
    got_mix = load(mix, mix_v, 7)
    got_heads = [
        load(query_all, query, 8), load(key_all, key, 9), load(value_all, value, 10),
        load(probs_all, probs, 11), load(cosine_all, cosine, 12), load(sine_all, sine, 13),
    ]
    for step in range(4):
        own_load(step).start()
    vec[...] = jnp.zeros_like(vec)
    sums[...] = jnp.zeros_like(sums)

    def add_two(target, left, right):
        target[...] = (left[...].astype(F32) + right[...].astype(F32)).astype(BF16)

    def chunks(refs, function):
        shape = refs[0].shape
        if len(shape) == 3:
            per = shape[1] // 16

            @pl.loop(0, shape[0] * per)
            def _(index):
                at = pl.ds(pl.multiple_of((index % per) * 16, 16), 16)
                function(*[ref.at[index // per, at, :] for ref in refs])
        else:

            @pl.loop(0, shape[0] // 16)
            def _(index):
                at = pl.ds(pl.multiple_of(index * 16, 16), 16)
                function(*[ref.at[at, :] for ref in refs])

    def across_sum(index):
        full, got, _ = grads[index]
        core_copy(index, 0).wait_recv()
        here = full.at[across]
        chunks((here, got.at[0]), lambda left, right: add_two(left, left, right))
        side_copy(index).start()

    def trade(index, slot):
        core_copy(index, slot).start()

    def wait(*copies):
        for copy in copies:
            copy.wait()

    def narrow_grad(order):
        quarter = (diagonal, twin, across, rep)[order]
        at = pl.ds(pl.multiple_of(quarter * 256, 256), 256)
        for part in range(width // 512):
            spot = pl.ds(part * 512, 512)
            grad_nar[quarter, :, spot] = dot(
                active[:, at], cot[:, spot], ((0,), (0,))
            ).astype(BF16)

    def mix_grad():
        for part in range(width // 512):
            spot = pl.ds(part * 512, 512)
            found = dot(context[...], cot[:, spot], ((0,), (0,))).astype(BF16)
            for quarter in range(4):
                grad_mix[quarter, :, spot] = found[quarter * share : (quarter + 1) * share]

    def through_gelu(low_index, high_index):
        @pl.loop(low_index, high_index)
        def _(index):
            at = pl.ds(pl.multiple_of(index * 256, 256), 256)
            for part in range(two_wide // 256):
                spot = pl.ds(part * 256, 256)
                low, high = pl.ds(part * 256, 256), pl.ds(two_wide + part * 256, 256)
                found = dot(cot[at, 0:half], pair[low, :], ((1,), (1,)))
                found = found + dot(cot[at, half:width], pair[high, :], ((1,), (1,)))
                found = (found * slope[at, spot].astype(F32)).astype(BF16)
                d_widened[at, spot] = found
                sums[5:6, spot] = sums[5:6, spot] + jnp.sum(
                    found.astype(F32), axis=0, keepdims=True
                )

    def wide_grad(low_index, high_index):
        @pl.loop(low_index, high_index)
        def _(shard):
            at = pl.ds(pl.multiple_of(shard * 256, 256), 256)
            for part in range(two_wide // 512):
                spot = pl.ds(part * 512, 512)
                found = dot(wide[:, at], d_widened[:, spot], ((0,), (0,))).astype(BF16)
                for quarter in range(4):
                    grad_two[quarter, shard, :, spot] = found[
                        quarter * share : (quarter + 1) * share
                    ]

    def through_mix():
        @pl.loop(0, tokens // 256)
        def _(index):
            at = pl.ds(pl.multiple_of(index * 256, 256), 256)
            d_context[at, :] = dot(cot[at, :], mix_v[...], ((1,), (1,))).astype(BF16)

        @pl.loop(0, length // 16)
        def _(index):
            at = pl.ds(pl.multiple_of(me * length + index * 16, 16), 16)
            sums[4:5, :] = sums[4:5, :] + jnp.sum(
                cot[at, :].astype(F32), axis=0, keepdims=True
            )

    def attend_back(low_index, high_index):
        @pl.loop(low_index, high_index)
        def _(block):
            at = pl.ds(pl.multiple_of(block * length, length), length)
            weights = probs[at, :]
            pull = d_context[at, :]
            d_weights = dot(pull, value[at, :], ((1,), (1,)))
            d_value = dot(weights.astype(BF16), pull, ((0,), (0,)))
            inner = jnp.sum(d_weights * weights, axis=-1, keepdims=True)
            d_scores = (weights * (d_weights - inner)).astype(BF16)
            d_query = dot(d_scores, key[at, :])
            d_key = dot(d_scores, query[at, :], ((0,), (0,)))
            turn_by, back = cosine[at, :], -sine[at, :]
            pieces = (
                turned(d_query, turn_by, back) * HEAD_DIM**-0.5,
                turned(d_key, turn_by, back),
                d_value,
            )
            for part, piece in enumerate(pieces):
                low = piece.astype(BF16)
                spot = slice(part * part_wide, (part + 1) * part_wide)
                d_joint[at, spot] = low
                sums[6:7, spot] = sums[6:7, spot] + jnp.sum(
                    low.astype(F32), axis=0, keepdims=True
                )

    def project_grad(low_index, high_index):
        @pl.loop(low_index, high_index)
        def _(shard):
            at = pl.ds(pl.multiple_of(shard * 256, 256), 256)
            for part in range(3):
                spot = pl.ds(part * part_wide, part_wide)
                found = dot(wide[:, at], d_joint[:, spot], ((0,), (0,))).astype(BF16)
                for quarter in range(4):
                    grad_one[quarter, shard, :, spot] = found[
                        quarter * share : (quarter + 1) * share
                    ]

    def send_along(index, step):
        col_copy(index, step).wait_recv()
        if index == 0:
            own_load(step).wait()
        here = own_block(index, step)

        def add(left, right):
            chunks((left, right), lambda one, two: add_two(one, one, two))

        add(here, col_act.at[index, step])

        if step > 0:
            @pl.when(inner)
            def _():
                there, copy = came(index, step - 1)
                copy.wait_recv()
                add(here, there)

        line_copy(index, step).start()

    def input_part(step):
        start = target_of(step) * 2 * length

        @pl.loop(0, width // 256)
        def _(index, start=start):
            at = pl.ds(pl.multiple_of(start, 2 * length), 2 * length)
            spot = pl.ds(pl.multiple_of(index * 256, 256), 256)
            d_one = dot(d_joint[at, :], duo[spot, 0:one_wide], ((1,), (1,)))
            d_two = dot(d_widened[at, :], pair[spot, :], ((1,), (1,)))
            now = cot[at, spot].astype(F32)
            rows = (d_one * now, d_one, d_two * now, d_two)
            for place, piece in enumerate(rows):
                sums[place : place + 1, spot] = sums[place : place + 1, spot] + jnp.sum(
                    piece, axis=0, keepdims=True
                )
            wide[at, spot] = (d_one * table[0:1, spot] + d_two * table[2:3, spot]).astype(
                BF16
            )

        col_copy(1, step).start()

    def send_sums():
        for shard in range(8):
            for place in range(5):
                start = place * 256 if place < 4 else 1792
                vec[shard, :, start : start + 256] = sums[
                    place : place + 1, shard * 256 : (shard + 1) * 256
                ]
        vec[me, :, 2048:3072] = sums[5:6, 0:two_wide]
        for part in range(3):
            place = part * 8 + me
            start = pl.multiple_of(1024 + (place % 3) * 256, 256)
            vec[place // 3, :, pl.ds(start, 256)] = sums[
                6:7, part * part_wide : (part + 1) * part_wide
            ]
        for step in range(1, 8):
            vec_copy(step).start()

    my_rows = pl.ds(pl.multiple_of(rep * share, share), share)

    def whole(index):
        full, got, arrived = grads[index]
        core_copy(index, 1).wait_recv()
        side_copy(index).wait_recv()

        def add(left, right, far):
            left[...] = (
                left[...].astype(F32) + right[...].astype(F32) + far[...].astype(F32)
            ).astype(BF16)

        chunks((full.at[rep], got.at[1], arrived), add)

    def pieces(index, step, source_shard, target_shard):
        local = grads[index][0].at[rep, target_shard]
        if index == 1:
            at = pl.ds(pl.multiple_of(source_shard * two_wide, two_wide), two_wide)
            return [
                remote(
                    local, two_full.at[my_rows, at], ps.at[step, 3], pr.at[step, 3],
                    (rep, target_shard),
                )
            ]
        out = []
        for part in range(3):
            start = pl.multiple_of((part * 8 + source_shard) * part_wide, part_wide)
            out.append(
                remote(
                    local.at[:, pl.ds(part * part_wide, part_wide)],
                    one_full.at[my_rows, pl.ds(start, part_wide)],
                    ps.at[step, part], pr.at[step, part], (rep, target_shard),
                )
            )
        return out

    def own_pieces(index):
        local = grads[index][0].at[rep, me]
        if index == 1:
            at = pl.ds(pl.multiple_of(me * two_wide, two_wide), two_wide)
            return [pltpu.make_async_copy(local, two_full.at[my_rows, at], ds_sem.at[3])]
        out = []
        for part in range(3):
            start = pl.multiple_of((part * 8 + me) * part_wide, part_wide)
            out.append(
                pltpu.make_async_copy(
                    local.at[:, pl.ds(part * part_wide, part_wide)],
                    one_full.at[my_rows, pl.ds(start, part_wide)],
                    ds_sem.at[part],
                )
            )
        return out

    fulls = (one_full, two_full, mix_full, narrow_full)

    def spot_of(index, quarter):
        count = fulls[index].shape[0] // 4
        return fulls[index].at[pl.ds(pl.multiple_of(quarter * count, count), count), :]

    def hand(index, lane, source, quarter, device):
        return remote(
            source, spot_of(index, quarter), fs.at[index, lane], fr.at[index, lane], device
        )

    own_full = []

    def scatter(index, *steps):
        for step in steps:
            for copy in pieces(index, step, me, (me + step) % 8):
                copy.start()
        for copy in own_pieces(index):
            copy.start()

    def hand_out(index):
        source = grads[index][0].at[rep]
        hand(index, 0, source, rep, (across, me)).start()
        hand(index, 1, source, rep, (twin, me)).start()
        copy = pltpu.make_async_copy(source, spot_of(index, rep), ds_sem.at[2 + index])
        copy.start()
        own_full.append(copy)

    def share_sums():
        for step in range(1, 8):
            vec_copy(step).wait_recv()
        running = vec[me]
        for step in range(1, 8):
            running = running + vec_got[step - 1]
        vec_mid[...] = running
        for step in range(1, 4):
            vec_share(step).start()

    def hand_on(index):
        for copy in own_pieces(index):
            copy.wait()
        for step in range(1, 8):
            for copy in pieces(index, step, (me + 8 - step) % 8, me):
                copy.wait_recv()
        hand(index, 0, spot_of(index, rep), rep, (across, me)).start()
        hand(index, 1, spot_of(index, rep), rep, (twin, me)).start()

    def end_sum(index):
        col_copy(index, 3).wait_recv()
        if index == 0:
            own_load(3).wait()
        here = own_block(index, 3)

        def add(left, right):
            left[...] = left[...] + right[...].astype(F32)

        def begin(left, right, both):
            both[...] = left[...].astype(F32) + right[...].astype(F32)

        chunks((here, col_act.at[index, 3], total), begin)

        for slot in (2, 3):
            there, copy = came(index, slot)
            copy.wait_recv()
            chunks((total, there), add)
        copy = pltpu.make_async_copy(total, (out_sum, in_sum)[index], ds_sem.at[6])
        copy.start()
        copy.wait()

    def end_vec():
        for step in range(1, 4):
            vec_share(step).wait_recv()
        vec_full[...] = vec_mid[...] + vec_rep[0] + vec_rep[1] + vec_rep[2]

    def hand_twin(index):
        hand(index, 0, spot_of(index, across), across, (across, me)).wait_recv()
        hand(index, 2, spot_of(index, across), across, (twin, me)).start()

    wait(got_active, got_cot)
    narrow_grad(0)
    trade(3, 0)
    narrow_grad(1)
    trade(3, 1)
    narrow_grad(2)
    across_sum(3)
    narrow_grad(3)
    wait(got_context)
    mix_grad()
    trade(2, 0)
    trade(2, 1)
    wait(*got_narrow, got_slope)
    through_gelu(0, 4)
    got_cols = [load(cols_two, pair, 3)]
    across_sum(2)
    wait(got_second)
    send_along(0, 0)
    wide_grad(0, 8)
    trade(1, 0)
    trade(1, 1)
    got_first = load(first, wide, 6)
    got_cols.append(load(cols_one, duo.at[:, pl.ds(0, one_wide)], 1))
    wait(got_mix, *got_heads)
    through_mix()
    got_norm = load(norm_all, cot, 0)
    across_sum(1)
    send_along(0, 1)
    attend_back(0, 8)
    wait(got_first)
    project_grad(0, 8)
    trade(0, 0)
    trade(0, 1)
    across_sum(0)
    wait(*got_cols, got_norm)
    send_along(0, 2)
    input_part(0)
    input_part(1)
    input_part(2)
    input_part(3)
    send_sums()
    whole(1)
    scatter(1, 1,7,2,6,3,5,4)
    send_along(1, 0)
    whole(0)
    scatter(0, 1,7,2,6,3,5,4)
    whole(3)
    hand_out(3)
    whole(2)
    hand_out(2)
    send_along(1, 1)
    end_sum(0)
    hand_on(1)
    send_along(1, 2)
    share_sums()
    hand_on(0)
    end_sum(1)
    end_vec()
    hand_twin(3)
    hand_twin(2)
    hand_twin(1)
    hand_twin(0)
    for index in range(4):
        source = grads[index][0].at[rep] if index > 1 else spot_of(index, rep)
        hand(index, 0, source, rep, (across, me)).wait_send()
        hand(index, 1, source, rep, (twin, me)).wait_send()
        hand(index, 1, spot_of(index, twin), twin, (twin, me)).wait_recv()
        hand(index, 2, spot_of(index, across), across, (twin, me)).wait_send()
        hand(index, 2, spot_of(index, diagonal), diagonal, (twin, me)).wait_recv()
        side_copy(index).wait_send()
        for slot in (0, 1):
            core_copy(index, slot).wait_send()
    for index in (0, 1):
        for step in range(1, 8):
            for copy in pieces(index, step, me, (me + step) % 8):
                copy.wait_send()
        for step in range(4):
            col_copy(index, step).wait_send()
            if step < 3:
                line_copy(index, step).wait_send()
    for step in range(1, 8):
        vec_copy(step).wait_send()
    for step in range(1, 4):
        vec_share(step).wait_send()
    for copy in own_full:
        copy.wait()


def backward(
    cot_all, norm, first, second, cols_one, cols_two, mix, narrow,
    heads, context, active, slope, cosine, sine, out_part, table,
):
    dma = pltpu.SemaphoreType.DMA
    struct = jax.ShapeDtypeStruct
    vmem = pl.BlockSpec(memory_space=pltpu.VMEM)
    tokens, width = cot_all.shape
    length = tokens // 8
    one, two = cols_one.shape[1], cols_two.shape[1]
    share = width // 32
    quarters = [
        (8, share, one), (8, share, two), (mix.shape[0] // 4, width),
        (narrow.shape[0] // 4, width),
    ]
    lanes = 4 * width // 8 + one + width // 8 + two
    return pl.pallas_call(
        backward_kernel,
        out_shape=(
            struct((length, width), F32),
            struct((length, width), F32),
            struct((4 * share, 8 * one), BF16),
            struct((4 * share, 8 * two), BF16),
            struct(mix.shape, BF16),
            struct(narrow.shape, BF16),
            struct((1, lanes), F32),
        ),
        in_specs=[ANY] * 18 + [vmem],
        out_specs=(ANY,) * 6 + (vmem,),
        scratch_shapes=[pltpu.VMEM((4,) + q, BF16) for q in quarters]
        + [pltpu.VMEM((2,) + q, BF16) for q in quarters]
        + [pltpu.VMEM(q, BF16) for q in quarters]
        + [
            pltpu.VMEM((tokens, width), BF16),
            pltpu.VMEM((width, two), BF16),
            pltpu.VMEM((2 * tokens, two), BF16),
            pltpu.VMEM((tokens, width), BF16),
            pltpu.VMEM((tokens, two), BF16),
            pltpu.VMEM(mix.shape, BF16),
        ]
        + [pltpu.VMEM(h.shape, h.dtype) for h in heads]
        + [
            pltpu.VMEM(context.shape, BF16),
            pltpu.VMEM(context.shape, BF16),
            pltpu.VMEM((tokens, one), BF16),
            pltpu.VMEM(cosine.shape, F32),
            pltpu.VMEM(sine.shape, F32),
            pltpu.VMEM((4, length, width), BF16),
            pltpu.VMEM((2, 4, length, width), BF16),
            pltpu.VMEM((2, 4, length, width), BF16),
            pltpu.VMEM((length, width), F32),
            pltpu.VMEM((8, width), F32),
            pltpu.VMEM((8, 1, lanes), F32),
            pltpu.VMEM((7, 1, lanes), F32),
            pltpu.VMEM((1, lanes), F32),
            pltpu.VMEM((3, 1, lanes), F32),
            dma((14,)), dma((4,)),
            dma((4, 2)), dma((4, 2)), dma((4,)), dma((4,)),
            dma((2, 4)), dma((2, 4)), dma((2, 3)), dma((2, 4)),
            dma((8, 4)), dma((8, 4)), dma((4, 3)), dma((4, 3)),
            dma((7,)), dma((7,)), dma((3,)), dma((3,)), dma((7,)),
        ],
        compiler_params=pltpu.CompilerParams(
            collective_id=1, has_side_effects=True, vmem_limit_bytes=60 << 20
        ),
        name="backward",
    )(
        cot_all, norm, first, second, cols_one, cols_two, mix, narrow,
        *heads, context, active, slope, cosine, sine, out_part, table,
    )


def finish_kernel(
    tok, cot, out_sum, in_sum, out_bias, one, two, mix, narrow, sums,
    output, input_grad, one_out, two_out, mix_out, narrow_out, narrow_sum, *vectors,
):
    own = tok[...].astype(F32)
    center = own - jnp.mean(own, axis=-1, keepdims=True)
    scale = lax.rsqrt(jnp.mean(center * center, axis=-1, keepdims=True) + 1e-05)
    norm = center * scale
    output[...] = (own + out_sum[...] + out_bias[...]).astype(BF16)
    pull = in_sum[...]
    inner = jnp.mean(pull * norm, axis=-1, keepdims=True)
    pull = scale * (pull - jnp.mean(pull, axis=-1, keepdims=True) - norm * inner)
    input_grad[...] = (cot[...].astype(F32) + pull).astype(BF16)
    for source, target in (
        (one, one_out), (two, two_out), (mix, mix_out), (narrow, narrow_out)
    ):
        target[...] = source[...].astype(F32)

    @pl.when(pl.program_id(0) == 0)
    def _():
        start = 0
        for target in vectors:
            count = target.shape[0]
            target[...] = sums[0, start : start + count]
            start += count
        narrow_sum[...] = vectors[5][...]


def finish(tok, cot, out_sum, in_sum, out_bias, one, two, mix, narrow, sums, counts):
    struct = jax.ShapeDtypeStruct
    steps = 8

    def rows(array):
        return pl.BlockSpec((array.shape[0] // steps, array.shape[1]), lambda i: (i, 0))

    def fixed(array):
        return pl.BlockSpec(array.shape, lambda i: (0, 0))

    moved = (one, two, mix, narrow)
    return pl.pallas_call(
        finish_kernel,
        grid=(steps,),
        out_shape=(struct(tok.shape, BF16), struct(tok.shape, BF16))
        + tuple(struct(m.shape, F32) for m in moved)
        + tuple(struct((count,), F32) for count in (counts[5], *counts)),
        in_specs=[rows(tok), rows(cot), rows(out_sum), rows(in_sum), fixed(out_bias)]
        + [rows(m) for m in moved]
        + [fixed(sums)],
        out_specs=(rows(tok), rows(tok))
        + tuple(rows(m) for m in moved)
        + tuple(pl.BlockSpec((count,), lambda i: (0,)) for count in (counts[5], *counts)),
        compiler_params=pltpu.CompilerParams(vmem_limit_bytes=60 << 20),
        name="finish",
    )(tok, cot, out_sum, in_sum, out_bias, *moved, sums)


def tensor_parallel(
    tokens,
    segment_ids,
    positions,
    first_gain,
    first_shift,
    project_weight,
    project_bias,
    mixing_weight,
    mixing_bias,
    second_gain,
    second_shift,
    widen_weight,
    widen_bias,
    narrow_weight,
    narrow_bias,
    cotangent,
):
    (
        cot_all, norm, cols_one, cols_two, first, second, query, keys, values, probs,
        context, active, slope, out_part, cosine, sine, table, out_bias,
    ) = forward(
        tokens, cotangent, project_weight, widen_weight, mixing_weight, narrow_weight,
        (
            first_gain, first_shift, second_gain, second_shift, mixing_bias, narrow_bias,
            project_bias, widen_bias, segment_ids, positions,
        ),
    )
    out_sum, in_sum, full_one, full_two, full_mix, full_narrow, sums = backward(
        cot_all.reshape(-1, D), norm, first, second, cols_one, cols_two, mixing_weight,
        narrow_weight, (query, keys, values, probs), context, active, slope, cosine, sine,
        out_part, table,
    )
    width = D // 8
    (
        output, input_grad, grad_one, grad_two, grad_mix, grad_narrow, sum_narrow,
        sum_first_gain, sum_first_shift, sum_second_gain, sum_second_shift,
        sum_project, sum_cot, sum_widen,
    ) = finish(
        tokens, cotangent, out_sum, in_sum, out_bias, full_one, full_two, full_mix,
        full_narrow, sums,
        (width, width, width, width, project_bias.shape[0], width, widen_bias.shape[0]),
    )
    return (
        output,
        input_grad,
        sum_first_gain,
        sum_first_shift,
        grad_one,
        sum_project,
        grad_mix,
        sum_cot,
        sum_second_gain,
        sum_second_shift,
        grad_two,
        sum_widen,
        grad_narrow,
        sum_narrow,
    )


def solution(mesh):
    head_per_shard = mesh.shape["shard"] == HEADS and mesh.shape["rep"] == 4
    chosen = tensor_parallel if head_per_shard else per_device
    in_specs = (
        P(("rep", "shard"), None),
        P(("rep", "shard")),
        P(("rep", "shard")),
        P("shard"),
        P("shard"),
        P("shard", None),
        P("shard"),
        P("shard", None),
        P("shard"),
        P("shard"),
        P("shard"),
        P("shard", None),
        P("shard"),
        P("shard", None),
        P("shard"),
        P(("rep", "shard"), None),
    )
    out_specs = (
        P(("rep", "shard"), None),
        P(("rep", "shard"), None),
        P("shard"),
        P("shard"),
        P("shard", None),
        P("shard"),
        P("shard", None),
        P("shard"),
        P("shard"),
        P("shard"),
        P("shard", None),
        P("shard"),
        P("shard", None),
        P("shard"),
    )
    return jax.shard_map(
        chosen, mesh=mesh, in_specs=in_specs, out_specs=out_specs, check_vma=False
    )
```

```python
import math

import jax
import jax.numpy as jnp
from jax import lax
from jax.experimental import pallas as pl
from jax.experimental.pallas import tpu as pltpu
from jax.sharding import PartitionSpec as P

D = 2048
HEADS = 8
HEAD_DIM = 256
ROT = 64
FF = 8192


def layer_norm(values, gain, shift):
    center = values - jnp.mean(values, axis=-1, keepdims=True)
    spread = jnp.mean(center * center, axis=-1, keepdims=True)
    return center * lax.rsqrt(spread + 1e-05) * gain + shift


def angles(positions):
    freqs = 10000.0 ** (-(jnp.arange(ROT // 2, dtype=jnp.float32) * 2.0 / ROT))
    turned = positions.astype(jnp.float32)[..., None] * freqs
    return (jnp.cos(turned), jnp.sin(turned))


def rotary(values, cosine, sine):
    half = ROT // 2
    front = values[..., :half]
    back = values[..., half:ROT]
    return jnp.concatenate(
        [front * cosine - back * sine, back * cosine + front * sine, values[..., ROT:]], axis=-1
    )


def exact_gelu(values):
    return jax.nn.gelu(values, approximate=False)


def contract_rows(left, right):
    return lax.dot_general(
        left, right, (((0,), (0,)), ((), ())), preferred_element_type=jnp.float32
    )


def times_rows(left, piece):
    return lax.dot_general(
        left, piece, (((1,), (1,)), ((), ())), preferred_element_type=jnp.float32
    )


def weight_terms(left_one, left_two, left_mix, left_act, d_joint, d_widened, cotangent):

    def wide_term(start, count):
        return jnp.concatenate(
            [
                contract_rows(left_one, d_joint),
                contract_rows(left_two, d_widened),
                contract_rows(left_mix, cotangent),
            ],
            axis=1,
        )

    def down_term(start, count):
        return contract_rows(left_act, cotangent)

    return (wide_term, down_term)


def per_device(
    tokens,
    segment_ids,
    positions,
    first_gain,
    first_shift,
    project_weight,
    project_bias,
    mixing_weight,
    mixing_bias,
    second_gain,
    second_shift,
    widen_weight,
    widen_bias,
    narrow_weight,
    narrow_bias,
    cotangent,
):
    length = tokens.shape[0]
    shards = lax.axis_size("shard")
    gain_one, shift_one, gain_two, shift_two, joint_bias, mix_bias, wide_bias, narrow_full = (
        lax.all_gather(first_gain, "shard", axis=0, tiled=True),
        lax.all_gather(first_shift, "shard", axis=0, tiled=True),
        lax.all_gather(second_gain, "shard", axis=0, tiled=True),
        lax.all_gather(second_shift, "shard", axis=0, tiled=True),
        lax.all_gather(project_bias, "shard", axis=0, tiled=True),
        lax.all_gather(mixing_bias, "shard", axis=0, tiled=True),
        lax.all_gather(widen_bias, "shard", axis=0, tiled=True),
        lax.all_gather(narrow_bias, "shard", axis=0, tiled=True),
    )
    inputs = tokens.astype(jnp.float32)
    first_norm, first_pull = jax.vjp(layer_norm, inputs, gain_one, shift_one)
    second_norm, second_pull = jax.vjp(layer_norm, inputs, gain_two, shift_two)
    first = first_norm.astype(jnp.bfloat16)
    second = second_norm.astype(jnp.bfloat16)
    pieces = (
        lax.all_gather(project_weight, "shard", axis=0, tiled=True),
        lax.all_gather(widen_weight, "shard", axis=0, tiled=True),
    )
    part_one = jnp.dot(first, pieces[0], preferred_element_type=jnp.float32)
    part_two = jnp.dot(second, pieces[1], preferred_element_type=jnp.float32)
    joint = part_one + joint_bias
    widened = part_two + wide_bias
    shaped = joint.reshape(length, 3, HEADS, HEAD_DIM)
    cosine, sine = angles(positions)
    cosine = cosine[:, None, :]
    sine = sine[:, None, :]

    def place(query_in, key_in):
        return (rotary(query_in, cosine, sine) * HEAD_DIM ** (-0.5), rotary(key_in, cosine, sine))

    (query_turned, key_turned), rotate_pull = jax.vjp(place, shaped[:, 0], shaped[:, 1])
    query = query_turned.astype(jnp.bfloat16)
    keys = key_turned.astype(jnp.bfloat16)
    values = shaped[:, 2].astype(jnp.bfloat16)
    order = jnp.arange(length)
    allowed = ((segment_ids[:, None] == segment_ids[None, :]) & (order[:, None] >= order[None, :]))[
        None
    ]

    def masked_scores():
        raw = jnp.einsum("qhe,khe->hqk", query, keys, preferred_element_type=jnp.float32)
        return jnp.where(allowed, raw, -1e30)

    scores = masked_scores()
    highest = jnp.max(scores, axis=-1, keepdims=True)
    raised = jnp.exp(scores - highest)
    summed = jnp.sum(raised, axis=-1, keepdims=True)
    log_summed = highest + jnp.log(summed)
    weights = (raised / summed).astype(jnp.bfloat16)
    context = (
        jnp.einsum("hqk,khe->qhe", weights, values, preferred_element_type=jnp.float32)
        .reshape(length, D)
        .astype(jnp.bfloat16)
    )
    attention = (
        jnp.dot(
            context,
            lax.all_gather(mixing_weight, "shard", axis=0, tiled=True),
            preferred_element_type=jnp.float32,
        )
        + mix_bias
    )
    active_full, gelu_pull = jax.vjp(exact_gelu, widened)
    active = active_full.astype(jnp.bfloat16)
    mlp = (
        jnp.dot(
            active,
            lax.all_gather(narrow_weight, "shard", axis=0, tiled=True),
            preferred_element_type=jnp.float32,
        )
        + narrow_full
    )
    output = (inputs + attention + mlp).astype(jnp.bfloat16)

    def back_rows(piece):
        return times_rows(cotangent, piece)

    d_active = back_rows(lax.all_gather(narrow_weight, "shard", axis=0, tiled=True))
    d_widened = gelu_pull(d_active)[0].astype(jnp.bfloat16)
    d_context = back_rows(lax.all_gather(mixing_weight, "shard", axis=0, tiled=True))
    d_context = d_context.astype(jnp.bfloat16).reshape(length, HEADS, HEAD_DIM)
    again = jnp.exp(masked_scores() - log_summed)
    again_low = again.astype(jnp.bfloat16)
    d_weights = jnp.einsum("qhe,khe->hqk", d_context, values, preferred_element_type=jnp.float32)
    d_values = jnp.einsum("hqk,qhe->khe", again_low, d_context, preferred_element_type=jnp.float32)
    d_scores = (again * (d_weights - jnp.sum(d_weights * again, axis=-1, keepdims=True))).astype(
        jnp.bfloat16
    )
    d_query = jnp.einsum("hqk,khe->qhe", d_scores, keys, preferred_element_type=jnp.float32)
    d_keys = jnp.einsum("hqk,qhe->khe", d_scores, query, preferred_element_type=jnp.float32)
    d_query_in, d_key_in = rotate_pull((d_query, d_keys))
    d_joint = jnp.concatenate(
        [d_query_in.reshape(length, D), d_key_in.reshape(length, D), d_values.reshape(length, D)],
        axis=1,
    ).astype(jnp.bfloat16)
    pieces = lax.all_gather((project_weight, widen_weight), "shard", axis=0, tiled=True)
    stacked = jnp.concatenate(
        [times_rows(d_joint, pieces[0]), times_rows(d_widened, pieces[1])], axis=0
    )
    d_in_one, d_gain_one, d_shift_one = first_pull(stacked[:length])
    d_in_two, d_gain_two, d_shift_two = second_pull(stacked[length:])
    input_grad = (cotangent.astype(jnp.float32) + d_in_one + d_in_two).astype(jnp.bfloat16)
    sums = lax.psum(
        (
            d_gain_one,
            d_shift_one,
            d_gain_two,
            d_shift_two,
            jnp.sum(d_joint, axis=0, dtype=jnp.float32),
            jnp.sum(cotangent, axis=0, dtype=jnp.float32),
            jnp.sum(d_widened, axis=0, dtype=jnp.float32),
        ),
        ("rep", "shard"),
    )
    owner = lax.axis_index("shard")

    def own_part(vector):
        share = vector.shape[0] // shards
        return lax.dynamic_slice_in_dim(vector, owner * share, share)

    owned = [own_part(vector) for vector in sums]
    wide_term, down_term = weight_terms(
        first, second, context, active, d_joint, d_widened, cotangent
    )
    wide_part = lax.psum_scatter(
        wide_term(jnp.int32(0), lax.axis_size("shard") * (D // shards)).astype(jnp.bfloat16),
        "shard",
        scatter_dimension=0,
        tiled=True,
    ).astype(jnp.float32)
    down_part = lax.psum_scatter(
        down_term(jnp.int32(0), lax.axis_size("shard") * (FF // shards)).astype(jnp.bfloat16),
        "shard",
        scatter_dimension=0,
        tiled=True,
    ).astype(jnp.float32)
    wide_part, down_part = (
        lax.psum(wide_part.astype(jnp.bfloat16), "rep").astype(jnp.float32),
        lax.psum(down_part.astype(jnp.bfloat16), "rep").astype(jnp.float32),
    )
    return (
        output,
        input_grad,
        owned[0],
        owned[1],
        wide_part[:, : 3 * D],
        owned[4],
        wide_part[:, 3 * D + FF :],
        owned[5],
        owned[2],
        owned[3],
        wide_part[:, 3 * D : 3 * D + FF],
        owned[6],
        down_part,
        owned[5],
    )


MESH = pl.DeviceIdType.MESH
ANY = pl.BlockSpec(memory_space=pl.ANY)


def places():
    rep, me = lax.axis_index("rep"), lax.axis_index("shard")
    core, side = rep % 2, rep // 2
    col, line = me % 2, me // 2
    return rep, me, core, side, col, line


def greet(peers):
    barrier = pltpu.get_barrier_semaphore()
    for peer in peers:
        pl.semaphore_signal(barrier, inc=1, device_id=peer, device_id_type=MESH)
    pl.semaphore_wait(barrier, len(peers))


def remote(source, target, send, recv, device):
    return pltpu.make_async_remote_copy(
        src_ref=source,
        dst_ref=target,
        send_sem=send,
        recv_sem=recv,
        device_id=device,
        device_id_type=MESH,
    )


F32, BF16 = jnp.float32, jnp.bfloat16
CHUNK = 256


def turned(value, cosine, sine):
    near = value[:, :128]
    lane = lax.broadcasted_iota(jnp.int32, near.shape, 1)
    partner = jnp.where(
        lane < ROT // 2,
        pltpu.roll(near, 128 - ROT // 2, 1),
        pltpu.roll(near, ROT // 2, 1),
    )
    return jnp.concatenate([near * cosine + partner * sine, value[:, 128:]], axis=1)


def dot(left, right, dims=((1,), (0,))):
    return lax.dot_general(left, right, (dims, ((), ())), preferred_element_type=F32)


def forward_kernel(
    tok, cot, wide_one, wide_two, mix, narrow,
    gain_one, shift_one, gain_two, shift_two, mix_bias, narrow_bias, joint_bias, wide_bias,
    segments, positions,
    cot_all, norm_out, cols_one_out, cols_two_out, first_out, second_out,
    query_out, key_out, value_out, probs_out, context_out, active_out, slope_out,
    out_part, cosine_out, sine_out, gains_out, bias_out,
    tok_all, cols_one, cols_two, mix_v, narrow_v, norms, first, second, joint, query, key, value,
    probs, context, active, slope, partial, cosines, sines, small, small_all, table,
    line_send, line_recv, col_send, col_recv,
    own_sem, piece_send, piece_recv, side_send, side_recv, core_send, core_recv,
    small_send, small_recv, load_sem, save_sem,
):
    rep, me, core, side, col, line = places()
    twin = rep + 1 - 2 * core
    across = rep + 2 - 4 * side
    twin_across = across + 1 - 2 * core
    other = me + 1 - 2 * col
    wide = cols_one.shape[1] // 3
    two_wide = cols_two.shape[1]
    rows = wide_one.shape[0]
    share = rows // 4
    length = tok.shape[0]
    width = tok.shape[1]

    offset = 0
    for ref in (gain_one, shift_one, gain_two, shift_two, mix_bias, narrow_bias, joint_bias,
                wide_bias, segments, positions):
        count = ref.shape[0]
        small[0:1, offset : offset + count] = ref[...].astype(F32)[None, :]
        offset += count

    greet(
        [(rep, (me + step) % 8) for step in range(1, 8)]
        + [(twin, me), (across, me)]
    )

    def along(which, direction, step):
        array, gathered, part = pairs[which]
        owner = line - direction * (step - 1)
        there = gathered.at[owner * 2 + col, part, :]
        source = array.at[part, :] if step == 1 else there
        lane = which * 6 + (0 if direction == 1 else 3) + step - 1
        return remote(
            source,
            there,
            line_send.at[lane],
            line_recv.at[lane],
            (rep, (line + direction) * 2 + col),
        )

    def sends(direction, step):
        if direction == 1:
            return (line >= step - 1) & (line <= 2)
        return (line <= 4 - step) & (line >= 1)

    def gets(direction, step):
        if direction == 1:
            return line >= step
        return line <= 3 - step

    def sideways(which, direction, step):
        array, gathered, part = pairs[which]
        owner = line - direction * step
        there = gathered.at[owner * 2 + col, part, :]
        source = array.at[part, :] if step == 0 else there
        lane = which * 7 + (0 if direction == 1 else 3) + step
        return remote(
            source,
            there,
            col_send.at[lane],
            col_recv.at[lane],
            (rep, other),
        )

    def from_other(which, direction, step):
        _, gathered, part = pairs[which]
        owner = line - direction * step
        lane = which * 7 + (0 if direction == 1 else 3) + step
        here = gathered.at[owner * 2 + 1 - col, part, :]
        return remote(here, here, col_send.at[lane], col_recv.at[lane], (rep, other))

    halves = (pl.ds(0, length // 2), pl.ds(length // 2, length // 2))
    pairs = [
        (array, gathered, part)
        for array, gathered in ((tok, tok_all), (cot, cot_all))
        for part in halves
    ]
    turns = [(direction, step) for step in (1, 2, 3) for direction in (1, -1)]

    def begin(which):
        for direction in (1, -1):
            @pl.when(sends(direction, 1))
            def _(direction=direction):
                along(which, direction, 1).start()
        sideways(which, 1, 0).start()

    def pass_on(which, direction, step):
        _, gathered, part = pairs[which]

        @pl.when(gets(direction, step))
        def _():
            owner = line - direction * step
            lane = which * 6 + (0 if direction == 1 else 3) + step - 1
            here = gathered.at[owner * 2 + col, part, :]
            remote(
                here, here, line_send.at[lane], line_recv.at[lane], (rep, other)
            ).wait_recv()
            sideways(which, direction, step).start()

        if step < 3:
            @pl.when(sends(direction, step + 1))
            def _():
                along(which, direction, step + 1).start()

    def landed(which):
        for direction, step in turns:
            @pl.when(gets(direction, step))
            def _(direction=direction, step=step):
                from_other(which, direction, step).wait_recv()

        from_other(which, 1, 0).wait_recv()

    def sent(which):
        for direction, step in turns:
            @pl.when(sends(direction, step))
            def _(direction=direction, step=step):
                along(which, direction, step).wait_send()

            @pl.when(gets(direction, step))
            def _(direction=direction, step=step):
                sideways(which, direction, step).wait_send()

        sideways(which, 1, 0).wait_send()

    mine = pl.multiple_of(rep * share, share)

    def pieces(step):
        target = (me + step) % 8
        place = pl.ds(pl.multiple_of(me * rows + rep * share, share), share)
        out = []
        for part in range(3):
            out.append(
                remote(
                    wide_one.at[
                        pl.ds(mine, share),
                        pl.ds(pl.multiple_of((part * 8 + target) * wide, wide), wide),
                    ],
                    cols_one.at[place, pl.ds(part * wide, wide)],
                    piece_send.at[step - 1, part],
                    piece_recv.at[step - 1, part],
                    (rep, target),
                )
            )
        out.append(
            remote(
                wide_two.at[
                    pl.ds(mine, share),
                    pl.ds(pl.multiple_of(target * two_wide, two_wide), two_wide),
                ],
                cols_two.at[place, :],
                piece_send.at[step - 1, 3],
                piece_recv.at[step - 1, 3],
                (rep, target),
            )
        )
        return out

    def arrived(step):
        source = (me + 8 - step) % 8
        place = pl.ds(pl.multiple_of(source * rows + rep * share, share), share)
        here = [cols_one.at[place, pl.ds(part * wide, wide)] for part in range(3)]
        here.append(cols_two.at[place, :])
        return [
            remote(
                ref, ref, piece_send.at[step - 1, part], piece_recv.at[step - 1, part],
                (rep, source),
            )
            for part, ref in enumerate(here)
        ]

    def shares(step, quarter, send, recv, lane, device):
        source = (me + 8 - step) % 8
        place = pl.ds(pl.multiple_of(source * rows + quarter * share, share), share)
        return [
            remote(
                array.at[place, :], array.at[place, :],
                send.at[lane, step - 1, index], recv.at[lane, step - 1, index], device,
            )
            for index, array in enumerate((cols_one, cols_two))
        ]

    def little(step):
        return remote(
            small, small_all.at[me], small_send.at[step - 1], small_recv.at[step - 1],
            (rep, (me + step) % 8),
        )

    here = pl.ds(pl.multiple_of(me * rows, rows), rows)
    own = [
        pltpu.make_async_copy(tok, tok_all.at[me], own_sem.at[0]),
        pltpu.make_async_copy(cot, cot_all.at[me], own_sem.at[1]),
        pltpu.make_async_copy(small, small_all.at[me], own_sem.at[2]),
        pltpu.make_async_copy(
            wide_two.at[:, pl.ds(pl.multiple_of(me * two_wide, two_wide), two_wide)],
            cols_two.at[here, :],
            own_sem.at[3],
        ),
    ] + [
        pltpu.make_async_copy(
            wide_one.at[:, pl.ds(pl.multiple_of((part * 8 + me) * wide, wide), wide)],
            cols_one.at[here, pl.ds(part * wide, wide)],
            own_sem.at[4 + part],
        )
        for part in range(3)
    ]
    loads = [
        pltpu.make_async_copy(mix, mix_v, load_sem.at[0]),
        pltpu.make_async_copy(narrow, narrow_v, load_sem.at[1]),
    ]

    def send_small():
        for step in range(1, 8):
            little(step).start()

    def send_pieces(*steps):
        for step in steps:
            for copy in pieces(step):
                copy.start()

    def load_own():
        for copy in own + loads:
            copy.start()

    def take_small():
        for step in range(1, 8):
            source = (me + 8 - step) % 8
            remote(
                small_all.at[source], small_all.at[source], small_send.at[step - 1],
                small_recv.at[step - 1], (rep, source),
            ).wait_recv()
        own[2].wait()
        for kind in range(6):
            for shard in range(8):
                table[kind : kind + 1, shard * 256 : shard * 256 + 256] = small_all[
                    shard, :, kind * 256 : kind * 256 + 256
                ]
        for part in range(3):
            spot = part * 8 + me
            table[6:7, part * wide : (part + 1) * wide] = small_all[
                spot // 3, :, pl.ds(pl.multiple_of(1536 + (spot % 3) * 256, 256), 256)
            ]
        gains_out[...] = table[...]
        bias_out[...] = table[4:5, :] + table[5:6, :]

    def relay(*steps):
        for step in steps:
            for copy in arrived(step):
                copy.wait_recv()
            for copy in shares(step, rep, side_send, side_recv, 0, (across, me)):
                copy.start()
            for copy in shares(step, rep, core_send, core_recv, 0, (twin, me)):
                copy.start()

    def relay_across(*steps):
        for step in steps:
            for copy in shares(step, across, side_send, side_recv, 0, (across, me)):
                copy.wait_recv()
            for copy in shares(step, across, core_send, core_recv, 1, (twin, me)):
                copy.start()

    def take_weights():
        for step in range(1, 8):
            for copy in shares(step, twin, core_send, core_recv, 0, (twin, me)):
                copy.wait_recv()
        for step in range(1, 8):
            for copy in shares(step, twin_across, core_send, core_recv, 1, (twin, me)):
                copy.wait_recv()
        for copy in own[3:]:
            copy.wait()
        for copy in loads:
            copy.wait()
        save((cols_one, cols_one_out), (cols_two, cols_two_out))

    saves = []

    def save(*items):
        for source, target in items:
            copy = pltpu.make_async_copy(source, target, save_sem.at[len(saves)])
            copy.start()
            saves.append(copy)

    def norm_all():
        gains_one, shifts_one = table[0:1, :], table[1:2, :]
        gains_two, shifts_two = table[2:3, :], table[3:4, :]

        @pl.loop(0, 8 * length // 32)
        def _(index):
            block, part = index // (length // 32), index % (length // 32)
            at = pl.ds(pl.multiple_of(part * 32, 32), 32)
            raw = tok_all[block, at, :].astype(F32)
            center = raw - jnp.mean(raw, axis=-1, keepdims=True)
            spread = jnp.mean(center * center, axis=-1, keepdims=True)
            norm = center * lax.rsqrt(spread + 1e-05)
            there = pl.ds(pl.multiple_of(index * 32, 32), 32)
            norms[there, :] = norm.astype(BF16)
            first[there, :] = (norm * gains_one + shifts_one).astype(BF16)
            second[there, :] = (norm * gains_two + shifts_two).astype(BF16)

        save((norms, norm_out), (first, first_out), (second, second_out))

    def project(index):
        bias_row = table[6:7, 0 : 3 * wide]
        wide_row = small[0:1, 2304 : 2304 + two_wide]
        at = pl.ds(index * CHUNK, CHUNK)
        for part in range(3):
            spot = slice(part * wide, (part + 1) * wide)
            joint[at, spot] = dot(first[at, :], cols_one[:, spot]) + bias_row[:, spot]
        for part in range(two_wide // 256):
            spot = slice(part * 256, (part + 1) * 256)
            value_now = dot(second[at, :], cols_two[:, spot]) + wide_row[:, spot]
            cdf = 0.5 * (1.0 + lax.erf(value_now * (0.5**0.5)))
            density = jnp.exp(-0.5 * value_now * value_now) * (0.5 / jnp.pi) ** 0.5
            active[at, spot] = (value_now * cdf).astype(BF16)
            slope[at, spot] = (cdf + value_now * density).astype(BF16)

    lane = lax.broadcasted_iota(jnp.int32, (1, 128), 1)
    frequency = jnp.where(
        lane < ROT,
        jnp.exp((lane % (ROT // 2)).astype(F32) * (-2.0 / ROT * math.log(10000.0))),
        0.0,
    )
    signs = jnp.where(lane < ROT // 2, -1.0, 1.0)
    tall = lax.broadcasted_iota(jnp.int32, (length, length), 0)
    flat = lax.broadcasted_iota(jnp.int32, (length, length), 1)
    ids_at = 2304 + two_wide

    def attend(block):
        at = pl.ds(block * length, length)
        ids = jnp.broadcast_to(small_all[block, :, ids_at : ids_at + 128], (length, length))
        spots = jnp.broadcast_to(
            small_all[block, :, ids_at + 128 : ids_at + 256], (length, length)
        )
        angle = spots.T * frequency
        cosine, sine = jnp.cos(angle), jnp.sin(angle) * signs
        query_now = (turned(joint[at, 0:wide], cosine, sine) * HEAD_DIM**-0.5).astype(BF16)
        key_now = turned(joint[at, wide : 2 * wide], cosine, sine).astype(BF16)
        value_now = joint[at, 2 * wide :].astype(BF16)
        scores = dot(query_now, key_now, ((1,), (1,)))
        allowed = (ids == ids.T) & (flat <= tall)
        scores = jnp.where(allowed, scores, -1e30)
        lifted = jnp.exp(scores - jnp.max(scores, axis=-1, keepdims=True))
        weights = lifted / jnp.sum(lifted, axis=-1, keepdims=True)
        cosines[at, :], sines[at, :] = cosine, sine
        query[at, :], key[at, :], value[at, :] = query_now, key_now, value_now
        probs[at, :] = weights
        context[at, :] = dot(weights.astype(BF16), value_now).astype(BF16)

    def finish(index):
        at = pl.ds(index * CHUNK, CHUNK)
        for part in range(width // 256):
            spot = slice(part * 256, (part + 1) * 256)
            partial[at, spot] = (
                dot(context[at, :], mix_v[:, spot]) + dot(active[at, :], narrow_v[:, spot])
            ).astype(BF16)

    def save_all():
        save(
            (query, query_out), (key, key_out), (value, value_out), (probs, probs_out),
            (context, context_out), (active, active_out), (slope, slope_out),
            (partial, out_part), (cosines, cosine_out), (sines, sine_out),
        )

    begin(0)
    begin(1)
    send_small()
    load_own()
    pass_on(0, 1, 1)
    pass_on(0, -1, 1)
    send_pieces(1,7)
    pass_on(1, 1, 1)
    pass_on(1, -1, 1)
    send_pieces(2,6)
    pass_on(0, 1, 2)
    pass_on(0, -1, 2)
    pass_on(1, 1, 2)
    pass_on(1, -1, 2)
    send_pieces(3,5,4)
    pass_on(0, 1, 3)
    pass_on(0, -1, 3)
    pass_on(1, 1, 3)
    pass_on(1, -1, 3)
    relay(1,7)
    begin(2)
    begin(3)
    take_small()
    own[0].wait()
    relay(2,6,3,5,4)
    landed(0)
    landed(1)
    norm_all()
    pass_on(2, 1, 1)
    pass_on(2, -1, 1)
    pass_on(3, 1, 1)
    pass_on(3, -1, 1)
    relay_across(1,7,2,6,3,5,4)
    pass_on(2, 1, 2)
    pass_on(2, -1, 2)
    pass_on(3, 1, 2)
    pass_on(3, -1, 2)
    take_weights()
    project(0)
    pass_on(2, 1, 3)
    pass_on(2, -1, 3)
    pass_on(3, 1, 3)
    pass_on(3, -1, 3)
    attend(0)
    attend(1)
    finish(0)
    project(1)
    attend(2)
    attend(3)
    finish(1)
    project(2)
    attend(4)
    attend(5)
    finish(2)
    project(3)
    attend(6)
    attend(7)
    finish(3)
    save_all()
    sent(0)
    sent(1)
    for step in range(1, 8):
        for copy in pieces(step):
            copy.wait_send()
        for copy in shares(step, rep, side_send, side_recv, 0, (across, me)):
            copy.wait_send()
        for copy in shares(step, rep, core_send, core_recv, 0, (twin, me)):
            copy.wait_send()
        for copy in shares(step, across, core_send, core_recv, 1, (twin, me)):
            copy.wait_send()
        little(step).wait_send()
    own[1].wait()
    for copy in saves:
        copy.wait()
    sent(2)
    sent(3)
    landed(2)
    landed(3)


def forward(tok, cot, wide_one, wide_two, mix, narrow, vectors):
    dma = pltpu.SemaphoreType.DMA
    length, width = tok.shape
    rows, one = wide_one.shape
    two = wide_two.shape[1]
    one, two = one // 8, two // 8
    total = 8 * length
    struct = jax.ShapeDtypeStruct
    vmem = pl.BlockSpec(memory_space=pltpu.VMEM)
    saved = [
        ((total, HEAD_DIM), BF16), ((total, HEAD_DIM), BF16), ((total, HEAD_DIM), BF16),
        ((total, length), F32), ((total, HEAD_DIM), BF16), ((total, two), BF16),
        ((total, two), BF16), ((total, width), BF16), ((total, length), F32),
        ((total, length), F32),
    ]
    packed = sum(v.shape[0] for v in vectors)
    return pl.pallas_call(
        forward_kernel,
        out_shape=(
            struct((8, length, width), BF16),
            struct((total, width), BF16),
            struct((rows * 8, one), BF16),
            struct((rows * 8, two), BF16),
            struct((total, width), BF16),
            struct((total, width), BF16),
        )
        + tuple(struct(*s) for s in saved)
        + (struct((8, width), F32), struct((1, width), F32)),
        in_specs=[ANY] * 6 + [vmem] * len(vectors),
        out_specs=(ANY,) * 16 + (vmem,) * 2,
        scratch_shapes=[
            pltpu.VMEM((8, length, width), BF16),
            pltpu.VMEM((rows * 8, one), BF16),
            pltpu.VMEM((rows * 8, two), BF16),
            pltpu.VMEM(mix.shape, BF16),
            pltpu.VMEM(narrow.shape, BF16),
            pltpu.VMEM((total, width), BF16),
            pltpu.VMEM((total, width), BF16),
            pltpu.VMEM((total, width), BF16),
            pltpu.VMEM((total, one), F32),
        ]
        + [pltpu.VMEM(*s) for s in saved]
        + [
            pltpu.VMEM((1, packed), F32),
            pltpu.VMEM((8, 1, packed), F32),
            pltpu.VMEM((8, width), F32),
            dma((24,)), dma((24,)), dma((28,)), dma((28,)),
            dma((7,)), dma((7, 4)), dma((7, 4)),
            dma((1, 7, 2)), dma((1, 7, 2)), dma((2, 7, 2)), dma((2, 7, 2)),
            dma((7,)), dma((7,)), dma((2,)), dma((15,)),
        ],
        compiler_params=pltpu.CompilerParams(
            collective_id=0, has_side_effects=True, vmem_limit_bytes=60 << 20
        ),
        name="forward",
    )(tok, cot, wide_one, wide_two, mix, narrow, *vectors)


def backward_kernel(
    cot_all, norm_all, first, second, cols_one, cols_two, mix, narrow,
    query_all, key_all, value_all, probs_all, context_all, active_all, slope_all,
    cosine_all, sine_all, out_part, table,
    out_sum, in_sum, one_full, two_full, mix_full, narrow_full, vec_full,
    grad_one, grad_two, grad_mix, grad_nar,
    core_one, core_two, core_mix, core_nar,
    side_one, side_two, side_mix, side_nar,
    cot, pair, duo, wide, d_widened, mix_v, query, key, value, probs, context, d_context,
    d_joint, cosine, sine, own_act, col_act, line_act, total, sums,
    vec, vec_got, vec_mid, vec_rep,
    load_sem, act_sem, cs, cr, ss, sr, ys, yr, zs, zr, ps, pr, fs, fr, vs, vr, us, ur, ds_sem,
):
    rep, me, core, side, col, line = places()
    twin = rep + 1 - 2 * core
    across = rep + 2 - 4 * side
    diagonal = across + 1 - 2 * core
    other = me + 1 - 2 * col
    length = out_sum.shape[0]
    width = out_sum.shape[1]
    tokens = wide.shape[0]
    half = width // 2
    two_wide = d_widened.shape[1]
    one_wide = d_joint.shape[1]
    part_wide = one_wide // 3
    share = grad_one.shape[2]
    greet(
        [(rep, (me + step) % 8) for step in range(1, 8)]
        + [(twin, me), (across, me), (diagonal, me)]
    )
    grads = (
        (grad_one, core_one, side_one),
        (grad_two, core_two, side_two),
        (grad_mix, core_mix, side_mix),
        (grad_nar, core_nar, side_nar),
    )

    def core_copy(index, slot):
        full, got, _ = grads[index]
        quarter = (across if slot == 0 else rep) + 1 - 2 * core
        return remote(
            full.at[quarter], got.at[slot], cs.at[index, slot], cr.at[index, slot],
            (twin, me),
        )

    def side_copy(index):
        full, _, got = grads[index]
        return remote(full.at[across], got, ss.at[index], sr.at[index], (across, me))

    inner = (line == 1) | (line == 2)

    def target_of(step):
        if step == 0:
            return 3 * ((line + 1) % 2)
        if step == 1:
            return (line + 2) % 4
        if step == 2:
            return 1 + line % 2
        return line

    def block_rows(target, column):
        return pl.ds(pl.multiple_of((target * 2 + column) * length, length), length)

    def col_copy(index, step):
        target = target_of(step)
        if index == 0:
            source = out_part.at[block_rows(target, 1 - col), :]
        else:
            source = wide.at[block_rows(target, 1 - col), :]
        return remote(
            source, col_act.at[index, step], ys.at[index, step], yr.at[index, step],
            (rep, other),
        )

    def own_block(index, step):
        if index == 0:
            return own_act.at[step]
        return wide.at[block_rows(target_of(step), col), :]

    def own_load(step):
        return pltpu.make_async_copy(
            out_part.at[block_rows(target_of(step), col), :], own_act.at[step],
            act_sem.at[step],
        )

    def line_copy(index, step):
        slot = jnp.where(inner, (2, 3, 3)[step], step)
        goal = jnp.where(inner, target_of(step), 1 + line // 2)
        return remote(
            own_block(index, step), line_act.at[index, slot], zs.at[index, step],
            zr.at[index, slot], (rep, goal * 2 + col),
        )

    def came(index, slot):
        here = line_act.at[index, slot]
        return here, remote(here, here, zs.at[index, 0], zr.at[index, slot], (rep, other))

    def vec_copy(step):
        target = (me + step) % 8
        return remote(
            vec.at[target], vec_got.at[step - 1], vs.at[step - 1], vr.at[step - 1],
            (rep, target),
        )

    def vec_share(step):
        return remote(
            vec_mid, vec_rep.at[step - 1], us.at[step - 1], ur.at[step - 1],
            ((rep + step) % 4, me),
        )

    def load(source, target, lane):
        copy = pltpu.make_async_copy(source, target, load_sem.at[lane])
        copy.start()
        return copy

    active, slope = duo.at[pl.ds(0, tokens), :], duo.at[pl.ds(tokens, tokens), :]
    got_cot = load(cot_all, cot, 0)
    got_active = load(active_all, active, 1)
    vec[...] = jnp.zeros_like(vec)
    sums[...] = jnp.zeros_like(sums)

    def add_two(target, left, right):
        target[...] = (left[...].astype(F32) + right[...].astype(F32)).astype(BF16)

    def chunks(refs, function):
        shape = refs[0].shape
        if len(shape) == 3:
            per = shape[1] // 16

            @pl.loop(0, shape[0] * per)
            def _(index):
                at = pl.ds(pl.multiple_of((index % per) * 16, 16), 16)
                function(*[ref.at[index // per, at, :] for ref in refs])
        else:

            @pl.loop(0, shape[0] // 16)
            def _(index):
                at = pl.ds(pl.multiple_of(index * 16, 16), 16)
                function(*[ref.at[at, :] for ref in refs])

    def across_sum(index):
        full, got, _ = grads[index]
        core_copy(index, 0).wait_recv()
        here = full.at[across]
        chunks((here, got.at[0]), lambda left, right: add_two(left, left, right))
        side_copy(index).start()

    def trade(index, slot):
        core_copy(index, slot).start()

    def wait(*copies):
        for copy in copies:
            copy.wait()

    def narrow_grad(order):
        quarter = (diagonal, twin, across, rep)[order]
        at = pl.ds(pl.multiple_of(quarter * 256, 256), 256)
        for part in range(width // 512):
            spot = pl.ds(part * 512, 512)
            grad_nar[quarter, :, spot] = dot(
                active[:, at], cot[:, spot], ((0,), (0,))
            ).astype(BF16)

    def mix_grad():
        for part in range(width // 512):
            spot = pl.ds(part * 512, 512)
            found = dot(context[...], cot[:, spot], ((0,), (0,))).astype(BF16)
            for quarter in range(4):
                grad_mix[quarter, :, spot] = found[quarter * share : (quarter + 1) * share]

    def through_gelu(low_index, high_index):
        @pl.loop(low_index, high_index)
        def _(index):
            at = pl.ds(pl.multiple_of(index * 256, 256), 256)
            for part in range(two_wide // 256):
                spot = pl.ds(part * 256, 256)
                low, high = pl.ds(part * 256, 256), pl.ds(two_wide + part * 256, 256)
                found = dot(cot[at, 0:half], pair[low, :], ((1,), (1,)))
                found = found + dot(cot[at, half:width], pair[high, :], ((1,), (1,)))
                found = (found * slope[at, spot].astype(F32)).astype(BF16)
                d_widened[at, spot] = found
                sums[5:6, spot] = sums[5:6, spot] + jnp.sum(
                    found.astype(F32), axis=0, keepdims=True
                )

    def wide_grad(low_index, high_index):
        @pl.loop(low_index, high_index)
        def _(shard):
            at = pl.ds(pl.multiple_of(shard * 256, 256), 256)
            for part in range(two_wide // 512):
                spot = pl.ds(part * 512, 512)
                found = dot(wide[:, at], d_widened[:, spot], ((0,), (0,))).astype(BF16)
                for quarter in range(4):
                    grad_two[quarter, shard, :, spot] = found[
                        quarter * share : (quarter + 1) * share
                    ]

    def through_mix():
        @pl.loop(0, tokens // 256)
        def _(index):
            at = pl.ds(pl.multiple_of(index * 256, 256), 256)
            d_context[at, :] = dot(cot[at, :], mix_v[...], ((1,), (1,))).astype(BF16)

        @pl.loop(0, length // 16)
        def _(index):
            at = pl.ds(pl.multiple_of(me * length + index * 16, 16), 16)
            sums[4:5, :] = sums[4:5, :] + jnp.sum(
                cot[at, :].astype(F32), axis=0, keepdims=True
            )

    def attend_back(low_index, high_index):
        @pl.loop(low_index, high_index)
        def _(block):
            at = pl.ds(pl.multiple_of(block * length, length), length)
            weights = probs[at, :]
            pull = d_context[at, :]
            d_weights = dot(pull, value[at, :], ((1,), (1,)))
            d_value = dot(weights.astype(BF16), pull, ((0,), (0,)))
            inner = jnp.sum(d_weights * weights, axis=-1, keepdims=True)
            d_scores = (weights * (d_weights - inner)).astype(BF16)
            d_query = dot(d_scores, key[at, :])
            d_key = dot(d_scores, query[at, :], ((0,), (0,)))
            turn_by, back = cosine[at, :], -sine[at, :]
            pieces = (
                turned(d_query, turn_by, back) * HEAD_DIM**-0.5,
                turned(d_key, turn_by, back),
                d_value,
            )
            for part, piece in enumerate(pieces):
                low = piece.astype(BF16)
                spot = slice(part * part_wide, (part + 1) * part_wide)
                d_joint[at, spot] = low
                sums[6:7, spot] = sums[6:7, spot] + jnp.sum(
                    low.astype(F32), axis=0, keepdims=True
                )

    def project_grad(low_index, high_index):
        @pl.loop(low_index, high_index)
        def _(shard):
            at = pl.ds(pl.multiple_of(shard * 256, 256), 256)
            for part in range(3):
                spot = pl.ds(part * part_wide, part_wide)
                found = dot(wide[:, at], d_joint[:, spot], ((0,), (0,))).astype(BF16)
                for quarter in range(4):
                    grad_one[quarter, shard, :, spot] = found[
                        quarter * share : (quarter + 1) * share
                    ]

    def send_along(index, step):
        col_copy(index, step).wait_recv()
        if index == 0:
            own_load(step).wait()
        here = own_block(index, step)

        def add(left, right):
            chunks((left, right), lambda one, two: add_two(one, one, two))

        add(here, col_act.at[index, step])

        if step > 0:
            @pl.when(inner)
            def _():
                there, copy = came(index, step - 1)
                copy.wait_recv()
                add(here, there)

        line_copy(index, step).start()

    def input_part(step):
        start = target_of(step) * 2 * length

        @pl.loop(0, width // 256)
        def _(index, start=start):
            at = pl.ds(pl.multiple_of(start, 2 * length), 2 * length)
            spot = pl.ds(pl.multiple_of(index * 256, 256), 256)
            d_one = dot(d_joint[at, :], duo[spot, 0:one_wide], ((1,), (1,)))
            d_two = dot(d_widened[at, :], pair[spot, :], ((1,), (1,)))
            now = cot[at, spot].astype(F32)
            rows = (d_one * now, d_one, d_two * now, d_two)
            for place, piece in enumerate(rows):
                sums[place : place + 1, spot] = sums[place : place + 1, spot] + jnp.sum(
                    piece, axis=0, keepdims=True
                )
            wide[at, spot] = (d_one * table[0:1, spot] + d_two * table[2:3, spot]).astype(
                BF16
            )

        col_copy(1, step).start()

    def send_sums():
        for shard in range(8):
            for place in range(5):
                start = place * 256 if place < 4 else 1792
                vec[shard, :, start : start + 256] = sums[
                    place : place + 1, shard * 256 : (shard + 1) * 256
                ]
        vec[me, :, 2048:3072] = sums[5:6, 0:two_wide]
        for part in range(3):
            place = part * 8 + me
            start = pl.multiple_of(1024 + (place % 3) * 256, 256)
            vec[place // 3, :, pl.ds(start, 256)] = sums[
                6:7, part * part_wide : (part + 1) * part_wide
            ]
        for step in range(1, 8):
            vec_copy(step).start()

    my_rows = pl.ds(pl.multiple_of(rep * share, share), share)

    def whole(index):
        full, got, arrived = grads[index]
        core_copy(index, 1).wait_recv()
        side_copy(index).wait_recv()

        def add(left, right, far):
            left[...] = (
                left[...].astype(F32) + right[...].astype(F32) + far[...].astype(F32)
            ).astype(BF16)

        chunks((full.at[rep], got.at[1], arrived), add)

    def pieces(index, step, source_shard, target_shard):
        local = grads[index][0].at[rep, target_shard]
        if index == 1:
            at = pl.ds(pl.multiple_of(source_shard * two_wide, two_wide), two_wide)
            return [
                remote(
                    local, two_full.at[my_rows, at], ps.at[step, 3], pr.at[step, 3],
                    (rep, target_shard),
                )
            ]
        out = []
        for part in range(3):
            start = pl.multiple_of((part * 8 + source_shard) * part_wide, part_wide)
            out.append(
                remote(
                    local.at[:, pl.ds(part * part_wide, part_wide)],
                    one_full.at[my_rows, pl.ds(start, part_wide)],
                    ps.at[step, part], pr.at[step, part], (rep, target_shard),
                )
            )
        return out

    def own_pieces(index):
        local = grads[index][0].at[rep, me]
        if index == 1:
            at = pl.ds(pl.multiple_of(me * two_wide, two_wide), two_wide)
            return [pltpu.make_async_copy(local, two_full.at[my_rows, at], ds_sem.at[3])]
        out = []
        for part in range(3):
            start = pl.multiple_of((part * 8 + me) * part_wide, part_wide)
            out.append(
                pltpu.make_async_copy(
                    local.at[:, pl.ds(part * part_wide, part_wide)],
                    one_full.at[my_rows, pl.ds(start, part_wide)],
                    ds_sem.at[part],
                )
            )
        return out

    fulls = (one_full, two_full, mix_full, narrow_full)

    def spot_of(index, quarter):
        count = fulls[index].shape[0] // 4
        return fulls[index].at[pl.ds(pl.multiple_of(quarter * count, count), count), :]

    def hand(index, lane, source, quarter, device):
        return remote(
            source, spot_of(index, quarter), fs.at[index, lane], fr.at[index, lane], device
        )

    own_full = []

    def scatter(index, *steps):
        for step in steps:
            for copy in pieces(index, step, me, (me + step) % 8):
                copy.start()
        for copy in own_pieces(index):
            copy.start()

    def hand_out(index):
        source = grads[index][0].at[rep]
        hand(index, 0, source, rep, (across, me)).start()
        hand(index, 1, source, rep, (twin, me)).start()
        copy = pltpu.make_async_copy(source, spot_of(index, rep), ds_sem.at[2 + index])
        copy.start()
        own_full.append(copy)

    def share_sums():
        for step in range(1, 8):
            vec_copy(step).wait_recv()
        running = vec[me]
        for step in range(1, 8):
            running = running + vec_got[step - 1]
        vec_mid[...] = running
        for step in range(1, 4):
            vec_share(step).start()

    def hand_on(index):
        for copy in own_pieces(index):
            copy.wait()
        for step in range(1, 8):
            for copy in pieces(index, step, (me + 8 - step) % 8, me):
                copy.wait_recv()
        hand(index, 0, spot_of(index, rep), rep, (across, me)).start()
        hand(index, 1, spot_of(index, rep), rep, (twin, me)).start()

    def end_sum(index):
        col_copy(index, 3).wait_recv()
        if index == 0:
            own_load(3).wait()
        here = own_block(index, 3)

        def add(left, right):
            left[...] = left[...] + right[...].astype(F32)

        def begin(left, right, both):
            both[...] = left[...].astype(F32) + right[...].astype(F32)

        chunks((here, col_act.at[index, 3], total), begin)

        for slot in (2, 3):
            there, copy = came(index, slot)
            copy.wait_recv()
            chunks((total, there), add)
        copy = pltpu.make_async_copy(total, (out_sum, in_sum)[index], ds_sem.at[6])
        copy.start()
        copy.wait()

    def end_vec():
        for step in range(1, 4):
            vec_share(step).wait_recv()
        vec_full[...] = vec_mid[...] + vec_rep[0] + vec_rep[1] + vec_rep[2]

    def hand_twin(index):
        hand(index, 0, spot_of(index, across), across, (across, me)).wait_recv()
        hand(index, 2, spot_of(index, across), across, (twin, me)).start()

    for step in range(4):
        col_copy(0, step).start()
    wait(got_active, got_cot)
    got_context = load(context_all, context, 2)
    got_narrow = [
        load(narrow.at[:, pl.ds(0, half)], pair.at[pl.ds(0, two_wide), :], 3),
        load(narrow.at[:, pl.ds(half, half)], pair.at[pl.ds(two_wide, two_wide), :], 4),
    ]
    got_slope = load(slope_all, slope, 5)
    got_second = load(second, wide, 6)
    got_mix = load(mix, mix_v, 7)
    got_heads = [
        load(query_all, query, 8), load(key_all, key, 9), load(value_all, value, 10),
        load(probs_all, probs, 11), load(cosine_all, cosine, 12), load(sine_all, sine, 13),
    ]
    for step in range(4):
        own_load(step).start()
    narrow_grad(0)
    trade(3, 0)
    narrow_grad(2)
    across_sum(3)
    narrow_grad(1)
    trade(3, 1)
    narrow_grad(3)
    wait(got_context)
    mix_grad()
    trade(2, 0)
    trade(2, 1)
    wait(*got_narrow, got_slope)
    through_gelu(0, 4)
    got_cols = [load(cols_two, pair, 3)]
    across_sum(2)
    wait(got_second)
    wide_grad(0, 8)
    trade(1, 0)
    trade(1, 1)
    got_first = load(first, wide, 6)
    got_cols.append(load(cols_one, duo.at[:, pl.ds(0, one_wide)], 1))
    wait(got_mix, *got_heads)
    through_mix()
    got_norm = load(norm_all, cot, 0)
    across_sum(1)
    send_along(0, 0)
    attend_back(0, 8)
    wait(got_first)
    project_grad(0, 8)
    trade(0, 0)
    trade(0, 1)
    across_sum(0)
    wait(*got_cols, got_norm)
    send_along(0, 1)
    input_part(0)
    input_part(1)
    send_along(0, 2)
    input_part(2)
    input_part(3)
    send_sums()
    whole(1)
    scatter(1, 1,7,2,6,3,5,4)
    send_along(1, 0)
    whole(0)
    scatter(0, 1,7,2,6,3,5,4)
    whole(3)
    hand_out(3)
    whole(2)
    hand_out(2)
    send_along(1, 1)
    end_sum(0)
    hand_on(1)
    send_along(1, 2)
    share_sums()
    hand_on(0)
    end_sum(1)
    end_vec()
    hand_twin(3)
    hand_twin(2)
    hand_twin(1)
    hand_twin(0)
    for index in range(4):
        source = grads[index][0].at[rep] if index > 1 else spot_of(index, rep)
        hand(index, 0, source, rep, (across, me)).wait_send()
        hand(index, 1, source, rep, (twin, me)).wait_send()
        hand(index, 1, spot_of(index, twin), twin, (twin, me)).wait_recv()
        hand(index, 2, spot_of(index, across), across, (twin, me)).wait_send()
        hand(index, 2, spot_of(index, diagonal), diagonal, (twin, me)).wait_recv()
        side_copy(index).wait_send()
        for slot in (0, 1):
            core_copy(index, slot).wait_send()
    for index in (0, 1):
        for step in range(1, 8):
            for copy in pieces(index, step, me, (me + step) % 8):
                copy.wait_send()
        for step in range(4):
            col_copy(index, step).wait_send()
            if step < 3:
                line_copy(index, step).wait_send()
    for step in range(1, 8):
        vec_copy(step).wait_send()
    for step in range(1, 4):
        vec_share(step).wait_send()
    for copy in own_full:
        copy.wait()


def backward(
    cot_all, norm, first, second, cols_one, cols_two, mix, narrow,
    heads, context, active, slope, cosine, sine, out_part, table,
):
    dma = pltpu.SemaphoreType.DMA
    struct = jax.ShapeDtypeStruct
    vmem = pl.BlockSpec(memory_space=pltpu.VMEM)
    tokens, width = cot_all.shape
    length = tokens // 8
    one, two = cols_one.shape[1], cols_two.shape[1]
    share = width // 32
    quarters = [
        (8, share, one), (8, share, two), (mix.shape[0] // 4, width),
        (narrow.shape[0] // 4, width),
    ]
    lanes = 4 * width // 8 + one + width // 8 + two
    return pl.pallas_call(
        backward_kernel,
        out_shape=(
            struct((length, width), F32),
            struct((length, width), F32),
            struct((4 * share, 8 * one), BF16),
            struct((4 * share, 8 * two), BF16),
            struct(mix.shape, BF16),
            struct(narrow.shape, BF16),
            struct((1, lanes), F32),
        ),
        in_specs=[ANY] * 18 + [vmem],
        out_specs=(ANY,) * 6 + (vmem,),
        scratch_shapes=[pltpu.VMEM((4,) + q, BF16) for q in quarters]
        + [pltpu.VMEM((2,) + q, BF16) for q in quarters]
        + [pltpu.VMEM(q, BF16) for q in quarters]
        + [
            pltpu.VMEM((tokens, width), BF16),
            pltpu.VMEM((width, two), BF16),
            pltpu.VMEM((2 * tokens, two), BF16),
            pltpu.VMEM((tokens, width), BF16),
            pltpu.VMEM((tokens, two), BF16),
            pltpu.VMEM(mix.shape, BF16),
        ]
        + [pltpu.VMEM(h.shape, h.dtype) for h in heads]
        + [
            pltpu.VMEM(context.shape, BF16),
            pltpu.VMEM(context.shape, BF16),
            pltpu.VMEM((tokens, one), BF16),
            pltpu.VMEM(cosine.shape, F32),
            pltpu.VMEM(sine.shape, F32),
            pltpu.VMEM((4, length, width), BF16),
            pltpu.VMEM((2, 4, length, width), BF16),
            pltpu.VMEM((2, 4, length, width), BF16),
            pltpu.VMEM((length, width), F32),
            pltpu.VMEM((8, width), F32),
            pltpu.VMEM((8, 1, lanes), F32),
            pltpu.VMEM((7, 1, lanes), F32),
            pltpu.VMEM((1, lanes), F32),
            pltpu.VMEM((3, 1, lanes), F32),
            dma((14,)), dma((4,)),
            dma((4, 2)), dma((4, 2)), dma((4,)), dma((4,)),
            dma((2, 4)), dma((2, 4)), dma((2, 3)), dma((2, 4)),
            dma((8, 4)), dma((8, 4)), dma((4, 3)), dma((4, 3)),
            dma((7,)), dma((7,)), dma((3,)), dma((3,)), dma((7,)),
        ],
        compiler_params=pltpu.CompilerParams(
            collective_id=1, has_side_effects=True, vmem_limit_bytes=60 << 20
        ),
        name="backward",
    )(
        cot_all, norm, first, second, cols_one, cols_two, mix, narrow,
        *heads, context, active, slope, cosine, sine, out_part, table,
    )


def finish_kernel(
    tok, cot, out_sum, in_sum, out_bias, one, two, mix, narrow, sums,
    output, input_grad, one_out, two_out, mix_out, narrow_out, narrow_sum, *vectors,
):
    own = tok[...].astype(F32)
    center = own - jnp.mean(own, axis=-1, keepdims=True)
    scale = lax.rsqrt(jnp.mean(center * center, axis=-1, keepdims=True) + 1e-05)
    norm = center * scale
    output[...] = (own + out_sum[...] + out_bias[...]).astype(BF16)
    pull = in_sum[...]
    inner = jnp.mean(pull * norm, axis=-1, keepdims=True)
    pull = scale * (pull - jnp.mean(pull, axis=-1, keepdims=True) - norm * inner)
    input_grad[...] = (cot[...].astype(F32) + pull).astype(BF16)
    for source, target in (
        (one, one_out), (two, two_out), (mix, mix_out), (narrow, narrow_out)
    ):
        target[...] = source[...].astype(F32)

    @pl.when(pl.program_id(0) == 0)
    def _():
        start = 0
        for target in vectors:
            count = target.shape[0]
            target[...] = sums[0, start : start + count]
            start += count
        narrow_sum[...] = vectors[5][...]


def finish(tok, cot, out_sum, in_sum, out_bias, one, two, mix, narrow, sums, counts):
    struct = jax.ShapeDtypeStruct
    steps = 8

    def rows(array):
        return pl.BlockSpec((array.shape[0] // steps, array.shape[1]), lambda i: (i, 0))

    def fixed(array):
        return pl.BlockSpec(array.shape, lambda i: (0, 0))

    moved = (one, two, mix, narrow)
    return pl.pallas_call(
        finish_kernel,
        grid=(steps,),
        out_shape=(struct(tok.shape, BF16), struct(tok.shape, BF16))
        + tuple(struct(m.shape, F32) for m in moved)
        + tuple(struct((count,), F32) for count in (counts[5], *counts)),
        in_specs=[rows(tok), rows(cot), rows(out_sum), rows(in_sum), fixed(out_bias)]
        + [rows(m) for m in moved]
        + [fixed(sums)],
        out_specs=(rows(tok), rows(tok))
        + tuple(rows(m) for m in moved)
        + tuple(pl.BlockSpec((count,), lambda i: (0,)) for count in (counts[5], *counts)),
        compiler_params=pltpu.CompilerParams(vmem_limit_bytes=60 << 20),
        name="finish",
    )(tok, cot, out_sum, in_sum, out_bias, *moved, sums)


def tensor_parallel(
    tokens,
    segment_ids,
    positions,
    first_gain,
    first_shift,
    project_weight,
    project_bias,
    mixing_weight,
    mixing_bias,
    second_gain,
    second_shift,
    widen_weight,
    widen_bias,
    narrow_weight,
    narrow_bias,
    cotangent,
):
    (
        cot_all, norm, cols_one, cols_two, first, second, query, keys, values, probs,
        context, active, slope, out_part, cosine, sine, table, out_bias,
    ) = forward(
        tokens, cotangent, project_weight, widen_weight, mixing_weight, narrow_weight,
        (
            first_gain, first_shift, second_gain, second_shift, mixing_bias, narrow_bias,
            project_bias, widen_bias, segment_ids, positions,
        ),
    )
    out_sum, in_sum, full_one, full_two, full_mix, full_narrow, sums = backward(
        cot_all.reshape(-1, D), norm, first, second, cols_one, cols_two, mixing_weight,
        narrow_weight, (query, keys, values, probs), context, active, slope, cosine, sine,
        out_part, table,
    )
    width = D // 8
    (
        output, input_grad, grad_one, grad_two, grad_mix, grad_narrow, sum_narrow,
        sum_first_gain, sum_first_shift, sum_second_gain, sum_second_shift,
        sum_project, sum_cot, sum_widen,
    ) = finish(
        tokens, cotangent, out_sum, in_sum, out_bias, full_one, full_two, full_mix,
        full_narrow, sums,
        (width, width, width, width, project_bias.shape[0], width, widen_bias.shape[0]),
    )
    return (
        output,
        input_grad,
        sum_first_gain,
        sum_first_shift,
        grad_one,
        sum_project,
        grad_mix,
        sum_cot,
        sum_second_gain,
        sum_second_shift,
        grad_two,
        sum_widen,
        grad_narrow,
        sum_narrow,
    )


def solution(mesh):
    head_per_shard = mesh.shape["shard"] == HEADS and mesh.shape["rep"] == 4
    chosen = tensor_parallel if head_per_shard else per_device
    in_specs = (
        P(("rep", "shard"), None),
        P(("rep", "shard")),
        P(("rep", "shard")),
        P("shard"),
        P("shard"),
        P("shard", None),
        P("shard"),
        P("shard", None),
        P("shard"),
        P("shard"),
        P("shard"),
        P("shard", None),
        P("shard"),
        P("shard", None),
        P("shard"),
        P(("rep", "shard"), None),
    )
    out_specs = (
        P(("rep", "shard"), None),
        P(("rep", "shard"), None),
        P("shard"),
        P("shard"),
        P("shard", None),
        P("shard"),
        P("shard", None),
        P("shard"),
        P("shard"),
        P("shard"),
        P("shard", None),
        P("shard"),
        P("shard", None),
        P("shard"),
    )
    return jax.shard_map(
        chosen, mesh=mesh, in_specs=in_specs, out_specs=out_specs, check_vma=False
    )
```
